32 devices in a mesh: groups: 2 (over y), gx: 8 (over z, x), gy: 2 (over core).
Axes of the slice: x: 2, y: 2, z: 4, core: 2. Of those that a mesh axis runs over, the one named last changes fastest.
Arguments:
- probe_vectors: bfloat16 [8192, 1536], P(('groups', 'gx', 'gy')), parts along dimension 0, may hold values from -60 to 60
- mesh_lookup_pair: bfloat16 [8192, 2, 1536], P(('groups', 'gx', 'gy')), parts along dimension 0, may hold values from -6 to 6
- landmark_lookup_pair: bfloat16 [128, 2, 1536], P(('groups', 'gx', 'gy')), parts along dimension 0, may hold values from -6 to 6
- softmax_warmth: float32 [24], P('groups'), parts along dimension 0, may hold values from 0.5 to 2
- output_adjoint: bfloat16 [8192, 1536], P(('groups', 'gx', 'gy')), parts along dimension 0, may hold values from -6 to 6
- exported_boundary_tiles: int32 [32, 3, 1], P(('groups', 'gx', 'gy')), parts along dimension 0, may hold values from 0 to 1
- adjacency_tile_filter: int32 [32, 2, 5], P(('groups', 'gx', 'gy')), parts along dimension 0, may hold values 0 or 1
Outputs:
- probe_derivative: bfloat16 [8192, 1536], P(('groups', 'gx', 'gy')), parts along dimension 0
- cell_kv_grad: bfloat16 [8192, 2, 1536], P(('groups', 'gx', 'gy')), parts along dimension 0
- anchor_kv_grad: float32 [128, 2, 1536], P(('groups', 'gx', 'gy')), parts along dimension 0
- temperature_grad: float32 [24], P('groups'), parts along dimension 0
The draws below stay inside these ranges and needn't reach their ends.
There are 2 independent parts, one for each index of `groups`. The reference program is written for one: setup_inputs(seed, part) draws one part's arguments, and reference() takes and returns one part's arrays. A program takes and returns all parts, laid end to end along the dimension named above; each array names one. Nothing has to cross between parts.
All inputs are finite; a program needn't handle non-finite values. No bound on the sum of `adjacency_tile_filter` on one device may be relied on, other than what follows from the above.
Results may differ from the reference program's by a relative error of at most 0.001.
The reference program's roundings to bfloat16 on the way count: a program that leaves them out, or rounds other values in their place, can miss the bound.
Values may be sent and summed in bfloat16 or wider, within the bound.
No kernel may reach another device: no remote copies, remote signals or barrier semaphores. Data moves between devices by JAX's collectives and lax.ppermute only.
A program may use at most 128 MiB of HBM per device.

```python
import math
import jax
import jax.numpy as jnp
from jax import lax

HEADS = 12
HEAD_DIM = 128
FEAT = 1536
BLOCK = 128
BLOCKS_DEV = 2
FACE_BLOCKS = 1
PARTS_SIZE = 16
CELLS = 4096
ANCHORS = 64
N_GX = 8
N_GY = 2


def shared_fields(key):
    cell_total = BLOCKS_DEV * BLOCK * N_GX * N_GY
    feat_width = HEADS * HEAD_DIM
    temper_vals = jnp.exp(jax.random.uniform(jax.random.fold_in(key, 31), (HEADS,), jnp.float32, math.log(0.5), math.log(2.0)))
    query_vals = jnp.clip(jax.random.normal(jax.random.fold_in(key, 32), (cell_total, feat_width), jnp.float32), -6.0, 6.0)
    pair_vals = jnp.clip(jax.random.normal(jax.random.fold_in(key, 33), (cell_total, 2, feat_width), jnp.float32), -6.0, 6.0)
    return (query_vals, pair_vals, temper_vals)


def draw_probe_vectors(key, part):
    return shared_fields(key)[0].astype(jnp.bfloat16)


def draw_mesh_lookup_pair(key, part):
    return shared_fields(key)[1].astype(jnp.bfloat16)


def draw_softmax_warmth(key, part):
    return shared_fields(key)[2]


def touch_ends(result, key, smallest, largest):
    longest = result.shape.index(max(result.shape))
    spots = []
    for shift in (0, 1):
        where = [jax.random.randint(jax.random.fold_in(key, axis), (), 0, length) for axis, length in enumerate(result.shape)]
        where[longest] = (where[longest] + shift) % result.shape[longest]
        spots.append(tuple(where))
    return result.at[spots[0]].set(smallest).at[spots[1]].set(largest)


def block_levels(own_key, shape, split, least, largest):
    gain, own = 1.0, jax.random.fold_in(own_key, 6)
    for dim, shards_of in split:
        heights = jnp.exp(jax.random.uniform(jax.random.fold_in(own, dim), (shards_of,), jnp.float32, least / len(split), largest / len(split)))
        gain = gain * jnp.repeat(heights, shape[dim] // shards_of).reshape([-1 if axis == dim else 1 for axis in range(len(shape))])
    return gain


def scatter_about(stream_key, shape, deviation, limit, split=(), kind=jnp.bfloat16):
    values = jax.random.normal(stream_key, shape, jnp.float32) * deviation
    if len(split) > 0:
        values = block_levels(stream_key, shape, split, -0.22, 0.18) * values
    return jnp.clip(values, min=-limit, max=limit).astype(kind)


def setup_inputs(seed: int = 0, part: int = 0) -> dict:
    keys = jax.random.split(jax.random.key(seed), 8)
    own_keys = jax.random.split(jax.random.fold_in(keys[7], part), 8)
    return {
        "probe_vectors": draw_probe_vectors(jax.random.fold_in(jax.random.fold_in(keys[7], part), 71), part),
        "mesh_lookup_pair": draw_mesh_lookup_pair(jax.random.fold_in(jax.random.fold_in(keys[7], part), 71), part),
        "landmark_lookup_pair": scatter_about(own_keys[2], (ANCHORS, 2, FEAT), 1.0, 6.0, ((0, 16),)),
        "softmax_warmth": draw_softmax_warmth(jax.random.fold_in(jax.random.fold_in(keys[7], part), 71), part),
        "output_adjoint": scatter_about(own_keys[4], (CELLS, FEAT), 1.0, 6.0, ((0, 16),)),
        "exported_boundary_tiles": touch_ends(jax.random.randint(own_keys[5], (PARTS_SIZE, 3, FACE_BLOCKS), 0, BLOCKS_DEV), jax.random.fold_in(own_keys[5], 1), 0, BLOCKS_DEV - 1).astype(jnp.int32),
        "adjacency_tile_filter": touch_ends((jax.random.randint(own_keys[6], (PARTS_SIZE, BLOCKS_DEV, BLOCKS_DEV + 3 * FACE_BLOCKS), 0, 4) < 3).astype(jnp.int32), jax.random.fold_in(own_keys[6], 1), 0, 1),
    }


def softmax_derivative_bundle(probe_vectors, lookup_entries, payload_entries, output_adjoint, allowed_couples, softmax_warmth):
    row_count = probe_vectors.shape[0]
    channel_group_count = softmax_warmth.shape[0]
    channel_width_each = probe_vectors.shape[1] // channel_group_count
    logit_multiplier = softmax_warmth / math.sqrt(channel_width_each)
    query_heads = probe_vectors.astype(jnp.float32).reshape(row_count, channel_group_count, channel_width_each)
    key_heads = lookup_entries.astype(jnp.float32).reshape(lookup_entries.shape[0], channel_group_count, channel_width_each)
    value_heads = payload_entries.astype(jnp.float32).reshape(payload_entries.shape[0], channel_group_count, channel_width_each)
    grad_heads = output_adjoint.astype(jnp.float32).reshape(row_count, channel_group_count, channel_width_each)
    unnormalised_logits = jnp.einsum('qhd,khd->hqk', query_heads, key_heads)
    scores = jnp.where(allowed_couples[None], unnormalised_logits * logit_multiplier[:, None, None], -jnp.inf)
    row_max = lax.optimization_barrier(jnp.max(scores, axis=2, keepdims=True))
    exp_scores = jnp.exp(scores - row_max)
    weights = exp_scores / lax.optimization_barrier(jnp.sum(exp_scores, axis=2, keepdims=True))
    weights_b = weights.astype(jnp.bfloat16)
    attended = jnp.einsum('hqk,khd->qhd', weights_b.astype(jnp.float32), value_heads)
    row_delta = lax.optimization_barrier(jnp.sum(grad_heads * attended, axis=2))
    weight_grad = jnp.einsum('qhd,khd->hqk', grad_heads, value_heads)
    logit_adjoint = weights * (weight_grad - jnp.transpose(row_delta)[:, :, None])
    warmth_contribution = lax.optimization_barrier(jnp.sum(logit_adjoint * unnormalised_logits, axis=(1, 2))) / math.sqrt(channel_width_each)
    dscore_b = (logit_adjoint * logit_multiplier[:, None, None]).astype(jnp.bfloat16)
    probe_derivative = jnp.einsum('hqk,khd->qhd', dscore_b.astype(jnp.float32), key_heads)
    probe_derivative = probe_derivative.reshape(row_count, channel_group_count * channel_width_each).astype(jnp.bfloat16)
    key_grad = jnp.einsum('hqk,qhd->khd', dscore_b.astype(jnp.float32), query_heads)
    value_grad = jnp.einsum('hqk,qhd->khd', weights_b.astype(jnp.float32), grad_heads)
    width = channel_group_count * channel_width_each
    lookup_derivative_parts = jnp.stack([key_grad.reshape(-1, width), value_grad.reshape(-1, width)], axis=1)
    return (probe_derivative, lookup_derivative_parts, warmth_contribution)

def reference(probe_vectors, mesh_lookup_pair, landmark_lookup_pair, softmax_warmth, output_adjoint, exported_boundary_tiles, adjacency_tile_filter):
    part_count = N_GX * N_GY
    feat_width = probe_vectors.shape[1]
    cell_dev = BLOCKS_DEV * BLOCK
    vicinity_length = cell_dev + 3 * FACE_BLOCKS * BLOCK
    kv_blocks = mesh_lookup_pair.reshape(part_count, BLOCKS_DEV, BLOCK, 2, feat_width)
    picked = jax.vmap(lambda kv_block, block_index: kv_block[block_index])(kv_blocks, exported_boundary_tiles)
    face_grid = picked.reshape(N_GX, N_GY, 3, FACE_BLOCKS, BLOCK, 2, feat_width)
    zero_rim = jnp.zeros_like(face_grid[:1, :, 0])
    from_lower = jnp.concatenate([zero_rim, face_grid[:-1, :, 1]], axis=0)
    from_upper = jnp.concatenate([face_grid[1:, :, 0], zero_rim], axis=0)
    from_partner = face_grid[:, ::-1, 2]
    halo_kv = jnp.stack([from_lower, from_upper, from_partner], axis=2)
    halo_kv = halo_kv.reshape(part_count, 3 * FACE_BLOCKS * BLOCK, 2, feat_width)
    part_index = jnp.arange(part_count, dtype=jnp.int32) // N_GY

    def allowed_table_entry(shard_allowance, primary_axis_position):
        near_mask = (shard_allowance > 0) | jnp.eye(BLOCKS_DEV, BLOCKS_DEV + 3 * FACE_BLOCKS, dtype=bool)
        valid = jnp.concatenate([jnp.ones((BLOCKS_DEV,), bool), jnp.full((FACE_BLOCKS,), primary_axis_position > 0), jnp.full((FACE_BLOCKS,), primary_axis_position < N_GX - 1), jnp.ones((FACE_BLOCKS,), bool)])
        near_mask = near_mask & valid[None]
        near_mask = jnp.repeat(jnp.repeat(near_mask, BLOCK, axis=0), BLOCK, axis=1)
        return jnp.concatenate([near_mask, jnp.ones((cell_dev, ANCHORS), bool)], axis=1)

    def scan_step(accumulated_state, inputs):
        shard_probes, kv_dev, halo_dev, shard_derivatives, shard_allowance, primary_axis_position = inputs
        combined_lookup_pair = jnp.concatenate([kv_dev, halo_dev, landmark_lookup_pair], axis=0)
        probe_derivative, lookup_derivative_parts, warmth_contribution = softmax_derivative_bundle(shard_probes, combined_lookup_pair[:, 0], combined_lookup_pair[:, 1], shard_derivatives, allowed_table_entry(shard_allowance, primary_axis_position), softmax_warmth)
        accumulated_state = (accumulated_state[0] + lookup_derivative_parts[vicinity_length:], accumulated_state[1] + warmth_contribution)
        return (accumulated_state, (probe_derivative, lookup_derivative_parts[:cell_dev], lookup_derivative_parts[cell_dev:vicinity_length].astype(jnp.bfloat16)))
    start_state = (jnp.zeros((ANCHORS, 2, feat_width), jnp.float32), jnp.zeros((HEADS,), jnp.float32))
    scan_inputs = (probe_vectors.reshape(part_count, cell_dev, feat_width), mesh_lookup_pair.reshape(part_count, cell_dev, 2, feat_width), halo_kv, output_adjoint.reshape(part_count, cell_dev, feat_width), adjacency_tile_filter, part_index)
    (anchor_grad, warmth_derivative), (probe_derivative, local_grad, halo_grad) = lax.scan(scan_step, start_state, scan_inputs)
    grad_grid = halo_grad.reshape(N_GX, N_GY, 3, FACE_BLOCKS, BLOCK, 2, feat_width)
    zero_back = jnp.zeros_like(grad_grid[:1, :, 0])
    back_lower = jnp.concatenate([zero_back, grad_grid[:-1, :, 1]], axis=0)
    back_upper = jnp.concatenate([grad_grid[1:, :, 0], zero_back], axis=0)
    back_partner = grad_grid[:, ::-1, 2]
    returned = jnp.stack([back_lower, back_upper, back_partner], axis=2)
    returned = returned.reshape(part_count, 3 * FACE_BLOCKS, BLOCK, 2, feat_width).astype(jnp.float32)
    local_blocks = local_grad.reshape(part_count, BLOCKS_DEV, BLOCK, 2, feat_width)
    totals = jax.vmap(lambda local_part, block_index, back_part: local_part.at[block_index.reshape(-1)].add(back_part))(local_blocks, exported_boundary_tiles, returned)
    cell_grad = totals.reshape(CELLS, 2, feat_width).astype(jnp.bfloat16)
    return (probe_derivative.reshape(CELLS, feat_width), cell_grad, anchor_grad, warmth_derivative)
```

```python
import functools
import math

import jax
import jax.numpy as jnp
from jax import lax
from jax.experimental import pallas as pl
from jax.experimental.pallas import tpu as pltpu
from jax.sharding import PartitionSpec as P

BLOCK = 128
F32 = jnp.float32
BF16 = jnp.bfloat16
SMEM = pltpu.MemorySpace.SMEM


def swap_bit(x, axis, bit):
    count = lax.axis_size(axis)
    return lax.ppermute(x, axis, [(i, i ^ (1 << bit)) for i in range(count)])


def swap_pairs(x, first):
    count = lax.axis_size("gx")
    route = []
    for low in range(first, count - 1, 2):
        route += [(low, low + 1), (low + 1, low)]
    return lax.ppermute(x, "gx", route)


def attention_kernel(
    pos_ref, filt_ref, warm_ref, q_ref, g_ref, own_ref, dir_ref, dia_ref, par_ref, anc_ref, *rest,
    gx_count, head0, width,
):
    (dq_ref, own_out, dir_out, dia_out, par_out, anc_out, temp_out, k_ref, v_ref) = rest[-9:]
    head = pl.program_id(0)
    gx = pos_ref[0]
    odd = lax.rem(gx, 2)
    own_rows = own_ref.shape[0]
    blocks = own_rows // BLOCK
    anchors = anc_ref.shape[0]
    queries = q_ref.shape[0]
    near = own_rows + 3 * BLOCK
    keys = near + anchors

    row = 0
    for ref in (own_ref, dir_ref, dia_ref, par_ref, anc_ref):
        n = ref.shape[0]
        k_ref[row : row + n, :] = ref[:, 0, :]
        v_ref[row : row + n, :] = ref[:, 1, :]
        row += n

    q = q_ref[...]
    g = g_ref[...]
    k = k_ref[...]
    v = v_ref[...]
    nt = (((1,), (1,)), ((), ()))
    s = lax.dot_general(k, q, nt, preferred_element_type=F32)
    dp = lax.dot_general(v, g, nt, preferred_element_type=F32)

    mult = warm_ref[head0 + head] / math.sqrt(width)
    lane = lax.broadcasted_iota(jnp.int32, (1, queries), 1) // BLOCK
    direct_col = blocks + 1 - odd
    diagonal_col = blocks + odd
    diagonal_there = jnp.where(odd == 1, gx < gx_count - 1, gx > 0)
    parts = []
    for b in range(blocks + 3):
        bias = jnp.zeros((1, queries), F32)
        for a in range(blocks):
            if b == a:
                continue
            col = (b if b < blocks else (direct_col, diagonal_col, blocks + 2)[b - blocks])
            ok = filt_ref[a, col] > 0
            if b == blocks + 1:
                ok = jnp.logical_and(ok, diagonal_there)
            bias = jnp.where(lane == a, jnp.where(ok, 0.0, -jnp.inf).astype(F32), bias)
        parts.append(s[b * BLOCK : (b + 1) * BLOCK] * mult + bias)
    parts.append(s[near:] * mult)
    scores = jnp.concatenate(parts, axis=0)
    top = jnp.max(scores, axis=0, keepdims=True)
    e = jnp.exp(scores - top)
    inv = 1.0 / jnp.sum(e, axis=0, keepdims=True)
    p = e * inv
    pb = p.astype(BF16)
    delta = jnp.sum(pb.astype(F32) * dp, axis=0, keepdims=True)
    ds = p * (dp - delta)
    temp_out[0] = jnp.sum(ds * s, axis=0, keepdims=True)
    dsb = (ds * mult).astype(BF16)
    nn = (((1,), (0,)), ((), ()))
    dv = lax.dot_general(pb, g, nn, preferred_element_type=F32)
    dk = lax.dot_general(dsb, q, nn, preferred_element_type=F32)
    dq = lax.dot_general(dsb, k, (((0,), (0,)), ((), ())), preferred_element_type=F32)
    dq_ref[...] = dq.astype(BF16)
    for j, terms in enumerate((dk, dv)):
        own_out[j] = terms[:own_rows]
        for i, ref in enumerate((dir_out, dia_out, par_out)):
            at = own_rows + i * BLOCK
            ref[j] = terms[at : at + BLOCK].astype(BF16)
        anc_out[j] = terms[near:]


def attention(pos, filt, warm, q, g, mesh_kv, halo, anchors, head0, heads, dq_prev, anc_prev):
    rows, feat = q.shape
    total = warm.shape[0]
    width = feat // total
    own_rows = mesh_kv.shape[0]
    a_rows = anchors.shape[0]
    keys = own_rows + 3 * BLOCK + a_rows
    full3 = lambda n: pl.BlockSpec((n, 2, width), lambda h: (0, 0, head0 + h))
    part3 = lambda n: pl.BlockSpec((n, 2, width), lambda h: (0, 0, h))
    smem = pl.BlockSpec(memory_space=SMEM)
    cols = pl.BlockSpec((rows, width), lambda h: (0, head0 + h))
    out_face = pl.BlockSpec((2, BLOCK, width), lambda h: (0, 0, h))
    in_specs = [smem, smem, smem, cols, cols, full3(own_rows), part3(BLOCK), part3(BLOCK), full3(BLOCK), full3(a_rows)]
    args = [pos, filt, warm, q, g, mesh_kv, *halo, anchors]
    alias = {}
    if dq_prev is not None:
        in_specs += [pl.BlockSpec(memory_space=pl.ANY)] * 2
        args += [dq_prev, anc_prev]
        alias = {10: 0, 11: 5}
    face = jax.ShapeDtypeStruct((2, BLOCK, heads * width), BF16)
    return pl.pallas_call(
        functools.partial(attention_kernel, gx_count=lax.axis_size("gx"), head0=head0, width=width),
        grid=(heads,),
        in_specs=in_specs,
        out_specs=[
            cols,
            pl.BlockSpec((2, own_rows, width), lambda h: (0, 0, h)),
            out_face,
            out_face,
            out_face,
            pl.BlockSpec((2, a_rows, width), lambda h: (0, 0, head0 + h)),
            pl.BlockSpec((1, 1, rows), lambda h: (h, 0, 0)),
        ],
        out_shape=[
            jax.ShapeDtypeStruct(q.shape, BF16),
            jax.ShapeDtypeStruct((2, own_rows, heads * width), F32),
            face,
            face,
            face,
            jax.ShapeDtypeStruct((2, a_rows, feat), F32),
            jax.ShapeDtypeStruct((heads, 1, rows), F32),
        ],
        scratch_shapes=[pltpu.VMEM((keys, width), BF16)] * 2,
        input_output_aliases=alias,
        compiler_params=pltpu.CompilerParams(vmem_limit_bytes=48 << 20),
        cost_estimate=pl.CostEstimate(
            flops=10 * heads * rows * keys * width,
            transcendentals=heads * rows * keys,
            bytes_accessed=heads * width * (rows * 6 + own_rows * 12 + 3 * BLOCK * 8 + a_rows * 12),
        ),
        name="attention",
    )(*args)


def combine_kernel(pos_ref, sent_ref, own_ref, dir_ref, dia_ref, par_ref, *rest):
    out_ref = rest[-1]
    odd = lax.rem(pos_ref[0], 2)
    blocks = own_ref.shape[1] // BLOCK
    spots = (
        jnp.where(odd == 1, sent_ref[0, 0], sent_ref[1, 0]),
        jnp.where(odd == 1, sent_ref[1, 0], sent_ref[0, 0]),
        sent_ref[2, 0],
    )
    for a in range(blocks):
        at = slice(a * BLOCK, (a + 1) * BLOCK)
        for j in range(2):
            total = own_ref[j, at, :]
            for spot, ref in zip(spots, (dir_ref, dia_ref, par_ref)):
                total = total + jnp.where(spot == a, 1.0, 0.0).astype(F32) * ref[j].astype(F32)
            out_ref[at, j, :] = total.astype(BF16)


def combine(pos, sent, own, faces, head0, heads, feat, width, prev):
    rows = own.shape[1]
    smem = pl.BlockSpec(memory_space=SMEM)
    w = width * (2 if heads % 2 == 0 and head0 % 2 == 0 else 1)
    steps = heads * width // w
    base = head0 * width // w
    face = pl.BlockSpec((2, BLOCK, w), lambda h: (0, 0, h))
    in_specs = [smem, smem, pl.BlockSpec((2, rows, w), lambda h: (0, 0, h)), face, face, face]
    args = [pos, sent, own, *faces]
    alias = {}
    if prev is not None:
        in_specs.append(pl.BlockSpec(memory_space=pl.ANY))
        args.append(prev)
        alias = {6: 0}
    return pl.pallas_call(
        combine_kernel,
        grid=(steps,),
        in_specs=in_specs,
        out_specs=pl.BlockSpec((rows, 2, w), lambda h: (0, 0, base + h)),
        out_shape=jax.ShapeDtypeStruct((rows, 2, feat), BF16),
        input_output_aliases=alias,
        compiler_params=pltpu.CompilerParams(vmem_limit_bytes=32 << 20),
        cost_estimate=pl.CostEstimate(
            flops=heads * width * rows * 16,
            transcendentals=0,
            bytes_accessed=heads * width * (rows * 12 + 3 * BLOCK * 4),
        ),
        name="combine",
    )(*args)


def local(q, mesh_kv, landmark, warm, g, exported, filt):
    rows, feat = q.shape
    total = warm.shape[0]
    width = feat // total
    gx_count = lax.axis_size("gx")
    bits = gx_count.bit_length() - 1
    gx = lax.axis_index("gx")
    pos = jnp.full((1,), gx, jnp.int32)
    sent = exported[0]
    filt = filt[0]
    odd = lax.rem(gx, 2)
    direct_block = jnp.where(odd == 1, sent[0, 0], sent[1, 0])
    diagonal_block = jnp.where(odd == 1, sent[1, 0], sent[0, 0])
    chunks = [(0, total // 2), (total // 2, total - total // 2)]

    def pick(block, head0, heads):
        return lax.dynamic_slice(
            mesh_kv, (block * BLOCK, 0, head0 * width), (BLOCK, 2, heads * width)
        )

    halos = []
    anchors = landmark[None]
    theirs = swap_bit(anchors, "gy", 0)
    anchors = jnp.concatenate([anchors, theirs], axis=0)
    for c, (head0, heads) in enumerate(chunks):
        diagonal = swap_pairs(pick(diagonal_block, head0, heads), 1)
        direct = swap_pairs(pick(direct_block, head0, heads), 0)
        halos.append((direct, diagonal))
    partner = swap_bit(pick(sent[2, 0], 0, total), "gy", 0)
    for bit in range(bits):
        theirs = swap_bit(anchors, "gx", bit)
        anchors = jnp.concatenate([anchors, theirs], axis=1)
    a_rows = anchors.shape[0] * anchors.shape[1]
    anchors = anchors.reshape(a_rows, 2, feat)

    dq = anc = None
    temps, owns, returned = [], [], []
    for (head0, heads), (direct, diagonal) in zip(chunks, halos):
        dq, own, f_dir, f_dia, f_par, anc, temp = attention(
            pos, filt, warm, q, g, mesh_kv, (direct, diagonal, partner), anchors, head0, heads, dq, anc
        )
        temps.append(temp)
        owns.append(own)
        returned.append((swap_pairs(f_dir, 0), swap_pairs(f_dia, 1), swap_bit(f_par, "gy", 0)))

    temp = jnp.sum(jnp.concatenate(temps, axis=0), axis=(1, 2)) / math.sqrt(width)
    extra = jnp.zeros((2, 1, feat), F32).at[0, 0, :total].set(temp)
    for axis, bit in [("gy", 0)] + [("gx", b) for b in reversed(range(bits))]:
        half = anc.shape[1] // 2
        got = swap_bit(jnp.concatenate([anc[:, half:], extra], axis=1), axis, bit)
        anc = anc[:, :half] + got[:, :half]
        extra = extra + got[:, half:]
    anchor_grad = jnp.transpose(anc, (1, 0, 2))
    temp = extra[0, 0, :total]

    cell = None
    for (head0, heads), own, faces in zip(chunks, owns, returned):
        cell = combine(pos, sent, own, faces, head0, heads, feat, width, cell)
    return (dq, cell, anchor_grad, temp)


def solution(mesh):
    rows = ("groups", "gx", "gy")
    placed = (
        P(rows, None),
        P(rows, None, None),
        P(rows, None, None),
        P("groups"),
        P(rows, None),
        P(rows, None, None),
        P(rows, None, None),
    )
    return jax.shard_map(
        local,
        mesh=mesh,
        in_specs=placed,
        out_specs=(P(rows, None), P(rows, None, None), P(rows, None, None), P("groups")),
        check_vma=False,
    )
```

```python
import functools
import math

import jax
import jax.numpy as jnp
from jax import lax
from jax.experimental import pallas as pl
from jax.experimental.pallas import tpu as pltpu
from jax.sharding import PartitionSpec as P

BLOCK = 128
F32 = jnp.float32
BF16 = jnp.bfloat16
SMEM = pltpu.MemorySpace.SMEM


def swap_mask(x, mask):
    count = lax.axis_size(("gx", "gy"))
    return lax.ppermute(x, ("gx", "gy"), [(i, i ^ mask) for i in range(count)])


def levels(count):
    bits = count.bit_length() - 1
    return [(at, (1 << min(2, bits - at)) - 1) for at in range(0, bits, 2)]


def swap_pairs(x, first):
    count = lax.axis_size("gx")
    route = []
    for low in range(first, count - 1, 2):
        route += [(low, low + 1), (low + 1, low)]
    return lax.ppermute(x, "gx", route)


def split_heads(total):
    first = (total + 1) // 2
    return [n for n in (first, total - first) if n > 0]


def prep_kernel(a_ref, b_ref, k_ref, v_ref):
    row = 0
    for ref in (a_ref, b_ref):
        n = ref.shape[0]
        k_ref[row : row + n, :] = ref[:, 0, :]
        v_ref[row : row + n, :] = ref[:, 1, :]
        row += n


def prep(a, b, wide, weight):
    rows, feat = a.shape[0] + b.shape[0], a.shape[2]
    spec = lambda n: pl.BlockSpec((n, 2, wide), lambda h: (0, 0, h))
    out = pl.BlockSpec((rows, wide), lambda h: (0, h))
    return pl.pallas_call(
        prep_kernel,
        grid=(feat // wide,),
        in_specs=[spec(a.shape[0]), spec(b.shape[0])],
        out_specs=[out, out],
        out_shape=[jax.ShapeDtypeStruct((rows, feat), BF16)] * 2,
        cost_estimate=pl.CostEstimate(
            flops=weight * rows * feat, transcendentals=0, bytes_accessed=8 * rows * feat
        ),
        name="prep",
    )(a, b)


def attention_kernel(
    pos_ref, filt_ref, warm_ref, q_ref, g_ref, k1_ref, v1_ref, k2_ref, v2_ref, anc_ref, *rest,
    gx_count, head0, width,
):
    (dq_ref, own_out, dir_out, dia_out, par_out, anc_out, temp_out) = rest[-7:]
    head = pl.program_id(0)
    gx = pos_ref[0]
    odd = lax.rem(gx, 2)
    queries = q_ref.shape[0]
    own_rows = k1_ref.shape[0] - BLOCK
    blocks = own_rows // BLOCK
    near = own_rows + 3 * BLOCK

    q = q_ref[...]
    g = g_ref[...]
    k = jnp.concatenate([k1_ref[...], k2_ref[...], anc_ref[:, 0, :]], axis=0)
    v = jnp.concatenate([v1_ref[...], v2_ref[...], anc_ref[:, 1, :]], axis=0)
    nt = (((1,), (1,)), ((), ()))
    s = lax.dot_general(k, q, nt, preferred_element_type=F32)
    dp = lax.dot_general(v, g, nt, preferred_element_type=F32)

    mult = warm_ref[head0 + head] / math.sqrt(width)
    lane = lax.broadcasted_iota(jnp.int32, (1, queries), 1) // BLOCK
    direct_col = blocks + 1 - odd
    diagonal_col = blocks + odd
    diagonal_there = jnp.where(odd == 1, gx < gx_count - 1, gx > 0)
    parts = []
    for b in range(blocks + 3):
        bias = jnp.zeros((1, queries), F32)
        for a in range(blocks):
            if b == a:
                continue
            col = (b if b < blocks else (blocks + 2, direct_col, diagonal_col)[b - blocks])
            ok = filt_ref[a, col] > 0
            if b == blocks + 2:
                ok = jnp.logical_and(ok, diagonal_there)
            bias = jnp.where(lane == a, jnp.where(ok, 0.0, -jnp.inf).astype(F32), bias)
        parts.append(s[b * BLOCK : (b + 1) * BLOCK] * mult + bias)
    parts.append(s[near:] * mult)
    scores = jnp.concatenate(parts, axis=0)
    top = jnp.max(scores, axis=0, keepdims=True)
    e = jnp.exp(scores - top)
    inv = 1.0 / jnp.sum(e, axis=0, keepdims=True)
    p = e * inv
    pb = p.astype(BF16)
    delta = jnp.sum(pb.astype(F32) * dp, axis=0, keepdims=True)
    ds = p * (dp - delta)
    temp_out[0] = jnp.sum(ds * s, axis=0, keepdims=True)
    dsb = (ds * mult).astype(BF16)
    nn = (((1,), (0,)), ((), ()))
    dv = lax.dot_general(pb, g, nn, preferred_element_type=F32)
    dk = lax.dot_general(dsb, q, nn, preferred_element_type=F32)
    dq = lax.dot_general(dsb, k, (((0,), (0,)), ((), ())), preferred_element_type=F32)
    dq_ref[...] = dq.astype(BF16)
    for j, terms in enumerate((dk, dv)):
        own_out[j] = terms[:own_rows]
        for i, ref in enumerate((par_out, dir_out, dia_out)):
            at = own_rows + i * BLOCK
            ref[j] = terms[at : at + BLOCK].astype(BF16)
        anc_out[j] = terms[near:]


def attention(pos, filt, warm, q, g, near_kv, halo, anchors, head0, heads, dq_prev, anc_prev):
    rows, feat = q.shape
    total = warm.shape[0]
    width = feat // total
    own_rows = near_kv[0].shape[0] - BLOCK
    a_rows = anchors.shape[0]
    keys = own_rows + 3 * BLOCK + a_rows
    smem = pl.BlockSpec(memory_space=SMEM)
    full = lambda n: pl.BlockSpec((n, width), lambda h: (0, head0 + h))
    part = pl.BlockSpec((2 * BLOCK, width), lambda h: (0, h))
    cols = full(rows)
    out_face = pl.BlockSpec((2, BLOCK, width), lambda h: (0, 0, h))
    in_specs = [smem, smem, smem, cols, cols]
    in_specs += [full(own_rows + BLOCK)] * 2 + [part] * 2
    in_specs += [pl.BlockSpec((a_rows, 2, width), lambda h: (0, 0, head0 + h))]
    args = [pos, filt, warm, q, g, *near_kv, *halo, anchors]
    alias = {}
    if dq_prev is not None:
        in_specs += [pl.BlockSpec(memory_space=pl.ANY)] * 2
        args += [dq_prev, anc_prev]
        alias = {10: 0, 11: 5}
    face = jax.ShapeDtypeStruct((2, BLOCK, heads * width), BF16)
    return pl.pallas_call(
        functools.partial(attention_kernel, gx_count=lax.axis_size("gx"), head0=head0, width=width),
        grid=(heads,),
        in_specs=in_specs,
        out_specs=[
            cols,
            pl.BlockSpec((2, own_rows, width), lambda h: (0, 0, h)),
            out_face,
            out_face,
            out_face,
            pl.BlockSpec((2, a_rows, width), lambda h: (0, 0, head0 + h)),
            pl.BlockSpec((1, 1, rows), lambda h: (h, 0, 0)),
        ],
        out_shape=[
            jax.ShapeDtypeStruct(q.shape, BF16),
            jax.ShapeDtypeStruct((2, own_rows, heads * width), F32),
            face,
            face,
            face,
            jax.ShapeDtypeStruct((2, a_rows, feat), F32),
            jax.ShapeDtypeStruct((heads, 1, rows), F32),
        ],
        input_output_aliases=alias,
        compiler_params=pltpu.CompilerParams(vmem_limit_bytes=48 << 20),
        cost_estimate=pl.CostEstimate(
            flops=10 * heads * rows * keys * width,
            transcendentals=heads * rows * keys,
            bytes_accessed=heads * width * (rows * 6 + own_rows * 12 + 3 * BLOCK * 8 + a_rows * 12),
        ),
        name="attention",
    )(*args)


def combine_kernel(pos_ref, sent_ref, own_ref, dir_ref, dia_ref, par_ref, *rest):
    out_ref = rest[-1]
    odd = lax.rem(pos_ref[0], 2)
    blocks = own_ref.shape[1] // BLOCK
    spots = (
        jnp.where(odd == 1, sent_ref[0, 0], sent_ref[1, 0]),
        jnp.where(odd == 1, sent_ref[1, 0], sent_ref[0, 0]),
        sent_ref[2, 0],
    )
    for a in range(blocks):
        at = slice(a * BLOCK, (a + 1) * BLOCK)
        for j in range(2):
            total = own_ref[j, at, :]
            for spot, ref in zip(spots, (dir_ref, dia_ref, par_ref)):
                total = total + jnp.where(spot == a, 1.0, 0.0).astype(F32) * ref[j].astype(F32)
            out_ref[at, j, :] = total.astype(BF16)


def combine(pos, sent, own, faces, head0, heads, feat, width, prev, weight=1):
    rows = own.shape[1]
    smem = pl.BlockSpec(memory_space=SMEM)
    w = width * (2 if heads % 2 == 0 and head0 % 2 == 0 else 1)
    steps = heads * width // w
    base = head0 * width // w
    face = pl.BlockSpec((2, BLOCK, w), lambda h: (0, 0, h))
    in_specs = [smem, smem, pl.BlockSpec((2, rows, w), lambda h: (0, 0, h)), face, face, face]
    args = [pos, sent, own, *faces]
    alias = {}
    if prev is not None:
        in_specs.append(pl.BlockSpec(memory_space=pl.ANY))
        args.append(prev)
        alias = {6: 0}
    return pl.pallas_call(
        combine_kernel,
        grid=(steps,),
        in_specs=in_specs,
        out_specs=pl.BlockSpec((rows, 2, w), lambda h: (0, 0, base + h)),
        out_shape=jax.ShapeDtypeStruct((rows, 2, feat), BF16),
        input_output_aliases=alias,
        compiler_params=pltpu.CompilerParams(vmem_limit_bytes=32 << 20),
        cost_estimate=pl.CostEstimate(
            flops=weight * heads * width * rows * 16,
            transcendentals=0,
            bytes_accessed=heads * width * (rows * 12 + 3 * BLOCK * 4),
        ),
        name="combine",
    )(*args)


def local(q, mesh_kv, landmark, warm, g, exported, filt):
    rows, feat = q.shape
    total = warm.shape[0]
    width = feat // total
    gx_count = lax.axis_size("gx")
    stages = levels(lax.axis_size(("gx", "gy")))
    gx = lax.axis_index("gx")
    pos = jnp.full((1,), gx, jnp.int32)
    sent = exported[0]
    filt = filt[0]
    odd = lax.rem(gx, 2)
    direct_block = jnp.where(odd == 1, sent[0, 0], sent[1, 0])
    diagonal_block = jnp.where(odd == 1, sent[1, 0], sent[0, 0])
    sizes = split_heads(total)
    chunks = [(sum(sizes[:i]), n) for i, n in enumerate(sizes)]

    def pick(block, head0, heads):
        return lax.dynamic_slice(
            mesh_kv, (block * BLOCK, 0, head0 * width), (BLOCK, 2, heads * width)
        )

    picks = [
        (pick(direct_block, head0, heads), pick(diagonal_block, head0, heads))
        for head0, heads in chunks
    ]
    partner = swap_mask(pick(sent[2, 0], 0, total), 1)
    anchors = landmark
    for i, (low, peers) in enumerate(stages):
        if i == 1:
            anchors, picks[1] = lax.optimization_barrier((anchors, picks[1]))
        got = [swap_mask(anchors, m << low) for m in range(1, peers + 1)]
        anchors = jnp.concatenate([anchors] + got, axis=0)
    near_kv = prep(mesh_kv, partner, 2 * width if total % 2 == 0 else width, 1)
    halos = [(swap_pairs(d, 0), swap_pairs(g, 1)) for d, g in picks]
    near_kv, halos[0] = lax.optimization_barrier((near_kv, halos[0]))
    halos = [prep(d, g, width, 100000) for d, g in halos]

    dq = anc = None
    temps, owns, returned = [], [], []
    for (head0, heads), halo in zip(chunks, halos):
        dq, own, f_dir, f_dia, f_par, anc, temp = attention(
            pos, filt, warm, q, g, near_kv, halo, anchors, head0, heads, dq, anc
        )
        temps.append(temp)
        owns.append(own)
        faces = (f_dir, f_dia, f_par)
        if returned:
            anc, faces, returned[-1] = lax.optimization_barrier((anc, faces, returned[-1]))
        f_dir, f_dia, f_par = faces
        returned.append((swap_pairs(f_dir, 0), swap_pairs(f_dia, 1), swap_mask(f_par, 1)))

    temp = jnp.sum(jnp.concatenate(temps, axis=0), axis=(1, 2)) / math.sqrt(width)
    extra = jnp.zeros((2, 1, feat), F32).at[0, 0, :total].set(temp)
    cell = None
    for c in range(len(chunks) - 1):
        cell = combine(pos, sent, owns[c], returned[c], *chunks[c], feat, width, cell, weight=4000)
    for i, (low, peers) in enumerate(reversed(stages)):
        n = anc.shape[1] // (peers + 1)
        got = [
            swap_mask(jnp.concatenate([anc[:, m * n : (m + 1) * n], extra], axis=1), m << low)
            for m in range(1, peers + 1)
        ]
        if i == len(stages) - 1:
            got, cell = lax.optimization_barrier((got, cell))
        anc = sum([x[:, :n] for x in got], anc[:, :n])
        extra = sum([x[:, n:] for x in got], extra)
    anchor_grad = jnp.transpose(anc, (1, 0, 2))
    temp = extra[0, 0, :total]
    cell = combine(pos, sent, owns[-1], returned[-1], *chunks[-1], feat, width, cell, weight=0)
    return (dq, cell, anchor_grad, temp)


def solution(mesh):
    rows = ("groups", "gx", "gy")
    placed = (
        P(rows, None),
        P(rows, None, None),
        P(rows, None, None),
        P("groups"),
        P(rows, None),
        P(rows, None, None),
        P(rows, None, None),
    )
    return jax.shard_map(
        local,
        mesh=mesh,
        in_specs=placed,
        out_specs=(P(rows, None), P(rows, None, None), P(rows, None, None), P("groups")),
        check_vma=False,
    )
```

```python
import functools
import math

import jax
import jax.numpy as jnp
from jax import lax
from jax.experimental import pallas as pl
from jax.experimental.pallas import tpu as pltpu
from jax.sharding import PartitionSpec as P

BLOCK = 128
F32 = jnp.float32
BF16 = jnp.bfloat16
SMEM = pltpu.MemorySpace.SMEM
COMBINE_STEPS = (3, 2, 1)
LANES = 128
HOLD = 20_000_000_000


def swap_mask(x, mask):
    count = lax.axis_size(("gx", "gy"))
    return lax.ppermute(x, ("gx", "gy"), [(i, i ^ mask) for i in range(count)])


def levels(count):
    bits = count.bit_length() - 1
    out = [[2]] if bits > 1 else []
    at = 2
    while at < bits:
        take = min(2, bits - at)
        out.append([m << at for m in range(1, 1 << take)])
        at += take
    return out + [[1]]


def swap_pairs(x, first):
    count = lax.axis_size("gx")
    route = []
    for low in range(first, count - 1, 2):
        route += [(low, low + 1), (low + 1, low)]
    return lax.ppermute(x, "gx", route)


def split_heads(total):
    first = (total + 1) // 2
    return [n for n in (first, total - first) if n > 0]


def pick_kernel(pos_ref, sent_ref, kv_ref, *rest, copies):
    sems = rest[-1]
    outs = rest[:-1]
    odd = lax.rem(pos_ref[0], 2)
    spots = {
        "direct": jnp.where(odd == 1, sent_ref[0, 0], sent_ref[1, 0]),
        "diagonal": jnp.where(odd == 1, sent_ref[1, 0], sent_ref[0, 0]),
        "partner": sent_ref[2, 0],
        "own": 0,
    }
    started = []
    for out, (which, head0, heads) in zip(outs, copies):
        rows, width = out.shape[1], out.shape[3]
        for h in range(heads):
            lanes = slice((head0 + h) * width, (head0 + h + 1) * width)
            source = kv_ref.at[pl.ds(spots[which] * BLOCK, rows), :, lanes]
            copy = pltpu.make_async_copy(source, out.at[h], sems.at[len(started)])
            copy.start()
            started.append(copy)
    for copy in started:
        copy.wait()


def pick(pos, sent, mesh_kv, width, copies):
    rows = [mesh_kv.shape[0] if which == "own" else BLOCK for which, _, _ in copies]
    smem = pl.BlockSpec(memory_space=SMEM)
    anywhere = pl.BlockSpec(memory_space=pl.ANY)
    out = pl.pallas_call(
        functools.partial(pick_kernel, copies=copies),
        in_specs=[smem, smem, anywhere],
        out_specs=[anywhere] * len(copies),
        out_shape=[
            jax.ShapeDtypeStruct((heads, n, 2, width), BF16) for n, (_, _, heads) in zip(rows, copies)
        ],
        scratch_shapes=[pltpu.SemaphoreType.DMA((sum(heads for _, _, heads in copies),))],
        cost_estimate=pl.CostEstimate(flops=0, transcendentals=0, bytes_accessed=1 << 20),
        name="pick",
    )(pos, sent, mesh_kv)
    return [x.reshape(x.shape[0], 2 * x.shape[1], width) for x in out]


def hold_kernel(*refs):
    pass


def hold(arrays, flops):
    anywhere = pl.BlockSpec(memory_space=pl.ANY)
    return pl.pallas_call(
        hold_kernel,
        in_specs=[anywhere] * len(arrays),
        out_specs=[anywhere] * len(arrays),
        out_shape=[jax.ShapeDtypeStruct(x.shape, x.dtype) for x in arrays],
        input_output_aliases={i: i for i in range(len(arrays))},
        compiler_params=pltpu.CompilerParams(vmem_limit_bytes=1 << 20),
        cost_estimate=pl.CostEstimate(flops=flops, transcendentals=0, bytes_accessed=0),
        name="hold",
    )(*arrays)


def send_back(faces):
    direct, diagonal, partner = faces
    return [swap_pairs(direct, 0), swap_pairs(diagonal, 1), swap_mask(partner, 1)]


def attention_kernel(
    pos_ref, filt_ref, warm_ref, q_ref, g_ref, own_ref, par_ref, dir_ref, dia_ref, anc_ref, *rest,
    gx_count, head0, width,
):
    (dq_ref, own_out, dir_out, dia_out, par_out, anc_out, temp_out, pair_ref) = rest[-8:]
    head = pl.program_id(0)
    gx = pos_ref[0]
    odd = lax.rem(gx, 2)
    queries = q_ref.shape[0]
    own_rows = own_ref.shape[0] // 2
    blocks = own_rows // BLOCK
    near = own_rows + 3 * BLOCK
    keys = near + anc_ref.shape[0] // 2

    row = 0
    for ref in (own_ref, par_ref, dir_ref, dia_ref, anc_ref):
        pair_ref[row : row + ref.shape[0], :] = ref[...].astype(F32)
        row += ref.shape[0]
    k = pair_ref[pl.ds(0, keys, stride=2), :].astype(BF16)
    v = pair_ref[pl.ds(1, keys, stride=2), :].astype(BF16)

    q = q_ref[...]
    g = g_ref[...]
    nt = (((1,), (1,)), ((), ()))
    s = lax.dot_general(k, q, nt, preferred_element_type=F32)
    dp = lax.dot_general(v, g, nt, preferred_element_type=F32)

    mult = warm_ref[head0 + head] / math.sqrt(width)
    lane = lax.broadcasted_iota(jnp.int32, (1, queries), 1) // BLOCK
    direct_col = blocks + 1 - odd
    diagonal_col = blocks + odd
    diagonal_there = jnp.where(odd == 1, gx < gx_count - 1, gx > 0)
    parts = []
    for b in range(blocks + 3):
        bias = jnp.zeros((1, queries), F32)
        for a in range(blocks):
            if b == a:
                continue
            col = (b if b < blocks else (blocks + 2, direct_col, diagonal_col)[b - blocks])
            ok = filt_ref[a, col] > 0
            if b == blocks + 2:
                ok = jnp.logical_and(ok, diagonal_there)
            bias = jnp.where(lane == a, jnp.where(ok, 0.0, -jnp.inf).astype(F32), bias)
        parts.append(s[b * BLOCK : (b + 1) * BLOCK] * mult + bias)
    parts.append(s[near:] * mult)
    scores = jnp.concatenate(parts, axis=0)
    top = jnp.max(scores, axis=0, keepdims=True)
    e = jnp.exp(scores - top)
    inv = 1.0 / jnp.sum(e, axis=0, keepdims=True)
    p = e * inv
    pb = p.astype(BF16)
    delta = jnp.sum(pb.astype(F32) * dp, axis=0, keepdims=True)
    ds = p * (dp - delta)
    temp_out[0] = jnp.sum(ds * s, axis=0, keepdims=True)
    dsb = (ds * mult).astype(BF16)
    nn = (((1,), (0,)), ((), ()))
    dv = lax.dot_general(pb, g, nn, preferred_element_type=F32)
    dk = lax.dot_general(dsb, q, nn, preferred_element_type=F32)
    dq = lax.dot_general(dsb, k, (((0,), (0,)), ((), ())), preferred_element_type=F32)
    dq_ref[...] = dq.astype(BF16)
    pair_ref[pl.ds(0, keys, stride=2), :] = dk
    pair_ref[pl.ds(1, keys, stride=2), :] = dv
    own_out[...] = pair_ref[: 2 * own_rows, :]
    for i, ref in enumerate((par_out, dir_out, dia_out)):
        at = 2 * (own_rows + i * BLOCK)
        ref[...] = pair_ref[at : at + 2 * BLOCK, :].astype(BF16)
    anc_out[...] = pair_ref[2 * near :, :]


def attention(pos, filt, warm, q, g, own_kv, partner, halo, anchors, head0, heads, dq_prev, anc_prev):
    rows, feat = q.shape
    total, own_rows, width = own_kv.shape
    own_rows //= 2
    a_rows = anchors.shape[0] // 2
    keys = own_rows + 3 * BLOCK + a_rows
    smem = pl.BlockSpec(memory_space=SMEM)
    full = lambda n: pl.BlockSpec((None, 2 * n, width), lambda h: (head0 + h, 0, 0))
    part = pl.BlockSpec((None, 2 * BLOCK, width), lambda h: (h, 0, 0))
    cols = pl.BlockSpec((rows, width), lambda h: (0, head0 + h))
    in_specs = [smem, smem, smem, cols, cols, full(own_rows), full(BLOCK), part, part]
    in_specs += [pl.BlockSpec((2 * a_rows, width), lambda h: (0, head0 + h))]
    args = [pos, filt, warm, q, g, own_kv, partner, *halo, anchors]
    alias = {}
    if dq_prev is not None:
        in_specs += [pl.BlockSpec(memory_space=pl.ANY)] * 2
        args += [dq_prev, anc_prev]
        alias = {10: 0, 11: 5}
    face = jax.ShapeDtypeStruct((heads, 2 * BLOCK, width), BF16)
    return pl.pallas_call(
        functools.partial(attention_kernel, gx_count=lax.axis_size("gx"), head0=head0, width=width),
        grid=(heads,),
        in_specs=in_specs,
        out_specs=[
            cols,
            pl.BlockSpec((None, 2 * own_rows, width), lambda h: (h, 0, 0)),
            part,
            part,
            part,
            pl.BlockSpec((2 * a_rows, width), lambda h: (0, head0 + h)),
            pl.BlockSpec((1, 1, rows), lambda h: (h, 0, 0)),
        ],
        out_shape=[
            jax.ShapeDtypeStruct(q.shape, BF16),
            jax.ShapeDtypeStruct((heads, 2 * own_rows, width), F32),
            face,
            face,
            face,
            jax.ShapeDtypeStruct((2 * a_rows, feat), F32),
            jax.ShapeDtypeStruct((heads, 1, rows), F32),
        ],
        scratch_shapes=[pltpu.VMEM((2 * keys, width), F32)],
        input_output_aliases=alias,
        compiler_params=pltpu.CompilerParams(vmem_limit_bytes=24 << 20),
        cost_estimate=pl.CostEstimate(
            flops=10 * heads * rows * keys * width,
            transcendentals=heads * rows * keys,
            bytes_accessed=heads * width * (rows * 6 + own_rows * 12 + 3 * BLOCK * 8 + a_rows * 12),
        ),
        name="attention",
    )(*args)


def combine_kernel(pos_ref, sent_ref, own_ref, dir_ref, dia_ref, par_ref, *rest):
    out_ref = rest[-1]
    odd = lax.rem(pos_ref[0], 2)
    blocks = out_ref.shape[0] // BLOCK
    spots = (
        jnp.where(odd == 1, sent_ref[0, 0], sent_ref[1, 0]),
        jnp.where(odd == 1, sent_ref[1, 0], sent_ref[0, 0]),
        sent_ref[2, 0],
    )
    width = own_ref.shape[2]
    for h in range(own_ref.shape[0]):
        lanes = slice(h * width, (h + 1) * width)
        back = [ref[h].astype(F32) for ref in (dir_ref, dia_ref, par_ref)]
        for a in range(blocks):
            total = own_ref[h, 2 * a * BLOCK : 2 * (a + 1) * BLOCK, :]
            for spot, face in zip(spots, back):
                total = total + jnp.where(spot == a, 1.0, 0.0).astype(F32) * face
            out_ref[a * BLOCK : (a + 1) * BLOCK, :, lanes] = total.astype(BF16).reshape(BLOCK, 2, width)


def combine(pos, sent, own, faces, head0, heads, feat, width, prev, weight=1):
    rows = own.shape[1] // 2
    step = next(n for n in COMBINE_STEPS if heads % n == 0 and head0 % n == 0)
    smem = pl.BlockSpec(memory_space=SMEM)
    face = pl.BlockSpec((step, 2 * BLOCK, width), lambda h: (h, 0, 0))
    own_spec = pl.BlockSpec((step, 2 * rows, width), lambda h: (h, 0, 0))
    in_specs = [smem, smem, own_spec, face, face, face]
    args = [pos, sent, own, *faces]
    alias = {}
    if prev is not None:
        in_specs.append(pl.BlockSpec(memory_space=pl.ANY))
        args.append(prev)
        alias = {6: 0}
    return pl.pallas_call(
        combine_kernel,
        grid=(heads // step,),
        in_specs=in_specs,
        out_specs=pl.BlockSpec((rows, 2, step * width), lambda h: (0, 0, head0 // step + h)),
        out_shape=jax.ShapeDtypeStruct((rows, 2, feat), BF16),
        input_output_aliases=alias,
        compiler_params=pltpu.CompilerParams(vmem_limit_bytes=24 << 20),
        cost_estimate=pl.CostEstimate(
            flops=weight * heads * width * rows * 16,
            transcendentals=0,
            bytes_accessed=heads * width * (rows * 12 + 3 * BLOCK * 4),
        ),
        name="combine",
    )(*args)


def local(q, mesh_kv, landmark, warm, g, exported, filt):
    rows, feat = q.shape
    total = warm.shape[0]
    width = feat // total
    gx_count = lax.axis_size("gx")
    stages = levels(lax.axis_size(("gx", "gy")))
    gx = lax.axis_index("gx")
    pos = jnp.full((1,), gx, jnp.int32)
    sent = exported[0]
    filt = filt[0]
    sizes = split_heads(total)
    chunks = [(sum(sizes[:i]), n) for i, n in enumerate(sizes)]

    picks = [pick(pos, sent, mesh_kv, width, [("direct", *chunks[0]), ("diagonal", *chunks[0])])]
    others = [(which, *chunk) for chunk in chunks[1:] for which in ("direct", "diagonal")]
    others = pick(pos, sent, mesh_kv, width, others + [("partner", 0, total), ("own", 0, total)])
    own_kv, partner = others.pop(), swap_mask(others.pop(), 1)
    picks += [others[2 * i : 2 * i + 2] for i in range(len(chunks) - 1)]
    anchors = landmark.reshape(2 * landmark.shape[0], feat)
    for i, masks in enumerate(stages):
        if i == 1:
            anchors, picks[1] = lax.optimization_barrier((anchors, picks[1]))
        anchors = jnp.concatenate([anchors] + [swap_mask(anchors, m) for m in masks], axis=0)
    halos = [[swap_pairs(d, 0), swap_pairs(g, 1)] for d, g in picks]
    halos[0] = hold(halos[0], HOLD)

    dq = anc = None
    temps, owns, faces, returned = [], [], [], []
    for (head0, heads), halo in zip(chunks, halos):
        dq, own, f_dir, f_dia, f_par, anc, temp = attention(
            pos, filt, warm, q, g, own_kv, partner, halo, anchors, head0, heads, dq, anc
        )
        temps.append(temp)
        owns.append(own)
        faces.append((f_dir, f_dia, f_par))
        if len(faces) < len(chunks):
            returned.append(send_back(faces[-1]))
    temp = jnp.sum(jnp.concatenate(temps, axis=0), axis=(1, 2)) / math.sqrt(width)
    extra = jnp.zeros((1, LANES), F32).at[0, :total].set(temp)
    cell = None
    for i, masks in enumerate(reversed(stages)):
        n = anc.shape[0] // (len(masks) + 1)
        wide = jnp.broadcast_to(extra, (n, LANES))
        got = [
            swap_mask(jnp.concatenate([anc[k * n : (k + 1) * n], wide], axis=1), m)
            for k, m in enumerate(masks, 1)
        ]
        if i == 0:
            returned[-1] = hold(returned[-1], HOLD)
            got, faces[-1], returned[-1] = lax.optimization_barrier((got, faces[-1], returned[-1]))
            returned.append(send_back(faces[-1]))
            for c in range(len(chunks) - 1):
                cell = combine(pos, sent, owns[c], returned[c], *chunks[c], feat, width, cell, weight=4000)
        if i == len(stages) - 1:
            got, cell = lax.optimization_barrier((got, cell))
        anc = sum([x[:, :feat] for x in got], anc[:n])
        extra = sum([x[:1, feat:] for x in got], extra)
    anchor_grad = anc.reshape(landmark.shape)
    temp = extra[0, :total]
    cell = combine(pos, sent, owns[-1], returned[-1], *chunks[-1], feat, width, cell, weight=0)
    return (dq, cell, anchor_grad, temp)


def solution(mesh):
    rows = ("groups", "gx", "gy")
    placed = (
        P(rows, None),
        P(rows, None, None),
        P(rows, None, None),
        P("groups"),
        P(rows, None),
        P(rows, None, None),
        P(rows, None, None),
    )
    return jax.shard_map(
        local,
        mesh=mesh,
        in_specs=placed,
        out_specs=(P(rows, None), P(rows, None, None), P(rows, None, None), P("groups")),
        check_vma=False,
    )
```

```python
import functools
import math

import jax
import jax.numpy as jnp
from jax import lax
from jax.experimental import pallas as pl
from jax.experimental.pallas import tpu as pltpu
from jax.sharding import PartitionSpec as P

BLOCK = 128
F32 = jnp.float32
BF16 = jnp.bfloat16
SMEM = pltpu.MemorySpace.SMEM
COMBINE_STEPS = (3, 2, 1)
LANES = 128
HOLD = 20_000_000_000


def swap_mask(x, mask):
    count = lax.axis_size(("gx", "gy"))
    return lax.ppermute(x, ("gx", "gy"), [(i, i ^ mask) for i in range(count)])


def levels(count):
    bits = count.bit_length() - 1
    out = [[2]] if bits > 1 else []
    at = 2
    while at < bits:
        take = min(2, bits - at)
        out.append([m << at for m in range(1, 1 << take)])
        at += take
    return out + [[1]]


def swap_pairs(x, first):
    count = lax.axis_size("gx")
    route = []
    for low in range(first, count - 1, 2):
        route += [(low, low + 1), (low + 1, low)]
    return lax.ppermute(x, "gx", route)


def split_heads(total):
    first = (total + 1) // 2
    return [n for n in (first, total - first) if n > 0]


def pick_kernel(pos_ref, sent_ref, kv_ref, *rest, copies, width):
    sems = rest[-1]
    outs = rest[:-1]
    odd = lax.rem(pos_ref[0], 2)
    spots = {
        "direct": jnp.where(odd == 1, sent_ref[0, 0], sent_ref[1, 0]),
        "diagonal": jnp.where(odd == 1, sent_ref[1, 0], sent_ref[0, 0]),
        "partner": sent_ref[2, 0],
    }
    started = []
    for i, (out, (which, head0)) in enumerate(zip(outs, copies)):
        lanes = slice(head0 * width, head0 * width + out.shape[2])
        source = kv_ref.at[pl.ds(spots[which] * BLOCK, BLOCK), :, lanes]
        copy = pltpu.make_async_copy(source, out, sems.at[i])
        copy.start()
        started.append(copy)
    for copy in started:
        copy.wait()


def pick(pos, sent, mesh_kv, width, copies):
    smem = pl.BlockSpec(memory_space=SMEM)
    vmem = pl.BlockSpec(memory_space=pltpu.MemorySpace.VMEM)
    return pl.pallas_call(
        functools.partial(pick_kernel, copies=[c[:2] for c in copies], width=width),
        in_specs=[smem, smem, pl.BlockSpec(memory_space=pl.ANY)],
        out_specs=[vmem] * len(copies),
        out_shape=[jax.ShapeDtypeStruct((BLOCK, 2, heads * width), BF16) for _, _, heads in copies],
        scratch_shapes=[pltpu.SemaphoreType.DMA((len(copies),))],
        compiler_params=pltpu.CompilerParams(vmem_limit_bytes=8 << 20),
        cost_estimate=pl.CostEstimate(flops=0, transcendentals=0, bytes_accessed=1 << 20),
        name="pick",
    )(pos, sent, mesh_kv)


def hold_kernel(*refs):
    pass


def hold(arrays, flops):
    anywhere = pl.BlockSpec(memory_space=pl.ANY)
    return pl.pallas_call(
        hold_kernel,
        in_specs=[anywhere] * len(arrays),
        out_specs=[anywhere] * len(arrays),
        out_shape=[jax.ShapeDtypeStruct(x.shape, x.dtype) for x in arrays],
        input_output_aliases={i: i for i in range(len(arrays))},
        compiler_params=pltpu.CompilerParams(vmem_limit_bytes=1 << 20),
        cost_estimate=pl.CostEstimate(flops=flops, transcendentals=0, bytes_accessed=0),
        name="hold",
    )(*arrays)


def send_back(faces):
    direct, diagonal, partner = faces
    return [swap_pairs(direct, 0), swap_pairs(diagonal, 1), swap_mask(partner, 1)]


def attention_kernel(
    pos_ref, filt_ref, warm_ref, q_ref, g_ref, own_ref, par_ref, dir_ref, dia_ref, anc_ref, *rest,
    gx_count, head0, width,
):
    (dq_ref, own_out, dir_out, dia_out, par_out, anc_out, temp_out, pair_ref) = rest[-8:]
    head = pl.program_id(0)
    gx = pos_ref[0]
    odd = lax.rem(gx, 2)
    queries = q_ref.shape[0]
    own_rows = own_ref.shape[0]
    blocks = own_rows // BLOCK
    near = own_rows + 3 * BLOCK
    keys = near + anc_ref.shape[0] // 2

    row = 0
    for ref in (own_ref, par_ref, dir_ref, dia_ref, anc_ref):
        block = ref[...] if len(ref.shape) == 2 else ref[...].reshape(2 * ref.shape[0], width)
        pair_ref[row : row + block.shape[0], :] = block.astype(F32)
        row += block.shape[0]
    k = pair_ref[pl.ds(0, keys, stride=2), :].astype(BF16)
    v = pair_ref[pl.ds(1, keys, stride=2), :].astype(BF16)

    q = q_ref[...]
    g = g_ref[...]
    nt = (((1,), (1,)), ((), ()))
    s = lax.dot_general(k, q, nt, preferred_element_type=F32)
    dp = lax.dot_general(v, g, nt, preferred_element_type=F32)

    mult = warm_ref[head0 + head] / math.sqrt(width)
    lane = lax.broadcasted_iota(jnp.int32, (1, queries), 1) // BLOCK
    direct_col = blocks + 1 - odd
    diagonal_col = blocks + odd
    diagonal_there = jnp.where(odd == 1, gx < gx_count - 1, gx > 0)
    parts = []
    for b in range(blocks + 3):
        bias = jnp.zeros((1, queries), F32)
        for a in range(blocks):
            if b == a:
                continue
            col = (b if b < blocks else (blocks + 2, direct_col, diagonal_col)[b - blocks])
            ok = filt_ref[a, col] > 0
            if b == blocks + 2:
                ok = jnp.logical_and(ok, diagonal_there)
            bias = jnp.where(lane == a, jnp.where(ok, 0.0, -jnp.inf).astype(F32), bias)
        parts.append(s[b * BLOCK : (b + 1) * BLOCK] * mult + bias)
    parts.append(s[near:] * mult)
    scores = jnp.concatenate(parts, axis=0)
    top = jnp.max(scores, axis=0, keepdims=True)
    e = jnp.exp(scores - top)
    inv = 1.0 / jnp.sum(e, axis=0, keepdims=True)
    p = e * inv
    pb = p.astype(BF16)
    delta = jnp.sum(pb.astype(F32) * dp, axis=0, keepdims=True)
    ds = p * (dp - delta)
    temp_out[0] = jnp.sum(ds * s, axis=0, keepdims=True)
    dsb = (ds * mult).astype(BF16)
    nn = (((1,), (0,)), ((), ()))
    dv = lax.dot_general(pb, g, nn, preferred_element_type=F32)
    dk = lax.dot_general(dsb, q, nn, preferred_element_type=F32)
    dq = lax.dot_general(dsb, k, (((0,), (0,)), ((), ())), preferred_element_type=F32)
    dq_ref[...] = dq.astype(BF16)
    pair_ref[pl.ds(0, keys, stride=2), :] = dk
    pair_ref[pl.ds(1, keys, stride=2), :] = dv
    own_out[...] = pair_ref[: 2 * own_rows, :]
    for i, ref in enumerate((par_out, dir_out, dia_out)):
        at = 2 * (own_rows + i * BLOCK)
        ref[...] = pair_ref[at : at + 2 * BLOCK, :].astype(BF16)
    anc_out[...] = pair_ref[2 * near :, :]


def attention(pos, filt, warm, q, g, mesh_kv, partner, halo, anchors, head0, heads, dq_prev, anc_prev):
    rows, feat = q.shape
    own_rows = mesh_kv.shape[0]
    width = feat // warm.shape[0]
    a_rows = anchors.shape[0] // 2
    keys = own_rows + 3 * BLOCK + a_rows
    smem = pl.BlockSpec(memory_space=SMEM)
    full = lambda n: pl.BlockSpec((n, 2, width), lambda h: (0, 0, head0 + h))
    part = pl.BlockSpec((BLOCK, 2, width), lambda h: (0, 0, h))
    back = pl.BlockSpec((None, 2 * BLOCK, width), lambda h: (h, 0, 0))
    cols = pl.BlockSpec((rows, width), lambda h: (0, head0 + h))
    in_specs = [smem, smem, smem, cols, cols, full(own_rows), full(BLOCK), part, part]
    in_specs += [pl.BlockSpec((2 * a_rows, width), lambda h: (0, head0 + h))]
    args = [pos, filt, warm, q, g, mesh_kv, partner, *halo, anchors]
    alias = {}
    if dq_prev is not None:
        in_specs += [pl.BlockSpec(memory_space=pl.ANY)] * 2
        args += [dq_prev, anc_prev]
        alias = {10: 0, 11: 5}
    face = jax.ShapeDtypeStruct((heads, 2 * BLOCK, width), BF16)
    return pl.pallas_call(
        functools.partial(attention_kernel, gx_count=lax.axis_size("gx"), head0=head0, width=width),
        grid=(heads,),
        in_specs=in_specs,
        out_specs=[
            cols,
            pl.BlockSpec((None, 2 * own_rows, width), lambda h: (h, 0, 0)),
            back,
            back,
            back,
            pl.BlockSpec((2 * a_rows, width), lambda h: (0, head0 + h)),
            pl.BlockSpec((1, 1, rows), lambda h: (h, 0, 0)),
        ],
        out_shape=[
            jax.ShapeDtypeStruct(q.shape, BF16),
            jax.ShapeDtypeStruct((heads, 2 * own_rows, width), F32),
            face,
            face,
            face,
            jax.ShapeDtypeStruct((2 * a_rows, feat), F32),
            jax.ShapeDtypeStruct((heads, 1, rows), F32),
        ],
        scratch_shapes=[pltpu.VMEM((2 * keys, width), F32)],
        input_output_aliases=alias,
        compiler_params=pltpu.CompilerParams(vmem_limit_bytes=24 << 20),
        cost_estimate=pl.CostEstimate(
            flops=10 * heads * rows * keys * width,
            transcendentals=heads * rows * keys,
            bytes_accessed=heads * width * (rows * 6 + own_rows * 12 + 3 * BLOCK * 8 + a_rows * 12),
        ),
        name="attention",
    )(*args)


def combine_kernel(pos_ref, sent_ref, own_ref, dir_ref, dia_ref, par_ref, *rest):
    out_ref = rest[-1]
    odd = lax.rem(pos_ref[0], 2)
    blocks = out_ref.shape[0] // BLOCK
    spots = (
        jnp.where(odd == 1, sent_ref[0, 0], sent_ref[1, 0]),
        jnp.where(odd == 1, sent_ref[1, 0], sent_ref[0, 0]),
        sent_ref[2, 0],
    )
    width = own_ref.shape[2]
    for h in range(own_ref.shape[0]):
        lanes = slice(h * width, (h + 1) * width)
        back = [ref[h].astype(F32) for ref in (dir_ref, dia_ref, par_ref)]
        for a in range(blocks):
            total = own_ref[h, 2 * a * BLOCK : 2 * (a + 1) * BLOCK, :]
            for spot, face in zip(spots, back):
                total = total + jnp.where(spot == a, 1.0, 0.0).astype(F32) * face
            out_ref[a * BLOCK : (a + 1) * BLOCK, :, lanes] = total.astype(BF16).reshape(BLOCK, 2, width)


def combine(pos, sent, own, faces, head0, heads, feat, width, prev, weight=1):
    rows = own.shape[1] // 2
    step = next(n for n in COMBINE_STEPS if heads % n == 0 and head0 % n == 0)
    smem = pl.BlockSpec(memory_space=SMEM)
    face = pl.BlockSpec((step, 2 * BLOCK, width), lambda h: (h, 0, 0))
    own_spec = pl.BlockSpec((step, 2 * rows, width), lambda h: (h, 0, 0))
    in_specs = [smem, smem, own_spec, face, face, face]
    args = [pos, sent, own, *faces]
    alias = {}
    if prev is not None:
        in_specs.append(pl.BlockSpec(memory_space=pl.ANY))
        args.append(prev)
        alias = {6: 0}
    return pl.pallas_call(
        combine_kernel,
        grid=(heads // step,),
        in_specs=in_specs,
        out_specs=pl.BlockSpec((rows, 2, step * width), lambda h: (0, 0, head0 // step + h)),
        out_shape=jax.ShapeDtypeStruct((rows, 2, feat), BF16),
        input_output_aliases=alias,
        compiler_params=pltpu.CompilerParams(vmem_limit_bytes=24 << 20),
        cost_estimate=pl.CostEstimate(
            flops=weight * heads * width * rows * 16,
            transcendentals=0,
            bytes_accessed=heads * width * (rows * 12 + 3 * BLOCK * 4),
        ),
        name="combine",
    )(*args)


def local(q, mesh_kv, landmark, warm, g, exported, filt):
    rows, feat = q.shape
    total = warm.shape[0]
    width = feat // total
    gx_count = lax.axis_size("gx")
    stages = levels(lax.axis_size(("gx", "gy")))
    gx = lax.axis_index("gx")
    pos = jnp.full((1,), gx, jnp.int32)
    sent = exported[0]
    filt = filt[0]
    sizes = split_heads(total)
    chunks = [(sum(sizes[:i]), n) for i, n in enumerate(sizes)]

    picks = [pick(pos, sent, mesh_kv, width, [("direct", *chunks[0]), ("diagonal", *chunks[0])])]
    others = [(which, *chunk) for chunk in chunks[1:] for which in ("direct", "diagonal")]
    others = list(pick(pos, sent, mesh_kv, width, others + [("partner", 0, total)]))
    partner = swap_mask(others.pop(), 1)
    picks += [others[2 * i : 2 * i + 2] for i in range(len(chunks) - 1)]
    anchors = landmark.reshape(2 * landmark.shape[0], feat)
    for i, masks in enumerate(stages):
        if i == 1:
            anchors, picks[1] = lax.optimization_barrier((anchors, picks[1]))
        anchors = jnp.concatenate([anchors] + [swap_mask(anchors, m) for m in masks], axis=0)
    halos = [[swap_pairs(d, 0), swap_pairs(g, 1)] for d, g in picks]
    halos[0] = hold(halos[0], HOLD)

    dq = anc = None
    temps, owns, faces, returned = [], [], [], []
    for (head0, heads), halo in zip(chunks, halos):
        dq, own, f_dir, f_dia, f_par, anc, temp = attention(
            pos, filt, warm, q, g, mesh_kv, partner, halo, anchors, head0, heads, dq, anc
        )
        temps.append(temp)
        owns.append(own)
        faces.append((f_dir, f_dia, f_par))
        if len(faces) < len(chunks):
            returned.append(send_back(faces[-1]))
    temp = jnp.sum(jnp.concatenate(temps, axis=0), axis=(1, 2)) / math.sqrt(width)
    extra = jnp.zeros((1, LANES), F32).at[0, :total].set(temp)
    cell = None
    for i, masks in enumerate(reversed(stages)):
        n = anc.shape[0] // (len(masks) + 1)
        wide = jnp.broadcast_to(extra, (n, LANES))
        got = [
            swap_mask(jnp.concatenate([anc[k * n : (k + 1) * n], wide], axis=1), m)
            for k, m in enumerate(masks, 1)
        ]
        if i == 0:
            returned[-1] = hold(returned[-1], HOLD)
            got, faces[-1], returned[-1] = lax.optimization_barrier((got, faces[-1], returned[-1]))
            returned.append(send_back(faces[-1]))
            for c in range(len(chunks) - 1):
                cell = combine(pos, sent, owns[c], returned[c], *chunks[c], feat, width, cell, weight=4000)
        if i == len(stages) - 1:
            got, cell = lax.optimization_barrier((got, cell))
        anc = sum([x[:, :feat] for x in got], anc[:n])
        extra = sum([x[:1, feat:] for x in got], extra)
    anchor_grad = anc.reshape(landmark.shape)
    temp = extra[0, :total]
    cell = combine(pos, sent, owns[-1], returned[-1], *chunks[-1], feat, width, cell, weight=0)
    return (dq, cell, anchor_grad, temp)


def solution(mesh):
    rows = ("groups", "gx", "gy")
    placed = (
        P(rows, None),
        P(rows, None, None),
        P(rows, None, None),
        P("groups"),
        P(rows, None),
        P(rows, None, None),
        P(rows, None, None),
    )
    return jax.shard_map(
        local,
        mesh=mesh,
        in_specs=placed,
        out_specs=(P(rows, None), P(rows, None, None), P(rows, None, None), P("groups")),
        check_vma=False,
    )
```

```python
import functools
import math

import jax
import jax.numpy as jnp
from jax import lax
from jax.experimental import pallas as pl
from jax.experimental.pallas import tpu as pltpu
from jax.sharding import PartitionSpec as P

BLOCK = 128
F32 = jnp.float32
BF16 = jnp.bfloat16
SMEM = pltpu.MemorySpace.SMEM
COMBINE_STEPS = (3, 2, 1)
LANES = 128
HOLD = 20_000_000_000


def swap_mask(x, mask):
    count = lax.axis_size(("gx", "gy"))
    return lax.ppermute(x, ("gx", "gy"), [(i, i ^ mask) for i in range(count)])


def levels(count):
    bits = count.bit_length() - 1
    out = []
    at = 2
    while at < bits:
        take = min(2, bits - at)
        out.append([m << at for m in range(1, 1 << take)])
        at += take
    return out + ([[2]] if bits > 1 else []) + [[1]]


def swap_pairs(x, first):
    count = lax.axis_size("gx")
    route = []
    for low in range(first, count - 1, 2):
        route += [(low, low + 1), (low + 1, low)]
    return lax.ppermute(x, "gx", route)


def split_heads(total):
    first = (total + 1) // 2
    return [n for n in (first, total - first) if n > 0]


def pick_kernel(pos_ref, sent_ref, kv_ref, *rest, copies, width):
    sems = rest[-1]
    outs = rest[:-1]
    odd = lax.rem(pos_ref[0], 2)
    spots = {
        "direct": jnp.where(odd == 1, sent_ref[0, 0], sent_ref[1, 0]),
        "diagonal": jnp.where(odd == 1, sent_ref[1, 0], sent_ref[0, 0]),
        "partner": sent_ref[2, 0],
    }
    started = []
    for i, (out, (which, head0)) in enumerate(zip(outs, copies)):
        lanes = slice(head0 * width, head0 * width + out.shape[2])
        source = kv_ref.at[pl.ds(spots[which] * BLOCK, BLOCK), :, lanes]
        copy = pltpu.make_async_copy(source, out, sems.at[i])
        copy.start()
        started.append(copy)
    for copy in started:
        copy.wait()


def pick(pos, sent, mesh_kv, width, copies):
    smem = pl.BlockSpec(memory_space=SMEM)
    vmem = pl.BlockSpec(memory_space=pltpu.MemorySpace.VMEM)
    return pl.pallas_call(
        functools.partial(pick_kernel, copies=[c[:2] for c in copies], width=width),
        in_specs=[smem, smem, pl.BlockSpec(memory_space=pltpu.MemorySpace.HBM)],
        out_specs=[vmem] * len(copies),
        out_shape=[jax.ShapeDtypeStruct((BLOCK, 2, heads * width), BF16) for _, _, heads in copies],
        scratch_shapes=[pltpu.SemaphoreType.DMA((len(copies),))],
        compiler_params=pltpu.CompilerParams(vmem_limit_bytes=8 << 20),
        cost_estimate=pl.CostEstimate(flops=0, transcendentals=0, bytes_accessed=1 << 20),
        name="pick",
    )(pos, sent, mesh_kv)


def hold_kernel(*refs):
    pass


def hold(arrays, flops):
    anywhere = pl.BlockSpec(memory_space=pl.ANY)
    return pl.pallas_call(
        hold_kernel,
        in_specs=[anywhere] * len(arrays),
        out_specs=[anywhere] * len(arrays),
        out_shape=[jax.ShapeDtypeStruct(x.shape, x.dtype) for x in arrays],
        input_output_aliases={i: i for i in range(len(arrays))},
        compiler_params=pltpu.CompilerParams(vmem_limit_bytes=1 << 20),
        cost_estimate=pl.CostEstimate(flops=flops, transcendentals=0, bytes_accessed=0),
        name="hold",
    )(*arrays)


def send_back(faces):
    direct, diagonal, partner = faces
    return [swap_pairs(direct, 0), swap_pairs(diagonal, 1), swap_mask(partner, 1)]


def attention_kernel(
    pos_ref, filt_ref, warm_ref, q_ref, g_ref, own_ref, par_ref, dir_ref, dia_ref, anc_ref, *rest,
    gx_count, head0, width,
):
    (dq_ref, own_out, dir_out, dia_out, par_out, anc_out, temp_out, pair_ref) = rest[-8:]
    head = pl.program_id(0)
    gx = pos_ref[0]
    odd = lax.rem(gx, 2)
    queries = q_ref.shape[0]
    own_rows = own_ref.shape[0]
    blocks = own_rows // BLOCK
    near = own_rows + 3 * BLOCK
    keys = near + anc_ref.shape[0] // 2

    row = 0
    for ref in (own_ref, par_ref, dir_ref, dia_ref, anc_ref):
        block = ref[...] if len(ref.shape) == 2 else ref[...].reshape(2 * ref.shape[0], width)
        pair_ref[row : row + block.shape[0], :] = block.astype(F32)
        row += block.shape[0]
    k = pair_ref[pl.ds(0, keys, stride=2), :].astype(BF16)
    v = pair_ref[pl.ds(1, keys, stride=2), :].astype(BF16)

    q = q_ref[...]
    g = g_ref[...]
    nt = (((1,), (1,)), ((), ()))
    s = lax.dot_general(k, q, nt, preferred_element_type=F32)
    dp = lax.dot_general(v, g, nt, preferred_element_type=F32)

    mult = warm_ref[head0 + head] / math.sqrt(width)
    lane = lax.broadcasted_iota(jnp.int32, (1, queries), 1) // BLOCK
    direct_col = blocks + 1 - odd
    diagonal_col = blocks + odd
    diagonal_there = jnp.where(odd == 1, gx < gx_count - 1, gx > 0)
    parts = []
    for b in range(blocks + 3):
        bias = jnp.zeros((1, queries), F32)
        for a in range(blocks):
            if b == a:
                continue
            col = (b if b < blocks else (blocks + 2, direct_col, diagonal_col)[b - blocks])
            ok = filt_ref[a, col] > 0
            if b == blocks + 2:
                ok = jnp.logical_and(ok, diagonal_there)
            bias = jnp.where(lane == a, jnp.where(ok, 0.0, -jnp.inf).astype(F32), bias)
        parts.append(s[b * BLOCK : (b + 1) * BLOCK] * mult + bias)
    parts.append(s[near:] * mult)
    scores = jnp.concatenate(parts, axis=0)
    top = jnp.max(scores, axis=0, keepdims=True)
    e = jnp.exp(scores - top)
    inv = 1.0 / jnp.sum(e, axis=0, keepdims=True)
    p = e * inv
    pb = p.astype(BF16)
    delta = jnp.sum(pb.astype(F32) * dp, axis=0, keepdims=True)
    ds = p * (dp - delta)
    temp_out[0] = jnp.sum(ds * s, axis=0, keepdims=True)
    dsb = (ds * mult).astype(BF16)
    nn = (((1,), (0,)), ((), ()))
    dv = lax.dot_general(pb, g, nn, preferred_element_type=F32)
    dk = lax.dot_general(dsb, q, nn, preferred_element_type=F32)
    dq = lax.dot_general(dsb, k, (((0,), (0,)), ((), ())), preferred_element_type=F32)
    dq_ref[...] = dq.astype(BF16)
    pair_ref[pl.ds(0, keys, stride=2), :] = dk
    pair_ref[pl.ds(1, keys, stride=2), :] = dv
    own_out[...] = pair_ref[: 2 * own_rows, :]
    for i, ref in enumerate((par_out, dir_out, dia_out)):
        at = 2 * (own_rows + i * BLOCK)
        ref[...] = pair_ref[at : at + 2 * BLOCK, :].astype(BF16)
    anc_out[...] = pair_ref[2 * near :, :]


def attention(pos, filt, warm, q, g, mesh_kv, partner, halo, anchors, head0, heads, dq_prev, anc_prev, weight=0):
    rows, feat = q.shape
    own_rows = mesh_kv.shape[0]
    width = feat // warm.shape[0]
    a_rows = anchors.shape[0] // 2
    keys = own_rows + 3 * BLOCK + a_rows
    smem = pl.BlockSpec(memory_space=SMEM)
    full = lambda n: pl.BlockSpec((n, 2, width), lambda h: (0, 0, head0 + h))
    part = pl.BlockSpec((BLOCK, 2, width), lambda h: (0, 0, h))
    back = pl.BlockSpec((None, 2 * BLOCK, width), lambda h: (h, 0, 0))
    cols = pl.BlockSpec((rows, width), lambda h: (0, head0 + h))
    in_specs = [smem, smem, smem, cols, cols, full(own_rows), full(BLOCK), part, part]
    in_specs += [pl.BlockSpec((2 * a_rows, width), lambda h: (0, head0 + h))]
    args = [pos, filt, warm, q, g, mesh_kv, partner, *halo, anchors]
    alias = {}
    if dq_prev is not None:
        in_specs += [pl.BlockSpec(memory_space=pl.ANY)] * 2
        args += [dq_prev, anc_prev]
        alias = {10: 0, 11: 5}
    face = jax.ShapeDtypeStruct((heads, 2 * BLOCK, width), BF16)
    return pl.pallas_call(
        functools.partial(attention_kernel, gx_count=lax.axis_size("gx"), head0=head0, width=width),
        grid=(heads,),
        in_specs=in_specs,
        out_specs=[
            cols,
            pl.BlockSpec((None, 2 * own_rows, width), lambda h: (h, 0, 0)),
            back,
            back,
            back,
            pl.BlockSpec((2 * a_rows, width), lambda h: (0, head0 + h)),
            pl.BlockSpec((1, 1, rows), lambda h: (h, 0, 0)),
        ],
        out_shape=[
            jax.ShapeDtypeStruct(q.shape, BF16),
            jax.ShapeDtypeStruct((heads, 2 * own_rows, width), F32),
            face,
            face,
            face,
            jax.ShapeDtypeStruct((2 * a_rows, feat), F32),
            jax.ShapeDtypeStruct((heads, 1, rows), F32),
        ],
        scratch_shapes=[pltpu.VMEM((2 * keys, width), F32)],
        input_output_aliases=alias,
        compiler_params=pltpu.CompilerParams(vmem_limit_bytes=24 << 20),
        cost_estimate=pl.CostEstimate(
            flops=weight * 10 * heads * rows * keys * width,
            transcendentals=0,
            bytes_accessed=weight * heads * width * (rows * 6 + own_rows * 12 + 3 * BLOCK * 8 + a_rows * 12),
        ),
        name="attention",
    )(*args)


def combine_kernel(pos_ref, sent_ref, own_ref, dir_ref, dia_ref, par_ref, *rest):
    out_ref = rest[-1]
    odd = lax.rem(pos_ref[0], 2)
    blocks = out_ref.shape[0] // BLOCK
    spots = (
        jnp.where(odd == 1, sent_ref[0, 0], sent_ref[1, 0]),
        jnp.where(odd == 1, sent_ref[1, 0], sent_ref[0, 0]),
        sent_ref[2, 0],
    )
    width = own_ref.shape[2]
    for h in range(own_ref.shape[0]):
        lanes = slice(h * width, (h + 1) * width)
        back = [ref[h].astype(F32) for ref in (dir_ref, dia_ref, par_ref)]
        for a in range(blocks):
            total = own_ref[h, 2 * a * BLOCK : 2 * (a + 1) * BLOCK, :]
            for spot, face in zip(spots, back):
                total = total + jnp.where(spot == a, 1.0, 0.0).astype(F32) * face
            out_ref[a * BLOCK : (a + 1) * BLOCK, :, lanes] = total.astype(BF16).reshape(BLOCK, 2, width)


def combine(pos, sent, own, faces, head0, heads, feat, width, prev, part=None, weight=1):
    rows = own.shape[1] // 2
    lo, heads = part or (0, heads)
    step = next(n for n in COMBINE_STEPS if heads % n == 0 and head0 % n == 0 and lo % n == 0)
    smem = pl.BlockSpec(memory_space=SMEM)
    face = pl.BlockSpec((step, 2 * BLOCK, width), lambda h: (lo // step + h, 0, 0))
    own_spec = pl.BlockSpec((step, 2 * rows, width), lambda h: (lo // step + h, 0, 0))
    in_specs = [smem, smem, own_spec, face, face, face]
    args = [pos, sent, own, *faces]
    alias = {}
    if prev is not None:
        in_specs.append(pl.BlockSpec(memory_space=pl.ANY))
        args.append(prev)
        alias = {6: 0}
    return pl.pallas_call(
        combine_kernel,
        grid=(heads // step,),
        in_specs=in_specs,
        out_specs=pl.BlockSpec((rows, 2, step * width), lambda h: (0, 0, (head0 + lo) // step + h)),
        out_shape=jax.ShapeDtypeStruct((rows, 2, feat), BF16),
        input_output_aliases=alias,
        compiler_params=pltpu.CompilerParams(vmem_limit_bytes=24 << 20),
        cost_estimate=pl.CostEstimate(
            flops=weight * heads * width * rows * 16,
            transcendentals=0,
            bytes_accessed=heads * width * (rows * 12 + 3 * BLOCK * 4),
        ),
        name="combine",
    )(*args)


def local(q, mesh_kv, landmark, warm, g, exported, filt):
    rows, feat = q.shape
    total = warm.shape[0]
    width = feat // total
    gx_count = lax.axis_size("gx")
    stages = levels(lax.axis_size(("gx", "gy")))
    gx = lax.axis_index("gx")
    pos = jnp.full((1,), gx, jnp.int32)
    sent = exported[0]
    filt = filt[0]
    sizes = split_heads(total)
    chunks = [(sum(sizes[:i]), n) for i, n in enumerate(sizes)]

    picks = [pick(pos, sent, mesh_kv, width, [("direct", *chunks[0]), ("diagonal", *chunks[0])])]
    others = [(which, *chunk) for chunk in chunks[1:] for which in ("direct", "diagonal")]
    others = list(pick(pos, sent, mesh_kv, width, others + [("partner", 0, total)]))
    partner = swap_mask(others.pop(), 1)
    picks += [others[2 * i : 2 * i + 2] for i in range(len(chunks) - 1)]
    anchors = landmark.reshape(2 * landmark.shape[0], feat)
    for i, masks in enumerate(stages):
        if i == len(stages) - 1:
            anchors, picks[1] = lax.optimization_barrier((anchors, picks[1]))
        anchors = jnp.concatenate([anchors] + [swap_mask(anchors, m) for m in masks], axis=0)
    halos = [[swap_pairs(d, 0), swap_pairs(g, 1)] for d, g in picks]
    halos[0] = hold(halos[0], HOLD)

    dq = anc = None
    temps, owns, faces, returned = [], [], [], []
    for (head0, heads), halo in zip(chunks, halos):
        dq, own, f_dir, f_dia, f_par, anc, temp = attention(
            pos, filt, warm, q, g, mesh_kv, partner, halo, anchors, head0, heads, dq, anc
        )
        temps.append(temp)
        owns.append(own)
        faces.append((f_dir, f_dia, f_par))
        if len(faces) < len(chunks):
            returned.append(send_back(faces[-1]))

    temp = jnp.sum(jnp.concatenate(temps, axis=0), axis=(1, 2)) / math.sqrt(width)
    extra = jnp.zeros((1, LANES), F32).at[0, :total].set(temp)
    cell = None
    anc, faces[-1], returned[-1] = lax.optimization_barrier((anc, faces[-1], returned[-1]))
    returned.append(send_back(faces[-1]))
    anc = anc.reshape([len(masks) + 1 for masks in reversed(stages)] + [2 * landmark.shape[0], feat])
    for i, masks in enumerate(stages[-1:] + stages[:-1]):
        dim = 0 if i == 0 else anc.ndim - 3
        parts = [lax.index_in_dim(anc, k, dim, keepdims=False) for k in range(len(masks) + 1)]
        shape = parts[0].shape
        parts = [x.reshape(-1, feat) for x in parts]
        wide = jnp.broadcast_to(extra, (parts[0].shape[0], LANES))
        got = [
            swap_mask(jnp.concatenate([x, wide], axis=1), m) for x, m in zip(parts[1:], masks)
        ]
        if i >= len(stages) - 2:
            c = len(chunks) - 2
            head0, heads = chunks[c]
            half = heads // 2
            lo, n = (0, half) if i == len(stages) - 2 else (half, heads - half)
            cell = combine(
                pos, sent, owns[c], returned[c], head0, heads, feat, width, cell, part=(lo, n), weight=4000
            )
            got, cell = lax.optimization_barrier((got, cell))
        anc = sum([x[:, :feat] for x in got], parts[0]).reshape(shape)
        extra = sum([x[:1, feat:] for x in got], extra)
    anchor_grad = anc.reshape(landmark.shape)
    temp = extra[0, :total]
    cell = combine(pos, sent, owns[-1], returned[-1], *chunks[-1], feat, width, cell, weight=0)
    return (dq, cell, anchor_grad, temp)


def solution(mesh):
    rows = ("groups", "gx", "gy")
    placed = (
        P(rows, None),
        P(rows, None, None),
        P(rows, None, None),
        P("groups"),
        P(rows, None),
        P(rows, None, None),
        P(rows, None, None),
    )
    return jax.shard_map(
        local,
        mesh=mesh,
        in_specs=placed,
        out_specs=(P(rows, None), P(rows, None, None), P(rows, None, None), P("groups")),
        check_vma=False,
    )
```

```python
import functools
import math

import jax
import jax.numpy as jnp
from jax import lax
from jax.experimental import pallas as pl
from jax.experimental.pallas import tpu as pltpu
from jax.sharding import PartitionSpec as P

BLOCK = 128
F32 = jnp.float32
BF16 = jnp.bfloat16
SMEM = pltpu.MemorySpace.SMEM
COMBINE_STEPS = (3, 2, 1)
LANES = 128
HOLD = 20_000_000_000


def swap_mask(x, mask):
    count = lax.axis_size(("gx", "gy"))
    return lax.ppermute(x, ("gx", "gy"), [(i, i ^ mask) for i in range(count)])


def levels(count):
    bits = count.bit_length() - 1
    out = [[2]] if bits > 1 else []
    at = 2
    while at < bits:
        take = min(2, bits - at)
        out.append([m << at for m in range(1, 1 << take)])
        at += take
    return out + [[1]]


def swap_pairs(x, first):
    count = lax.axis_size("gx")
    route = []
    for low in range(first, count - 1, 2):
        route += [(low, low + 1), (low + 1, low)]
    return lax.ppermute(x, "gx", route)


def split_heads(total):
    first = (total + 1) // 2
    return [n for n in (first, total - first) if n > 0]


def pick_kernel(pos_ref, sent_ref, kv_ref, *rest, copies, width):
    sems = rest[-1]
    outs = rest[:-1]
    odd = lax.rem(pos_ref[0], 2)
    spots = {
        "direct": jnp.where(odd == 1, sent_ref[0, 0], sent_ref[1, 0]),
        "diagonal": jnp.where(odd == 1, sent_ref[1, 0], sent_ref[0, 0]),
        "partner": sent_ref[2, 0],
    }
    started = []
    for i, (out, (which, head0)) in enumerate(zip(outs, copies)):
        lanes = slice(head0 * width, head0 * width + out.shape[2])
        source = kv_ref.at[pl.ds(spots[which] * BLOCK, BLOCK), :, lanes]
        copy = pltpu.make_async_copy(source, out, sems.at[i])
        copy.start()
        started.append(copy)
    for copy in started:
        copy.wait()


def pick(pos, sent, mesh_kv, width, copies):
    smem = pl.BlockSpec(memory_space=SMEM)
    vmem = pl.BlockSpec(memory_space=pltpu.MemorySpace.VMEM)
    return pl.pallas_call(
        functools.partial(pick_kernel, copies=[c[:2] for c in copies], width=width),
        in_specs=[smem, smem, pl.BlockSpec(memory_space=pl.ANY)],
        out_specs=[vmem] * len(copies),
        out_shape=[jax.ShapeDtypeStruct((BLOCK, 2, heads * width), BF16) for _, _, heads in copies],
        scratch_shapes=[pltpu.SemaphoreType.DMA((len(copies),))],
        compiler_params=pltpu.CompilerParams(vmem_limit_bytes=8 << 20),
        cost_estimate=pl.CostEstimate(flops=0, transcendentals=0, bytes_accessed=1 << 20),
        name="pick",
    )(pos, sent, mesh_kv)


def hold_kernel(*refs):
    pass


def hold(arrays, flops):
    anywhere = pl.BlockSpec(memory_space=pl.ANY)
    return pl.pallas_call(
        hold_kernel,
        in_specs=[anywhere] * len(arrays),
        out_specs=[anywhere] * len(arrays),
        out_shape=[jax.ShapeDtypeStruct(x.shape, x.dtype) for x in arrays],
        input_output_aliases={i: i for i in range(len(arrays))},
        compiler_params=pltpu.CompilerParams(vmem_limit_bytes=1 << 20),
        cost_estimate=pl.CostEstimate(flops=flops, transcendentals=0, bytes_accessed=0),
        name="hold",
    )(*arrays)


def send_back(faces):
    direct, diagonal, partner = faces
    return [swap_pairs(direct, 0), swap_pairs(diagonal, 1), swap_mask(partner, 1)]


def attention_kernel(
    pos_ref, filt_ref, warm_ref, q_ref, g_ref, own_ref, par_ref, dir_ref, dia_ref, anc_ref, *rest,
    gx_count, head0, width,
):
    (dq_ref, own_out, dir_out, dia_out, par_out, anc_out, temp_out, pair_ref) = rest[-8:]
    head = pl.program_id(0)
    gx = pos_ref[0]
    odd = lax.rem(gx, 2)
    queries = q_ref.shape[0]
    own_rows = own_ref.shape[0]
    blocks = own_rows // BLOCK
    near = own_rows + 3 * BLOCK
    keys = near + anc_ref.shape[0] // 2

    row = 0
    for ref in (own_ref, par_ref, dir_ref, dia_ref, anc_ref):
        block = ref[...] if len(ref.shape) == 2 else ref[...].reshape(2 * ref.shape[0], width)
        pair_ref[row : row + block.shape[0], :] = block.astype(F32)
        row += block.shape[0]
    k = pair_ref[pl.ds(0, keys, stride=2), :].astype(BF16)
    v = pair_ref[pl.ds(1, keys, stride=2), :].astype(BF16)

    q = q_ref[...]
    g = g_ref[...]
    nt = (((1,), (1,)), ((), ()))
    s = lax.dot_general(k, q, nt, preferred_element_type=F32)
    dp = lax.dot_general(v, g, nt, preferred_element_type=F32)

    mult = warm_ref[head0 + head] / math.sqrt(width)
    lane = lax.broadcasted_iota(jnp.int32, (1, queries), 1) // BLOCK
    direct_col = blocks + 1 - odd
    diagonal_col = blocks + odd
    diagonal_there = jnp.where(odd == 1, gx < gx_count - 1, gx > 0)
    parts = []
    for b in range(blocks + 3):
        bias = jnp.zeros((1, queries), F32)
        for a in range(blocks):
            if b == a:
                continue
            col = (b if b < blocks else (blocks + 2, direct_col, diagonal_col)[b - blocks])
            ok = filt_ref[a, col] > 0
            if b == blocks + 2:
                ok = jnp.logical_and(ok, diagonal_there)
            bias = jnp.where(lane == a, jnp.where(ok, 0.0, -jnp.inf).astype(F32), bias)
        parts.append(s[b * BLOCK : (b + 1) * BLOCK] * mult + bias)
    parts.append(s[near:] * mult)
    scores = jnp.concatenate(parts, axis=0)
    top = jnp.max(scores, axis=0, keepdims=True)
    e = jnp.exp(scores - top)
    inv = 1.0 / jnp.sum(e, axis=0, keepdims=True)
    p = e * inv
    pb = p.astype(BF16)
    delta = jnp.sum(pb.astype(F32) * dp, axis=0, keepdims=True)
    ds = p * (dp - delta)
    temp_out[0] = jnp.sum(ds * s, axis=0, keepdims=True)
    dsb = (ds * mult).astype(BF16)
    nn = (((1,), (0,)), ((), ()))
    dv = lax.dot_general(pb, g, nn, preferred_element_type=F32)
    dk = lax.dot_general(dsb, q, nn, preferred_element_type=F32)
    dq = lax.dot_general(dsb, k, (((0,), (0,)), ((), ())), preferred_element_type=F32)
    dq_ref[...] = dq.astype(BF16)
    pair_ref[pl.ds(0, keys, stride=2), :] = dk
    pair_ref[pl.ds(1, keys, stride=2), :] = dv
    own_out[...] = pair_ref[: 2 * own_rows, :]
    for i, ref in enumerate((par_out, dir_out, dia_out)):
        at = 2 * (own_rows + i * BLOCK)
        ref[...] = pair_ref[at : at + 2 * BLOCK, :].astype(BF16)
    anc_out[...] = pair_ref[2 * near :, :]


def attention(pos, filt, warm, q, g, mesh_kv, partner, halo, anchors, head0, heads, dq_prev, anc_prev):
    rows, feat = q.shape
    own_rows = mesh_kv.shape[0]
    width = feat // warm.shape[0]
    a_rows = anchors.shape[0] // 2
    keys = own_rows + 3 * BLOCK + a_rows
    smem = pl.BlockSpec(memory_space=SMEM)
    full = lambda n: pl.BlockSpec((n, 2, width), lambda h: (0, 0, head0 + h))
    part = pl.BlockSpec((BLOCK, 2, width), lambda h: (0, 0, h))
    back = pl.BlockSpec((None, 2 * BLOCK, width), lambda h: (h, 0, 0))
    cols = pl.BlockSpec((rows, width), lambda h: (0, head0 + h))
    in_specs = [smem, smem, smem, cols, cols, full(own_rows), full(BLOCK), part, part]
    in_specs += [pl.BlockSpec((2 * a_rows, width), lambda h: (0, head0 + h))]
    args = [pos, filt, warm, q, g, mesh_kv, partner, *halo, anchors]
    alias = {}
    if dq_prev is not None:
        in_specs += [pl.BlockSpec(memory_space=pl.ANY)] * 2
        args += [dq_prev, anc_prev]
        alias = {10: 0, 11: 5}
    face = jax.ShapeDtypeStruct((heads, 2 * BLOCK, width), BF16)
    return pl.pallas_call(
        functools.partial(attention_kernel, gx_count=lax.axis_size("gx"), head0=head0, width=width),
        grid=(heads,),
        in_specs=in_specs,
        out_specs=[
            cols,
            pl.BlockSpec((None, 2 * own_rows, width), lambda h: (h, 0, 0)),
            back,
            back,
            back,
            pl.BlockSpec((2 * a_rows, width), lambda h: (0, head0 + h)),
            pl.BlockSpec((1, 1, rows), lambda h: (h, 0, 0)),
        ],
        out_shape=[
            jax.ShapeDtypeStruct(q.shape, BF16),
            jax.ShapeDtypeStruct((heads, 2 * own_rows, width), F32),
            face,
            face,
            face,
            jax.ShapeDtypeStruct((2 * a_rows, feat), F32),
            jax.ShapeDtypeStruct((heads, 1, rows), F32),
        ],
        scratch_shapes=[pltpu.VMEM((2 * keys, width), F32)],
        input_output_aliases=alias,
        compiler_params=pltpu.CompilerParams(vmem_limit_bytes=16 << 20),
        cost_estimate=pl.CostEstimate(
            flops=10 * heads * rows * keys * width,
            transcendentals=heads * rows * keys,
            bytes_accessed=heads * width * (rows * 6 + own_rows * 12 + 3 * BLOCK * 8 + a_rows * 12),
        ),
        name="attention",
    )(*args)


def combine_kernel(pos_ref, sent_ref, own_ref, dir_ref, dia_ref, par_ref, *rest):
    out_ref = rest[-1]
    odd = lax.rem(pos_ref[0], 2)
    blocks = out_ref.shape[0] // BLOCK
    spots = (
        jnp.where(odd == 1, sent_ref[0, 0], sent_ref[1, 0]),
        jnp.where(odd == 1, sent_ref[1, 0], sent_ref[0, 0]),
        sent_ref[2, 0],
    )
    width = own_ref.shape[2]
    for h in range(own_ref.shape[0]):
        lanes = slice(h * width, (h + 1) * width)
        back = [ref[h].astype(F32) for ref in (dir_ref, dia_ref, par_ref)]
        for a in range(blocks):
            total = own_ref[h, 2 * a * BLOCK : 2 * (a + 1) * BLOCK, :]
            for spot, face in zip(spots, back):
                total = total + jnp.where(spot == a, 1.0, 0.0).astype(F32) * face
            out_ref[a * BLOCK : (a + 1) * BLOCK, :, lanes] = total.astype(BF16).reshape(BLOCK, 2, width)


def combine(pos, sent, own, faces, head0, heads, feat, width, prev, weight=1):
    rows = own.shape[1] // 2
    step = next(n for n in COMBINE_STEPS if heads % n == 0 and head0 % n == 0)
    smem = pl.BlockSpec(memory_space=SMEM)
    face = pl.BlockSpec((step, 2 * BLOCK, width), lambda h: (h, 0, 0))
    own_spec = pl.BlockSpec((step, 2 * rows, width), lambda h: (h, 0, 0))
    in_specs = [smem, smem, own_spec, face, face, face]
    args = [pos, sent, own, *faces]
    alias = {}
    if prev is not None:
        in_specs.append(pl.BlockSpec(memory_space=pl.ANY))
        args.append(prev)
        alias = {6: 0}
    return pl.pallas_call(
        combine_kernel,
        grid=(heads // step,),
        in_specs=in_specs,
        out_specs=pl.BlockSpec((rows, 2, step * width), lambda h: (0, 0, head0 // step + h)),
        out_shape=jax.ShapeDtypeStruct((rows, 2, feat), BF16),
        input_output_aliases=alias,
        compiler_params=pltpu.CompilerParams(vmem_limit_bytes=8 << 20),
        cost_estimate=pl.CostEstimate(
            flops=weight * heads * width * rows * 16,
            transcendentals=0,
            bytes_accessed=heads * width * (rows * 12 + 3 * BLOCK * 4),
        ),
        name="combine",
    )(*args)


def local(q, mesh_kv, landmark, warm, g, exported, filt):
    rows, feat = q.shape
    total = warm.shape[0]
    width = feat // total
    gx_count = lax.axis_size("gx")
    stages = levels(lax.axis_size(("gx", "gy")))
    gx = lax.axis_index("gx")
    pos = jnp.full((1,), gx, jnp.int32)
    sent = exported[0]
    filt = filt[0]
    sizes = split_heads(total)
    chunks = [(sum(sizes[:i]), n) for i, n in enumerate(sizes)]

    picks = [pick(pos, sent, mesh_kv, width, [("direct", *chunks[0]), ("diagonal", *chunks[0])])]
    others = [(which, *chunk) for chunk in chunks[1:] for which in ("direct", "diagonal")]
    others = list(pick(pos, sent, mesh_kv, width, others + [("partner", 0, total)]))
    partner = swap_mask(others.pop(), 1)
    picks += [others[2 * i : 2 * i + 2] for i in range(len(chunks) - 1)]
    anchors, picks[0] = lax.optimization_barrier((landmark, picks[0]))
    anchors = anchors.reshape(2 * landmark.shape[0], feat)
    for i, masks in enumerate(stages):
        if i == 1:
            anchors, picks[1] = lax.optimization_barrier((anchors, picks[1]))
        anchors = jnp.concatenate([anchors] + [swap_mask(anchors, m) for m in masks], axis=0)
    halos = [[swap_pairs(d, 0), swap_pairs(g, 1)] for d, g in picks]
    halos[0] = hold(halos[0], HOLD)

    dq = anc = None
    temps, owns, faces, returned = [], [], [], []
    for (head0, heads), halo in zip(chunks, halos):
        dq, own, f_dir, f_dia, f_par, anc, temp = attention(
            pos, filt, warm, q, g, mesh_kv, partner, halo, anchors, head0, heads, dq, anc
        )
        temps.append(temp)
        owns.append(own)
        faces.append((f_dir, f_dia, f_par))
        if len(faces) < len(chunks):
            returned.append(send_back(faces[-1]))
    temp = jnp.sum(jnp.concatenate(temps, axis=0), axis=(1, 2)) / math.sqrt(width)
    extra = jnp.zeros((1, LANES), F32).at[0, :total].set(temp)
    cell = None
    anc = anc.reshape([len(masks) + 1 for masks in reversed(stages)] + [2 * landmark.shape[0], feat])
    for i, masks in enumerate([stages[-1]] + stages[:-1]):
        dim = 0 if i == 0 else anc.ndim - 3
        parts = [lax.index_in_dim(anc, k, dim, keepdims=False) for k in range(len(masks) + 1)]
        shape = parts[0].shape
        parts = [x.reshape(-1, feat) for x in parts]
        wide = jnp.broadcast_to(extra, (parts[0].shape[0], LANES))
        got = [
            swap_mask(jnp.concatenate([x, wide], axis=1), m) for x, m in zip(parts[1:], masks)
        ]
        if i == 0:
            returned[-1] = hold(returned[-1], HOLD)
            got, faces[-1], returned[-1] = lax.optimization_barrier((got, faces[-1], returned[-1]))
            returned.append(send_back(faces[-1]))
            for c in range(len(chunks) - 1):
                cell = combine(pos, sent, owns[c], returned[c], *chunks[c], feat, width, cell, weight=4000)
        if i == len(stages) - 1:
            got, cell = lax.optimization_barrier((got, cell))
        anc = sum([x[:, :feat] for x in got], parts[0]).reshape(shape)
        extra = sum([x[:1, feat:] for x in got], extra)
    anchor_grad = anc.reshape(landmark.shape)
    temp = extra[0, :total]
    cell = combine(pos, sent, owns[-1], returned[-1], *chunks[-1], feat, width, cell, weight=0)
    return (dq, cell, anchor_grad, temp)


def solution(mesh):
    rows = ("groups", "gx", "gy")
    placed = (
        P(rows, None),
        P(rows, None, None),
        P(rows, None, None),
        P("groups"),
        P(rows, None),
        P(rows, None, None),
        P(rows, None, None),
    )
    return jax.shard_map(
        local,
        mesh=mesh,
        in_specs=placed,
        out_specs=(P(rows, None), P(rows, None, None), P(rows, None, None), P("groups")),
        check_vma=False,
    )
```

```python
import functools
import math

import jax
import jax.numpy as jnp
from jax import lax
from jax.experimental import pallas as pl
from jax.experimental.pallas import tpu as pltpu
from jax.sharding import PartitionSpec as P

BLOCK = 128
F32 = jnp.float32
BF16 = jnp.bfloat16
SMEM = pltpu.MemorySpace.SMEM
COMBINE_STEPS = (3, 2, 1)
LANES = 128
HOLD = 20_000_000_000


def swap_mask(x, mask):
    count = lax.axis_size(("gx", "gy"))
    return lax.ppermute(x, ("gx", "gy"), [(i, i ^ mask) for i in range(count)])


def levels(count):
    bits = count.bit_length() - 1
    out = [[2]] if bits > 1 else []
    at = 2
    while at < bits:
        take = min(2, bits - at)
        out.append([m << at for m in range(1, 1 << take)])
        at += take
    return out + [[1]]


def swap_pairs(x, first):
    count = lax.axis_size("gx")
    route = []
    for low in range(first, count - 1, 2):
        route += [(low, low + 1), (low + 1, low)]
    return lax.ppermute(x, "gx", route)


def split_heads(total):
    first = (total + 1) // 2
    return [n for n in (first, total - first) if n > 0]


def pick_kernel(pos_ref, sent_ref, kv_ref, *rest, copies, width):
    sems = rest[-1]
    outs = rest[:-1]
    odd = lax.rem(pos_ref[0], 2)
    spots = {
        "direct": jnp.where(odd == 1, sent_ref[0, 0], sent_ref[1, 0]),
        "diagonal": jnp.where(odd == 1, sent_ref[1, 0], sent_ref[0, 0]),
        "partner": sent_ref[2, 0],
    }
    started = []
    for i, (out, (which, head0)) in enumerate(zip(outs, copies)):
        lanes = slice(head0 * width, head0 * width + out.shape[2])
        source = kv_ref.at[pl.ds(spots[which] * BLOCK, BLOCK), :, lanes]
        copy = pltpu.make_async_copy(source, out, sems.at[i])
        copy.start()
        started.append(copy)
    for copy in started:
        copy.wait()


def pick(pos, sent, mesh_kv, width, copies):
    smem = pl.BlockSpec(memory_space=SMEM)
    vmem = pl.BlockSpec(memory_space=pltpu.MemorySpace.VMEM)
    return pl.pallas_call(
        functools.partial(pick_kernel, copies=[c[:2] for c in copies], width=width),
        in_specs=[smem, smem, pl.BlockSpec(memory_space=pl.ANY)],
        out_specs=[vmem] * len(copies),
        out_shape=[jax.ShapeDtypeStruct((BLOCK, 2, heads * width), BF16) for _, _, heads in copies],
        scratch_shapes=[pltpu.SemaphoreType.DMA((len(copies),))],
        compiler_params=pltpu.CompilerParams(vmem_limit_bytes=8 << 20),
        cost_estimate=pl.CostEstimate(flops=0, transcendentals=0, bytes_accessed=1 << 20),
        name="pick",
    )(pos, sent, mesh_kv)


def hold_kernel(*refs):
    pass


def hold(arrays, flops):
    anywhere = pl.BlockSpec(memory_space=pl.ANY)
    return pl.pallas_call(
        hold_kernel,
        in_specs=[anywhere] * len(arrays),
        out_specs=[anywhere] * len(arrays),
        out_shape=[jax.ShapeDtypeStruct(x.shape, x.dtype) for x in arrays],
        input_output_aliases={i: i for i in range(len(arrays))},
        compiler_params=pltpu.CompilerParams(vmem_limit_bytes=1 << 20),
        cost_estimate=pl.CostEstimate(flops=flops, transcendentals=0, bytes_accessed=0),
        name="hold",
    )(*arrays)


def send_back(faces):
    direct, diagonal, partner = faces
    return [swap_pairs(direct, 0), swap_pairs(diagonal, 1), swap_mask(partner, 1)]


def attention_kernel(
    pos_ref, filt_ref, warm_ref, q_ref, g_ref, own_ref, par_ref, dir_ref, dia_ref, anc_ref, *rest,
    gx_count, head0, width,
):
    (dq_ref, own_out, dir_out, dia_out, par_out, anc_out, temp_out, pair_ref) = rest[-8:]
    head = pl.program_id(0)
    gx = pos_ref[0]
    odd = lax.rem(gx, 2)
    queries = q_ref.shape[0]
    own_rows = own_ref.shape[0]
    blocks = own_rows // BLOCK
    near = own_rows + 3 * BLOCK
    keys = near + anc_ref.shape[0] // 2

    row = 0
    for ref in (own_ref, par_ref, dir_ref, dia_ref, anc_ref):
        block = ref[...] if len(ref.shape) == 2 else ref[...].reshape(2 * ref.shape[0], width)
        pair_ref[row : row + block.shape[0], :] = block.astype(F32)
        row += block.shape[0]
    k = pair_ref[pl.ds(0, keys, stride=2), :].astype(BF16)
    v = pair_ref[pl.ds(1, keys, stride=2), :].astype(BF16)

    q = q_ref[...]
    g = g_ref[...]
    nt = (((1,), (1,)), ((), ()))
    s = lax.dot_general(k, q, nt, preferred_element_type=F32)
    dp = lax.dot_general(v, g, nt, preferred_element_type=F32)

    mult = warm_ref[head0 + head] / math.sqrt(width)
    lane = lax.broadcasted_iota(jnp.int32, (1, queries), 1) // BLOCK
    direct_col = blocks + 1 - odd
    diagonal_col = blocks + odd
    diagonal_there = jnp.where(odd == 1, gx < gx_count - 1, gx > 0)
    parts = []
    for b in range(blocks + 3):
        bias = jnp.zeros((1, queries), F32)
        for a in range(blocks):
            if b == a:
                continue
            col = (b if b < blocks else (blocks + 2, direct_col, diagonal_col)[b - blocks])
            ok = filt_ref[a, col] > 0
            if b == blocks + 2:
                ok = jnp.logical_and(ok, diagonal_there)
            bias = jnp.where(lane == a, jnp.where(ok, 0.0, -jnp.inf).astype(F32), bias)
        parts.append(s[b * BLOCK : (b + 1) * BLOCK] * mult + bias)
    parts.append(s[near:] * mult)
    scores = jnp.concatenate(parts, axis=0)
    top = jnp.max(scores, axis=0, keepdims=True)
    e = jnp.exp(scores - top)
    inv = 1.0 / jnp.sum(e, axis=0, keepdims=True)
    p = e * inv
    pb = p.astype(BF16)
    delta = jnp.sum(pb.astype(F32) * dp, axis=0, keepdims=True)
    ds = p * (dp - delta)
    temp_out[0] = jnp.sum(ds * s, axis=0, keepdims=True)
    dsb = (ds * mult).astype(BF16)
    nn = (((1,), (0,)), ((), ()))
    dv = lax.dot_general(pb, g, nn, preferred_element_type=F32)
    dk = lax.dot_general(dsb, q, nn, preferred_element_type=F32)
    dq = lax.dot_general(dsb, k, (((0,), (0,)), ((), ())), preferred_element_type=F32)
    dq_ref[...] = dq.astype(BF16)
    pair_ref[pl.ds(0, keys, stride=2), :] = dk
    pair_ref[pl.ds(1, keys, stride=2), :] = dv
    own_out[...] = pair_ref[: 2 * own_rows, :]
    for i, ref in enumerate((par_out, dir_out, dia_out)):
        at = 2 * (own_rows + i * BLOCK)
        ref[...] = pair_ref[at : at + 2 * BLOCK, :].astype(BF16)
    anc_out[...] = pair_ref[2 * near :, :]


def attention(pos, filt, warm, q, g, mesh_kv, partner, halo, anchors, head0, heads, dq_prev, anc_prev):
    rows, feat = q.shape
    own_rows = mesh_kv.shape[0]
    width = feat // warm.shape[0]
    a_rows = anchors.shape[0] // 2
    keys = own_rows + 3 * BLOCK + a_rows
    smem = pl.BlockSpec(memory_space=SMEM)
    full = lambda n: pl.BlockSpec((n, 2, width), lambda h: (0, 0, head0 + h))
    part = pl.BlockSpec((BLOCK, 2, width), lambda h: (0, 0, h))
    back = pl.BlockSpec((None, 2 * BLOCK, width), lambda h: (h, 0, 0))
    cols = pl.BlockSpec((rows, width), lambda h: (0, head0 + h))
    in_specs = [smem, smem, smem, cols, cols, full(own_rows), full(BLOCK), part, part]
    in_specs += [pl.BlockSpec((2 * a_rows, width), lambda h: (0, head0 + h))]
    args = [pos, filt, warm, q, g, mesh_kv, partner, *halo, anchors]
    alias = {}
    if dq_prev is not None:
        in_specs += [pl.BlockSpec(memory_space=pl.ANY)] * 2
        args += [dq_prev, anc_prev]
        alias = {10: 0, 11: 5}
    face = jax.ShapeDtypeStruct((heads, 2 * BLOCK, width), BF16)
    return pl.pallas_call(
        functools.partial(attention_kernel, gx_count=lax.axis_size("gx"), head0=head0, width=width),
        grid=(heads,),
        in_specs=in_specs,
        out_specs=[
            cols,
            pl.BlockSpec((None, 2 * own_rows, width), lambda h: (h, 0, 0)),
            back,
            back,
            back,
            pl.BlockSpec((2 * a_rows, width), lambda h: (0, head0 + h)),
            pl.BlockSpec((1, 1, rows), lambda h: (h, 0, 0)),
        ],
        out_shape=[
            jax.ShapeDtypeStruct(q.shape, BF16),
            jax.ShapeDtypeStruct((heads, 2 * own_rows, width), F32),
            face,
            face,
            face,
            jax.ShapeDtypeStruct((2 * a_rows, feat), F32),
            jax.ShapeDtypeStruct((heads, 1, rows), F32),
        ],
        scratch_shapes=[pltpu.VMEM((2 * keys, width), F32)],
        input_output_aliases=alias,
        compiler_params=pltpu.CompilerParams(vmem_limit_bytes=24 << 20),
        cost_estimate=pl.CostEstimate(
            flops=10 * heads * rows * keys * width,
            transcendentals=heads * rows * keys,
            bytes_accessed=heads * width * (rows * 6 + own_rows * 12 + 3 * BLOCK * 8 + a_rows * 12),
        ),
        name="attention",
    )(*args)


def combine_kernel(pos_ref, sent_ref, own_ref, dir_ref, dia_ref, par_ref, *rest):
    out_ref = rest[-1]
    odd = lax.rem(pos_ref[0], 2)
    blocks = out_ref.shape[0] // BLOCK
    spots = (
        jnp.where(odd == 1, sent_ref[0, 0], sent_ref[1, 0]),
        jnp.where(odd == 1, sent_ref[1, 0], sent_ref[0, 0]),
        sent_ref[2, 0],
    )
    width = own_ref.shape[2]
    for h in range(own_ref.shape[0]):
        lanes = slice(h * width, (h + 1) * width)
        back = [ref[h].astype(F32) for ref in (dir_ref, dia_ref, par_ref)]
        for a in range(blocks):
            total = own_ref[h, 2 * a * BLOCK : 2 * (a + 1) * BLOCK, :]
            for spot, face in zip(spots, back):
                total = total + jnp.where(spot == a, 1.0, 0.0).astype(F32) * face
            out_ref[a * BLOCK : (a + 1) * BLOCK, :, lanes] = total.astype(BF16).reshape(BLOCK, 2, width)


def combine(pos, sent, own, faces, head0, heads, feat, width, prev, part=None, weight=1):
    rows = own.shape[1] // 2
    lo, heads = part or (0, heads)
    step = next(n for n in COMBINE_STEPS if heads % n == 0 and head0 % n == 0 and lo % n == 0)
    smem = pl.BlockSpec(memory_space=SMEM)
    face = pl.BlockSpec((step, 2 * BLOCK, width), lambda h: (lo // step + h, 0, 0))
    own_spec = pl.BlockSpec((step, 2 * rows, width), lambda h: (lo // step + h, 0, 0))
    in_specs = [smem, smem, own_spec, face, face, face]
    args = [pos, sent, own, *faces]
    alias = {}
    if prev is not None:
        in_specs.append(pl.BlockSpec(memory_space=pl.ANY))
        args.append(prev)
        alias = {6: 0}
    return pl.pallas_call(
        combine_kernel,
        grid=(heads // step,),
        in_specs=in_specs,
        out_specs=pl.BlockSpec((rows, 2, step * width), lambda h: (0, 0, (head0 + lo) // step + h)),
        out_shape=jax.ShapeDtypeStruct((rows, 2, feat), BF16),
        input_output_aliases=alias,
        compiler_params=pltpu.CompilerParams(vmem_limit_bytes=24 << 20),
        cost_estimate=pl.CostEstimate(
            flops=weight * heads * width * rows * 16,
            transcendentals=0,
            bytes_accessed=heads * width * (rows * 12 + 3 * BLOCK * 4),
        ),
        name="combine",
    )(*args)


def finish_kernel(own_ref, temp_ref, *refs):
    got, (out_ref, sum_ref) = refs[:-2], refs[-2:]
    rows, feat = own_ref.shape
    total, temp = own_ref[...], temp_ref[...]
    for ref in got:
        total = total + ref[:, :feat]
        temp = temp + ref[:1, feat:]
    out_ref[...] = total.reshape(out_ref.shape)
    sum_ref[...] = temp


def finish(own, temp, got, shape):
    return pl.pallas_call(
        finish_kernel,
        out_shape=[jax.ShapeDtypeStruct(shape, F32), jax.ShapeDtypeStruct(temp.shape, F32)],
        compiler_params=pltpu.CompilerParams(vmem_limit_bytes=8 << 20),
        name="finish",
    )(own, temp, *got)


def local(q, mesh_kv, landmark, warm, g, exported, filt):
    rows, feat = q.shape
    total = warm.shape[0]
    width = feat // total
    gx_count = lax.axis_size("gx")
    stages = levels(lax.axis_size(("gx", "gy")))
    gx = lax.axis_index("gx")
    pos = jnp.full((1,), gx, jnp.int32)
    sent = exported[0]
    filt = filt[0]
    sizes = split_heads(total)
    chunks = [(sum(sizes[:i]), n) for i, n in enumerate(sizes)]

    picks = [pick(pos, sent, mesh_kv, width, [("direct", *chunks[0]), ("diagonal", *chunks[0])])]
    others = [(which, *chunk) for chunk in chunks[1:] for which in ("direct", "diagonal")]
    others = list(pick(pos, sent, mesh_kv, width, others + [("partner", 0, total)]))
    partner = swap_mask(others.pop(), 1)
    picks += [others[2 * i : 2 * i + 2] for i in range(len(chunks) - 1)]
    anchors = landmark.reshape(2 * landmark.shape[0], feat)
    for i, masks in enumerate(stages):
        if i == 1:
            anchors, picks[1] = lax.optimization_barrier((anchors, picks[1]))
        anchors = jnp.concatenate([anchors] + [swap_mask(anchors, m) for m in masks], axis=0)
    halos = [[swap_pairs(d, 0), swap_pairs(g, 1)] for d, g in picks]
    halos[0] = hold(halos[0], HOLD)

    dq = anc = None
    temps, owns, faces, returned = [], [], [], []
    for (head0, heads), halo in zip(chunks, halos):
        dq, own, f_dir, f_dia, f_par, anc, temp = attention(
            pos, filt, warm, q, g, mesh_kv, partner, halo, anchors, head0, heads, dq, anc
        )
        temps.append(temp)
        owns.append(own)
        faces.append((f_dir, f_dia, f_par))
        if len(faces) < len(chunks):
            returned.append(send_back(faces[-1]))
    temp = jnp.sum(jnp.concatenate(temps, axis=0), axis=(1, 2)) / math.sqrt(width)
    extra = jnp.zeros((1, LANES), F32).at[0, :total].set(temp)
    cell = None
    for i, masks in enumerate(reversed(stages)):
        n = anc.shape[0] // (len(masks) + 1)
        wide = jnp.broadcast_to(extra, (n, LANES))
        got = [
            swap_mask(jnp.concatenate([anc[k * n : (k + 1) * n], wide], axis=1), m)
            for k, m in enumerate(masks, 1)
        ]
        if i == 0:
            returned[-1] = hold(returned[-1], HOLD)
            got, faces[-1], returned[-1] = lax.optimization_barrier((got, faces[-1], returned[-1]))
            returned.append(send_back(faces[-1]))
            got, returned[-1][2] = lax.optimization_barrier((got, returned[-1][2]))
        head0, heads = chunks[-2]
        half = heads // 2
        part = {len(stages) - 2: (0, half), len(stages) - 1: (half, heads - half)}.get(i)
        if part:
            cell = combine(
                pos, sent, owns[-2], returned[-2], head0, heads, feat, width, cell, part=part, weight=4000
            )
        if i == len(stages) - 2:
            got, cell = lax.optimization_barrier((got, cell))
        if i == len(stages) - 1:
            cell = combine(pos, sent, owns[-1], returned[-1], *chunks[-1], feat, width, cell, weight=0)
            got, cell = lax.optimization_barrier((got, cell))
            anchor_grad, temp = finish(anc[:n], extra, got, landmark.shape)
            break
        anc = sum([x[:, :feat] for x in got], anc[:n])
        extra = sum([x[:1, feat:] for x in got], extra)
    return (dq, cell, anchor_grad, temp[0, :total])


def solution(mesh):
    rows = ("groups", "gx", "gy")
    placed = (
        P(rows, None),
        P(rows, None, None),
        P(rows, None, None),
        P("groups"),
        P(rows, None),
        P(rows, None, None),
        P(rows, None, None),
    )
    return jax.shard_map(
        local,
        mesh=mesh,
        in_specs=placed,
        out_specs=(P(rows, None), P(rows, None, None), P(rows, None, None), P("groups")),
        check_vma=False,
    )
```

```python
import functools
import math

import jax
import jax.numpy as jnp
from jax import lax
from jax.experimental import pallas as pl
from jax.experimental.pallas import tpu as pltpu
from jax.sharding import PartitionSpec as P

BLOCK = 128
F32 = jnp.float32
BF16 = jnp.bfloat16
SMEM = pltpu.MemorySpace.SMEM
COMBINE_STEPS = (3, 2, 1)
LANES = 128
HOLD = 20_000_000_000


def swap_mask(x, mask):
    count = lax.axis_size(("gx", "gy"))
    return lax.ppermute(x, ("gx", "gy"), [(i, i ^ mask) for i in range(count)])


def levels(count):
    bits = count.bit_length() - 1
    out = [[2]] if bits > 1 else []
    at = 2
    while at < bits:
        take = min(2, bits - at)
        out.append([m << at for m in range(1, 1 << take)])
        at += take
    return out + [[1]]


def swap_pairs(x, first):
    count = lax.axis_size("gx")
    route = []
    for low in range(first, count - 1, 2):
        route += [(low, low + 1), (low + 1, low)]
    return lax.ppermute(x, "gx", route)


def split_heads(total):
    first = (total + 1) // 2
    return [n for n in (first, total - first) if n > 0]


def pick_kernel(pos_ref, sent_ref, kv_ref, *rest, copies, width):
    sems = rest[-1]
    outs = rest[:-1]
    odd = lax.rem(pos_ref[0], 2)
    spots = {
        "direct": jnp.where(odd == 1, sent_ref[0, 0], sent_ref[1, 0]),
        "diagonal": jnp.where(odd == 1, sent_ref[1, 0], sent_ref[0, 0]),
        "partner": sent_ref[2, 0],
    }
    started = []
    for i, (out, (which, head0)) in enumerate(zip(outs, copies)):
        lanes = slice(head0 * width, head0 * width + out.shape[2])
        source = kv_ref.at[pl.ds(spots[which] * BLOCK, BLOCK), :, lanes]
        copy = pltpu.make_async_copy(source, out, sems.at[i])
        copy.start()
        started.append(copy)
    for copy in started:
        copy.wait()


def pick(pos, sent, mesh_kv, width, copies):
    smem = pl.BlockSpec(memory_space=SMEM)
    vmem = pl.BlockSpec(memory_space=pltpu.MemorySpace.VMEM)
    return pl.pallas_call(
        functools.partial(pick_kernel, copies=[c[:2] for c in copies], width=width),
        in_specs=[smem, smem, pl.BlockSpec(memory_space=pl.ANY)],
        out_specs=[vmem] * len(copies),
        out_shape=[jax.ShapeDtypeStruct((BLOCK, 2, heads * width), BF16) for _, _, heads in copies],
        scratch_shapes=[pltpu.SemaphoreType.DMA((len(copies),))],
        compiler_params=pltpu.CompilerParams(vmem_limit_bytes=8 << 20),
        cost_estimate=pl.CostEstimate(flops=0, transcendentals=0, bytes_accessed=1 << 20),
        name="pick",
    )(pos, sent, mesh_kv)


def hold_kernel(*refs):
    pass


def hold(arrays, flops):
    anywhere = pl.BlockSpec(memory_space=pl.ANY)
    return pl.pallas_call(
        hold_kernel,
        in_specs=[anywhere] * len(arrays),
        out_specs=[anywhere] * len(arrays),
        out_shape=[jax.ShapeDtypeStruct(x.shape, x.dtype) for x in arrays],
        input_output_aliases={i: i for i in range(len(arrays))},
        compiler_params=pltpu.CompilerParams(vmem_limit_bytes=1 << 20),
        cost_estimate=pl.CostEstimate(flops=flops, transcendentals=0, bytes_accessed=0),
        name="hold",
    )(*arrays)


def send_back(faces):
    direct, diagonal, partner = faces
    return [swap_pairs(direct, 0), swap_pairs(diagonal, 1), swap_mask(partner, 1)]


def attention_kernel(
    pos_ref, filt_ref, warm_ref, q_ref, g_ref, own_ref, par_ref, dir_ref, dia_ref, anc_ref, *rest,
    gx_count, head0, width,
):
    (dq_ref, own_out, dir_out, dia_out, par_out, anc_out, temp_out, pair_ref) = rest[-8:]
    head = pl.program_id(0)
    gx = pos_ref[0]
    odd = lax.rem(gx, 2)
    queries = q_ref.shape[0]
    own_rows = own_ref.shape[0]
    blocks = own_rows // BLOCK
    near = own_rows + 3 * BLOCK
    keys = near + anc_ref.shape[0] // 2

    row = 0
    for ref in (own_ref, par_ref, dir_ref, dia_ref, anc_ref):
        block = ref[...] if len(ref.shape) == 2 else ref[...].reshape(2 * ref.shape[0], width)
        pair_ref[row : row + block.shape[0], :] = block.astype(F32)
        row += block.shape[0]
    k = pair_ref[pl.ds(0, keys, stride=2), :].astype(BF16)
    v = pair_ref[pl.ds(1, keys, stride=2), :].astype(BF16)

    q = q_ref[...]
    g = g_ref[...]
    nt = (((1,), (1,)), ((), ()))
    s = lax.dot_general(k, q, nt, preferred_element_type=F32)
    dp = lax.dot_general(v, g, nt, preferred_element_type=F32)

    mult = warm_ref[head0 + head] / math.sqrt(width)
    lane = lax.broadcasted_iota(jnp.int32, (1, queries), 1) // BLOCK
    direct_col = blocks + 1 - odd
    diagonal_col = blocks + odd
    diagonal_there = jnp.where(odd == 1, gx < gx_count - 1, gx > 0)
    parts = []
    for b in range(blocks + 3):
        bias = jnp.zeros((1, queries), F32)
        for a in range(blocks):
            if b == a:
                continue
            col = (b if b < blocks else (blocks + 2, direct_col, diagonal_col)[b - blocks])
            ok = filt_ref[a, col] > 0
            if b == blocks + 2:
                ok = jnp.logical_and(ok, diagonal_there)
            bias = jnp.where(lane == a, jnp.where(ok, 0.0, -jnp.inf).astype(F32), bias)
        parts.append(s[b * BLOCK : (b + 1) * BLOCK] * mult + bias)
    parts.append(s[near:] * mult)
    scores = jnp.concatenate(parts, axis=0)
    top = jnp.max(scores, axis=0, keepdims=True)
    e = jnp.exp(scores - top)
    inv = 1.0 / jnp.sum(e, axis=0, keepdims=True)
    p = e * inv
    pb = p.astype(BF16)
    delta = jnp.sum(pb.astype(F32) * dp, axis=0, keepdims=True)
    ds = p * (dp - delta)
    temp_out[0] = jnp.sum(ds * s, axis=0, keepdims=True)
    dsb = (ds * mult).astype(BF16)
    nn = (((1,), (0,)), ((), ()))
    dv = lax.dot_general(pb, g, nn, preferred_element_type=F32)
    dk = lax.dot_general(dsb, q, nn, preferred_element_type=F32)
    dq = lax.dot_general(dsb, k, (((0,), (0,)), ((), ())), preferred_element_type=F32)
    dq_ref[...] = dq.astype(BF16)
    pair_ref[pl.ds(0, keys, stride=2), :] = dk
    pair_ref[pl.ds(1, keys, stride=2), :] = dv
    own_out[...] = pair_ref[: 2 * own_rows, :]
    for i, ref in enumerate((par_out, dir_out, dia_out)):
        at = 2 * (own_rows + i * BLOCK)
        ref[...] = pair_ref[at : at + 2 * BLOCK, :].astype(BF16)
    anc_out[...] = pair_ref[2 * near :, :]


def attention(pos, filt, warm, q, g, mesh_kv, partner, halo, anchors, head0, heads, dq_prev, anc_prev):
    rows, feat = q.shape
    own_rows = mesh_kv.shape[0]
    width = feat // warm.shape[0]
    a_rows = anchors.shape[0] // 2
    keys = own_rows + 3 * BLOCK + a_rows
    smem = pl.BlockSpec(memory_space=SMEM)
    full = lambda n: pl.BlockSpec((n, 2, width), lambda h: (0, 0, head0 + h))
    part = pl.BlockSpec((BLOCK, 2, width), lambda h: (0, 0, h))
    back = pl.BlockSpec((None, 2 * BLOCK, width), lambda h: (h, 0, 0))
    cols = pl.BlockSpec((rows, width), lambda h: (0, head0 + h))
    in_specs = [smem, smem, smem, cols, cols, full(own_rows), full(BLOCK), part, part]
    in_specs += [pl.BlockSpec((2 * a_rows, width), lambda h: (0, head0 + h))]
    args = [pos, filt, warm, q, g, mesh_kv, partner, *halo, anchors]
    alias = {}
    if dq_prev is not None:
        in_specs += [pl.BlockSpec(memory_space=pl.ANY)] * 2
        args += [dq_prev, anc_prev]
        alias = {10: 0, 11: 5}
    face = jax.ShapeDtypeStruct((heads, 2 * BLOCK, width), BF16)
    return pl.pallas_call(
        functools.partial(attention_kernel, gx_count=lax.axis_size("gx"), head0=head0, width=width),
        grid=(heads,),
        in_specs=in_specs,
        out_specs=[
            cols,
            pl.BlockSpec((None, 2 * own_rows, width), lambda h: (h, 0, 0)),
            back,
            back,
            back,
            pl.BlockSpec((2 * a_rows, width), lambda h: (0, head0 + h)),
            pl.BlockSpec((1, 1, rows), lambda h: (h, 0, 0)),
        ],
        out_shape=[
            jax.ShapeDtypeStruct(q.shape, BF16),
            jax.ShapeDtypeStruct((heads, 2 * own_rows, width), F32),
            face,
            face,
            face,
            jax.ShapeDtypeStruct((2 * a_rows, feat), F32),
            jax.ShapeDtypeStruct((heads, 1, rows), F32),
        ],
        scratch_shapes=[pltpu.VMEM((2 * keys, width), F32)],
        input_output_aliases=alias,
        compiler_params=pltpu.CompilerParams(vmem_limit_bytes=24 << 20),
        cost_estimate=pl.CostEstimate(
            flops=10 * heads * rows * keys * width,
            transcendentals=heads * rows * keys,
            bytes_accessed=heads * width * (rows * 6 + own_rows * 12 + 3 * BLOCK * 8 + a_rows * 12),
        ),
        name="attention",
    )(*args)


def combine_kernel(pos_ref, sent_ref, own_ref, dir_ref, dia_ref, par_ref, *rest):
    out_ref = rest[-1]
    odd = lax.rem(pos_ref[0], 2)
    blocks = out_ref.shape[0] // BLOCK
    spots = (
        jnp.where(odd == 1, sent_ref[0, 0], sent_ref[1, 0]),
        jnp.where(odd == 1, sent_ref[1, 0], sent_ref[0, 0]),
        sent_ref[2, 0],
    )
    width = own_ref.shape[2]
    for h in range(own_ref.shape[0]):
        lanes = slice(h * width, (h + 1) * width)
        back = [ref[h].astype(F32) for ref in (dir_ref, dia_ref, par_ref)]
        for a in range(blocks):
            total = own_ref[h, 2 * a * BLOCK : 2 * (a + 1) * BLOCK, :]
            for spot, face in zip(spots, back):
                total = total + jnp.where(spot == a, 1.0, 0.0).astype(F32) * face
            out_ref[a * BLOCK : (a + 1) * BLOCK, :, lanes] = total.astype(BF16).reshape(BLOCK, 2, width)


def combine(pos, sent, own, faces, head0, heads, feat, width, prev, part=None, weight=1):
    rows = own.shape[1] // 2
    lo, heads = part or (0, heads)
    step = next(n for n in COMBINE_STEPS if heads % n == 0 and head0 % n == 0 and lo % n == 0)
    smem = pl.BlockSpec(memory_space=SMEM)
    face = pl.BlockSpec((step, 2 * BLOCK, width), lambda h: (lo // step + h, 0, 0))
    own_spec = pl.BlockSpec((step, 2 * rows, width), lambda h: (lo // step + h, 0, 0))
    in_specs = [smem, smem, own_spec, face, face, face]
    args = [pos, sent, own, *faces]
    alias = {}
    if prev is not None:
        in_specs.append(pl.BlockSpec(memory_space=pl.ANY))
        args.append(prev)
        alias = {6: 0}
    return pl.pallas_call(
        combine_kernel,
        grid=(heads // step,),
        in_specs=in_specs,
        out_specs=pl.BlockSpec((rows, 2, step * width), lambda h: (0, 0, (head0 + lo) // step + h)),
        out_shape=jax.ShapeDtypeStruct((rows, 2, feat), BF16),
        input_output_aliases=alias,
        compiler_params=pltpu.CompilerParams(vmem_limit_bytes=24 << 20),
        cost_estimate=pl.CostEstimate(
            flops=weight * heads * width * rows * 16,
            transcendentals=0,
            bytes_accessed=heads * width * (rows * 12 + 3 * BLOCK * 4),
        ),
        name="combine",
    )(*args)


def finish_kernel(own_ref, temp_ref, *refs):
    got, (out_ref, sum_ref) = refs[:-2], refs[-2:]
    rows, feat = own_ref.shape
    total, temp = own_ref[...], temp_ref[...]
    for ref in got:
        total = total + ref[:, :feat]
        temp = temp + ref[:1, feat:]
    out_ref[...] = total.reshape(out_ref.shape)
    sum_ref[...] = temp


def finish(own, temp, got, shape):
    return pl.pallas_call(
        finish_kernel,
        out_shape=[jax.ShapeDtypeStruct(shape, F32), jax.ShapeDtypeStruct(temp.shape, F32)],
        compiler_params=pltpu.CompilerParams(vmem_limit_bytes=8 << 20),
        name="finish",
    )(own, temp, *got)


def local(q, mesh_kv, landmark, warm, g, exported, filt):
    rows, feat = q.shape
    total = warm.shape[0]
    width = feat // total
    gx_count = lax.axis_size("gx")
    stages = levels(lax.axis_size(("gx", "gy")))
    gx = lax.axis_index("gx")
    pos = jnp.full((1,), gx, jnp.int32)
    sent = exported[0]
    filt = filt[0]
    sizes = split_heads(total)
    chunks = [(sum(sizes[:i]), n) for i, n in enumerate(sizes)]

    picks = [pick(pos, sent, mesh_kv, width, [("direct", *chunks[0]), ("diagonal", *chunks[0])])]
    others = [(which, *chunk) for chunk in chunks[1:] for which in ("direct", "diagonal")]
    others = list(pick(pos, sent, mesh_kv, width, others + [("partner", 0, total)]))
    partner = swap_mask(others.pop(), 1)
    picks += [others[2 * i : 2 * i + 2] for i in range(len(chunks) - 1)]
    anchors = landmark.reshape(2 * landmark.shape[0], feat)
    for i, masks in enumerate(stages):
        if i == 1:
            anchors, picks[1] = lax.optimization_barrier((anchors, picks[1]))
        anchors = jnp.concatenate([anchors] + [swap_mask(anchors, m) for m in masks], axis=0)
    halos = [[swap_pairs(d, 0), swap_pairs(g, 1)] for d, g in picks]
    halos[0] = hold(halos[0], HOLD)

    dq = anc = None
    temps, owns, faces, returned = [], [], [], []
    for (head0, heads), halo in zip(chunks, halos):
        dq, own, f_dir, f_dia, f_par, anc, temp = attention(
            pos, filt, warm, q, g, mesh_kv, partner, halo, anchors, head0, heads, dq, anc
        )
        temps.append(temp)
        owns.append(own)
        faces.append((f_dir, f_dia, f_par))
        if len(faces) < len(chunks):
            returned.append(send_back(faces[-1]))
    temp = jnp.sum(jnp.concatenate(temps, axis=0), axis=(1, 2)) / math.sqrt(width)
    extra = jnp.zeros((1, LANES), F32).at[0, :total].set(temp)
    cell = None
    anc, faces[-1], returned[-1] = lax.optimization_barrier((anc, faces[-1], returned[-1]))
    returned.append(send_back(faces[-1]))
    for i, masks in enumerate(reversed(stages)):
        n = anc.shape[0] // (len(masks) + 1)
        wide = jnp.broadcast_to(extra, (n, LANES))
        got = [
            swap_mask(jnp.concatenate([anc[k * n : (k + 1) * n], wide], axis=1), m)
            for k, m in enumerate(masks, 1)
        ]
        if i == len(stages) - 2:
            cell = combine(pos, sent, owns[-2], returned[-2], *chunks[-2], feat, width, cell, weight=4000)
            got, cell = lax.optimization_barrier((got, cell))
        if i == len(stages) - 1:
            cell = combine(pos, sent, owns[-1], returned[-1], *chunks[-1], feat, width, cell, weight=0)
            got, cell = lax.optimization_barrier((got, cell))
            anchor_grad, temp = finish(anc[:n], extra, got, landmark.shape)
            break
        anc = sum([x[:, :feat] for x in got], anc[:n])
        extra = sum([x[:1, feat:] for x in got], extra)
    return (dq, cell, anchor_grad, temp[0, :total])


def solution(mesh):
    rows = ("groups", "gx", "gy")
    placed = (
        P(rows, None),
        P(rows, None, None),
        P(rows, None, None),
        P("groups"),
        P(rows, None),
        P(rows, None, None),
        P(rows, None, None),
    )
    return jax.shard_map(
        local,
        mesh=mesh,
        in_specs=placed,
        out_specs=(P(rows, None), P(rows, None, None), P(rows, None, None), P("groups")),
        check_vma=False,
    )
```

```python
import functools
import math

import jax
import jax.numpy as jnp
from jax import lax
from jax.experimental import pallas as pl
from jax.experimental.pallas import tpu as pltpu
from jax.sharding import PartitionSpec as P

BLOCK = 128
F32 = jnp.float32
BF16 = jnp.bfloat16
SMEM = pltpu.MemorySpace.SMEM
COMBINE_STEPS = (3, 2, 1)
LANES = 128
HOLD = 20_000_000_000


def swap_mask(x, mask):
    count = lax.axis_size(("gx", "gy"))
    return lax.ppermute(x, ("gx", "gy"), [(i, i ^ mask) for i in range(count)])


def levels(count):
    bits = count.bit_length() - 1
    out = [[2]] if bits > 1 else []
    at = 2
    while at < bits:
        take = min(2, bits - at)
        out.append([m << at for m in range(1, 1 << take)])
        at += take
    return out + [[1]]


def swap_pairs(x, first):
    count = lax.axis_size("gx")
    route = []
    for low in range(first, count - 1, 2):
        route += [(low, low + 1), (low + 1, low)]
    return lax.ppermute(x, "gx", route)


def split_heads(total):
    first = (total + 1) // 2
    return [n for n in (first, total - first) if n > 0]


def pick_kernel(pos_ref, sent_ref, kv_ref, *rest, copies, width):
    sems = rest[-1]
    outs = rest[:-1]
    odd = lax.rem(pos_ref[0], 2)
    spots = {
        "direct": jnp.where(odd == 1, sent_ref[0], sent_ref[1]),
        "diagonal": jnp.where(odd == 1, sent_ref[1], sent_ref[0]),
        "partner": sent_ref[2],
    }
    started = []
    for i, (out, (which, head0)) in enumerate(zip(outs, copies)):
        lanes = slice(head0 * width, head0 * width + out.shape[2])
        source = kv_ref.at[pl.ds(spots[which] * BLOCK, BLOCK), :, lanes]
        copy = pltpu.make_async_copy(source, out, sems.at[i])
        copy.start()
        started.append(copy)
    for copy in started:
        copy.wait()


def pick(pos, sent, mesh_kv, width, copies):
    smem = pl.BlockSpec(memory_space=SMEM)
    vmem = pl.BlockSpec(memory_space=pltpu.MemorySpace.VMEM)
    return pl.pallas_call(
        functools.partial(pick_kernel, copies=[c[:2] for c in copies], width=width),
        in_specs=[smem, smem, pl.BlockSpec(memory_space=pl.ANY)],
        out_specs=[vmem] * len(copies),
        out_shape=[jax.ShapeDtypeStruct((BLOCK, 2, heads * width), BF16) for _, _, heads in copies],
        scratch_shapes=[pltpu.SemaphoreType.DMA((len(copies),))],
        compiler_params=pltpu.CompilerParams(vmem_limit_bytes=60 << 20),
        cost_estimate=pl.CostEstimate(flops=0, transcendentals=0, bytes_accessed=1 << 20),
        name="pick",
    )(pos, sent, mesh_kv)


def hold_kernel(*refs):
    pass


def hold(arrays, flops):
    anywhere = pl.BlockSpec(memory_space=pl.ANY)
    return pl.pallas_call(
        hold_kernel,
        in_specs=[anywhere] * len(arrays),
        out_specs=[anywhere] * len(arrays),
        out_shape=[jax.ShapeDtypeStruct(x.shape, x.dtype) for x in arrays],
        input_output_aliases={i: i for i in range(len(arrays))},
        compiler_params=pltpu.CompilerParams(vmem_limit_bytes=1 << 20),
        cost_estimate=pl.CostEstimate(flops=flops, transcendentals=0, bytes_accessed=0),
        name="hold",
    )(*arrays)


def send_back(faces):
    direct, diagonal, partner = faces
    return [swap_pairs(direct, 0), swap_pairs(diagonal, 1), swap_mask(partner, 1)]


def attention_kernel(
    pos_ref, filt_ref, warm_ref, q_ref, g_ref, own_ref, par_ref, dir_ref, dia_ref, anc_ref, *rest,
    gx_count, head0, width,
):
    (dq_ref, own_out, dir_out, dia_out, par_out, anc_out, temp_out, pair_ref) = rest[-8:]
    head = pl.program_id(0)
    gx = pos_ref[0]
    odd = lax.rem(gx, 2)
    queries = q_ref.shape[0]
    own_rows = own_ref.shape[0]
    blocks = own_rows // BLOCK
    near = own_rows + 3 * BLOCK
    keys = near + anc_ref.shape[0]

    row = 0
    for ref in (own_ref, par_ref, dir_ref, dia_ref, anc_ref):
        block = ref[...] if len(ref.shape) == 2 else ref[...].reshape(2 * ref.shape[0], width)
        pair_ref[row : row + block.shape[0], :] = block.astype(F32)
        row += block.shape[0]
    k = pair_ref[pl.ds(0, keys, stride=2), :].astype(BF16)
    v = pair_ref[pl.ds(1, keys, stride=2), :].astype(BF16)

    q = q_ref[...]
    g = g_ref[...]
    nt = (((1,), (1,)), ((), ()))
    s = lax.dot_general(k, q, nt, preferred_element_type=F32)
    dp = lax.dot_general(v, g, nt, preferred_element_type=F32)

    mult = warm_ref[head0 + head] / math.sqrt(width)
    lane = lax.broadcasted_iota(jnp.int32, (1, queries), 1) // BLOCK
    direct_col = blocks + 1 - odd
    diagonal_col = blocks + odd
    diagonal_there = jnp.where(odd == 1, gx < gx_count - 1, gx > 0)
    parts = []
    for b in range(blocks + 3):
        bias = jnp.zeros((1, queries), F32)
        for a in range(blocks):
            if b == a:
                continue
            col = (b if b < blocks else (blocks + 2, direct_col, diagonal_col)[b - blocks])
            ok = filt_ref[a, col] > 0
            if b == blocks + 2:
                ok = jnp.logical_and(ok, diagonal_there)
            bias = jnp.where(lane == a, jnp.where(ok, 0.0, -jnp.inf).astype(F32), bias)
        parts.append(s[b * BLOCK : (b + 1) * BLOCK] * mult + bias)
    parts.append(s[near:] * mult)
    scores = jnp.concatenate(parts, axis=0)
    top = jnp.max(scores, axis=0, keepdims=True)
    e = jnp.exp(scores - top)
    inv = 1.0 / jnp.sum(e, axis=0, keepdims=True)
    p = e * inv
    pb = p.astype(BF16)
    delta = jnp.sum(pb.astype(F32) * dp, axis=0, keepdims=True)
    ds = p * (dp - delta)
    temp_out[0] = jnp.sum(ds * s, axis=0, keepdims=True)
    dsb = (ds * mult).astype(BF16)
    nn = (((1,), (0,)), ((), ()))
    dv = lax.dot_general(pb, g, nn, preferred_element_type=F32)
    dk = lax.dot_general(dsb, q, nn, preferred_element_type=F32)
    dq = lax.dot_general(dsb, k, (((0,), (0,)), ((), ())), preferred_element_type=F32)
    dq_ref[...] = dq.astype(BF16)
    pair_ref[pl.ds(0, keys, stride=2), :] = dk
    pair_ref[pl.ds(1, keys, stride=2), :] = dv
    own_out[...] = pair_ref[: 2 * own_rows, :]
    for i, ref in enumerate((par_out, dir_out, dia_out)):
        at = 2 * (own_rows + i * BLOCK)
        ref[...] = pair_ref[at : at + 2 * BLOCK, :].astype(BF16)
    anc_out[...] = pair_ref[2 * near :, :]


def attention(pos, filt, warm, q, g, mesh_kv, partner, halo, anchors, head0, heads, dq_prev, anc_prev):
    rows, feat = q.shape
    own_rows = mesh_kv.shape[0]
    width = feat // warm.shape[0]
    a_rows = anchors.shape[0]
    keys = own_rows + 3 * BLOCK + a_rows
    smem = pl.BlockSpec(memory_space=SMEM)
    full = lambda n: pl.BlockSpec((n, 2, width), lambda h: (0, 0, head0 + h))
    part = pl.BlockSpec((BLOCK, 2, width), lambda h: (0, 0, h))
    back = pl.BlockSpec((None, 2 * BLOCK, width), lambda h: (h, 0, 0))
    cols = pl.BlockSpec((rows, width), lambda h: (0, head0 + h))
    in_specs = [smem, smem, smem, cols, cols, full(own_rows), full(BLOCK), part, part]
    in_specs += [full(a_rows)]
    args = [pos, filt, warm, q, g, mesh_kv, partner, *halo, anchors]
    alias = {}
    if dq_prev is not None:
        in_specs += [pl.BlockSpec(memory_space=pl.ANY)] * 2
        args += [dq_prev, anc_prev]
        alias = {10: 0, 11: 5}
    face = jax.ShapeDtypeStruct((heads, 2 * BLOCK, width), BF16)
    return pl.pallas_call(
        functools.partial(attention_kernel, gx_count=lax.axis_size("gx"), head0=head0, width=width),
        grid=(heads,),
        in_specs=in_specs,
        out_specs=[
            cols,
            pl.BlockSpec((None, 2 * own_rows, width), lambda h: (h, 0, 0)),
            back,
            back,
            back,
            pl.BlockSpec((2 * a_rows, width), lambda h: (0, head0 + h)),
            pl.BlockSpec((1, 1, rows), lambda h: (h, 0, 0)),
        ],
        out_shape=[
            jax.ShapeDtypeStruct(q.shape, BF16),
            jax.ShapeDtypeStruct((heads, 2 * own_rows, width), F32),
            face,
            face,
            face,
            jax.ShapeDtypeStruct((2 * a_rows, feat), F32),
            jax.ShapeDtypeStruct((heads, 1, rows), F32),
        ],
        scratch_shapes=[pltpu.VMEM((2 * keys, width), F32)],
        input_output_aliases=alias,
        compiler_params=pltpu.CompilerParams(vmem_limit_bytes=24 << 20),
        cost_estimate=pl.CostEstimate(
            flops=10 * heads * rows * keys * width,
            transcendentals=heads * rows * keys,
            bytes_accessed=heads * width * (rows * 6 + own_rows * 12 + 3 * BLOCK * 8 + a_rows * 12),
        ),
        name="attention",
    )(*args)


def combine_kernel(pos_ref, sent_ref, own_ref, dir_ref, dia_ref, par_ref, *rest):
    out_ref = rest[-1]
    odd = lax.rem(pos_ref[0], 2)
    blocks = out_ref.shape[0] // BLOCK
    spots = (
        jnp.where(odd == 1, sent_ref[0], sent_ref[1]),
        jnp.where(odd == 1, sent_ref[1], sent_ref[0]),
        sent_ref[2],
    )
    width = own_ref.shape[2]
    for h in range(own_ref.shape[0]):
        lanes = slice(h * width, (h + 1) * width)
        back = [ref[h].astype(F32) for ref in (dir_ref, dia_ref, par_ref)]
        for a in range(blocks):
            total = own_ref[h, 2 * a * BLOCK : 2 * (a + 1) * BLOCK, :]
            for spot, face in zip(spots, back):
                total = total + jnp.where(spot == a, 1.0, 0.0).astype(F32) * face
            out_ref[a * BLOCK : (a + 1) * BLOCK, :, lanes] = total.astype(BF16).reshape(BLOCK, 2, width)


def combine(pos, sent, own, faces, head0, heads, feat, width, prev, part=None, weight=1):
    rows = own.shape[1] // 2
    lo, heads = part or (0, heads)
    step = next(n for n in COMBINE_STEPS if heads % n == 0 and head0 % n == 0 and lo % n == 0)
    smem = pl.BlockSpec(memory_space=SMEM)
    face = pl.BlockSpec((step, 2 * BLOCK, width), lambda h: (lo // step + h, 0, 0))
    own_spec = pl.BlockSpec((step, 2 * rows, width), lambda h: (lo // step + h, 0, 0))
    in_specs = [smem, smem, own_spec, face, face, face]
    args = [pos, sent, own, *faces]
    alias = {}
    if prev is not None:
        in_specs.append(pl.BlockSpec(memory_space=pl.ANY))
        args.append(prev)
        alias = {6: 0}
    return pl.pallas_call(
        combine_kernel,
        grid=(heads // step,),
        in_specs=in_specs,
        out_specs=pl.BlockSpec((rows, 2, step * width), lambda h: (0, 0, (head0 + lo) // step + h)),
        out_shape=jax.ShapeDtypeStruct((rows, 2, feat), BF16),
        input_output_aliases=alias,
        compiler_params=pltpu.CompilerParams(vmem_limit_bytes=24 << 20),
        cost_estimate=pl.CostEstimate(
            flops=weight * heads * width * rows * 16,
            transcendentals=0,
            bytes_accessed=heads * width * (rows * 12 + 3 * BLOCK * 4),
        ),
        name="combine",
    )(*args)


def finish_kernel(own_ref, temp_ref, *refs):
    got, (out_ref, sum_ref) = refs[:-2], refs[-2:]
    rows, feat = own_ref.shape
    total, temp = own_ref[...], temp_ref[...]
    for ref in got:
        total = total + ref[:, :feat]
        temp = temp + ref[:1, feat:]
    out_ref[...] = total.reshape(out_ref.shape)
    sum_ref[...] = temp


def finish(own, temp, got, shape):
    return pl.pallas_call(
        finish_kernel,
        out_shape=[jax.ShapeDtypeStruct(shape, F32), jax.ShapeDtypeStruct(temp.shape, F32)],
        compiler_params=pltpu.CompilerParams(vmem_limit_bytes=8 << 20),
        name="finish",
    )(own, temp, *got)


def local(q, mesh_kv, landmark, warm, g, exported, filt):
    rows, feat = q.shape
    total = warm.shape[0]
    width = feat // total
    gx_count = lax.axis_size("gx")
    stages = levels(lax.axis_size(("gx", "gy")))
    gx = lax.axis_index("gx")
    pos = jnp.full((1,), gx, jnp.int32)
    sent = exported.reshape(-1)
    filt = filt[0]
    sizes = split_heads(total)
    chunks = [(sum(sizes[:i]), n) for i, n in enumerate(sizes)]

    picks = [pick(pos, sent, mesh_kv, width, [("direct", *chunks[0]), ("diagonal", *chunks[0])])]
    others = [(which, *chunk) for chunk in chunks[1:] for which in ("direct", "diagonal")]
    others = list(pick(pos, sent, mesh_kv, width, others + [("partner", 0, total)]))
    partner = swap_mask(others.pop(), 1)
    picks += [others[2 * i : 2 * i + 2] for i in range(len(chunks) - 1)]
    anchors = landmark
    for i, masks in enumerate(stages):
        if i == 1:
            anchors, picks[1] = lax.optimization_barrier((anchors, picks[1]))
        anchors = jnp.concatenate([anchors] + [swap_mask(anchors, m) for m in masks], axis=0)
    halos = [[swap_pairs(d, 0), swap_pairs(g, 1)] for d, g in picks]
    halos[0] = hold(halos[0], HOLD)

    dq = anc = None
    temps, owns, faces, returned = [], [], [], []
    for (head0, heads), halo in zip(chunks, halos):
        dq, own, f_dir, f_dia, f_par, anc, temp = attention(
            pos, filt, warm, q, g, mesh_kv, partner, halo, anchors, head0, heads, dq, anc
        )
        temps.append(temp)
        owns.append(own)
        faces.append((f_dir, f_dia, f_par))
        if len(faces) < len(chunks):
            returned.append(send_back(faces[-1]))
    temp = jnp.sum(jnp.concatenate(temps, axis=0), axis=(1, 2)) / math.sqrt(width)
    extra = jnp.zeros((1, LANES), F32).at[0, :total].set(temp)
    cell = None
    anc, faces[-1], returned[-1] = lax.optimization_barrier((anc, faces[-1], returned[-1]))
    returned.append(send_back(faces[-1]))
    for i, masks in enumerate(reversed(stages)):
        n = anc.shape[0] // (len(masks) + 1)
        wide = jnp.broadcast_to(extra, (n, LANES))
        got = [
            swap_mask(jnp.concatenate([anc[k * n : (k + 1) * n], wide], axis=1), m)
            for k, m in enumerate(masks, 1)
        ]
        if i == len(stages) - 2:
            cell = combine(pos, sent, owns[-2], returned[-2], *chunks[-2], feat, width, cell, weight=4000)
            got, cell = lax.optimization_barrier((got, cell))
        if i == len(stages) - 1:
            cell = combine(pos, sent, owns[-1], returned[-1], *chunks[-1], feat, width, cell, weight=0)
            got, cell = lax.optimization_barrier((got, cell))
            anchor_grad, temp = finish(anc[:n], extra, got, landmark.shape)
            break
        anc = sum([x[:, :feat] for x in got], anc[:n])
        extra = sum([x[:1, feat:] for x in got], extra)
    return (dq, cell, anchor_grad, temp[0, :total])


def solution(mesh):
    rows = ("groups", "gx", "gy")
    placed = (
        P(rows, None),
        P(rows, None, None),
        P(rows, None, None),
        P("groups"),
        P(rows, None),
        P(rows, None, None),
        P(rows, None, None),
    )
    return jax.shard_map(
        local,
        mesh=mesh,
        in_specs=placed,
        out_specs=(P(rows, None), P(rows, None, None), P(rows, None, None), P("groups")),
        check_vma=False,
    )
```

```python
import functools
import math

import jax
import jax.numpy as jnp
from jax import lax
from jax.experimental import pallas as pl
from jax.experimental.pallas import tpu as pltpu
from jax.sharding import PartitionSpec as P

BLOCK = 128
F32 = jnp.float32
BF16 = jnp.bfloat16
SMEM = pltpu.MemorySpace.SMEM
COMBINE_STEPS = (3, 2, 1)
LANES = 128
HOLD = 20_000_000_000


def swap_mask(x, mask):
    count = lax.axis_size(("gx", "gy"))
    return lax.ppermute(x, ("gx", "gy"), [(i, i ^ mask) for i in range(count)])


def levels(count):
    bits = count.bit_length() - 1
    out = [[2]] if bits > 1 else []
    at = 2
    while at < bits:
        take = min(2, bits - at)
        out.append([m << at for m in range(1, 1 << take)])
        at += take
    return out + [[1]]


def swap_pairs(x, first):
    count = lax.axis_size("gx")
    route = []
    for low in range(first, count - 1, 2):
        route += [(low, low + 1), (low + 1, low)]
    return lax.ppermute(x, "gx", route)


def split_heads(total):
    first = (total + 1) // 2
    return [n for n in (first, total - first) if n > 0]


def pick_kernel(pos_ref, sent_ref, kv_ref, *rest, copies, width):
    sems = rest[-1]
    outs = rest[:-1]
    odd = lax.rem(pos_ref[0], 2)
    spots = {
        "direct": jnp.where(odd == 1, sent_ref[0], sent_ref[1]),
        "diagonal": jnp.where(odd == 1, sent_ref[1], sent_ref[0]),
        "partner": sent_ref[2],
    }
    started = []
    for i, (out, (which, head0)) in enumerate(zip(outs, copies)):
        lanes = slice(head0 * width, head0 * width + out.shape[2])
        source = kv_ref.at[pl.ds(spots[which] * BLOCK, BLOCK), :, lanes]
        copy = pltpu.make_async_copy(source, out, sems.at[i])
        copy.start()
        started.append(copy)
    for copy in started:
        copy.wait()


def pick(pos, sent, mesh_kv, width, copies):
    smem = pl.BlockSpec(memory_space=SMEM)
    vmem = pl.BlockSpec(memory_space=pltpu.MemorySpace.VMEM)
    return pl.pallas_call(
        functools.partial(pick_kernel, copies=[c[:2] for c in copies], width=width),
        in_specs=[smem, smem, pl.BlockSpec(memory_space=pl.ANY)],
        out_specs=[vmem] * len(copies),
        out_shape=[jax.ShapeDtypeStruct((BLOCK, 2, heads * width), BF16) for _, _, heads in copies],
        scratch_shapes=[pltpu.SemaphoreType.DMA((len(copies),))],
        compiler_params=pltpu.CompilerParams(vmem_limit_bytes=8 << 20),
        cost_estimate=pl.CostEstimate(flops=0, transcendentals=0, bytes_accessed=1 << 20),
        name="pick",
    )(pos, sent, mesh_kv)


def hold_kernel(*refs):
    pass


def hold(arrays, flops):
    anywhere = pl.BlockSpec(memory_space=pl.ANY)
    return pl.pallas_call(
        hold_kernel,
        in_specs=[anywhere] * len(arrays),
        out_specs=[anywhere] * len(arrays),
        out_shape=[jax.ShapeDtypeStruct(x.shape, x.dtype) for x in arrays],
        input_output_aliases={i: i for i in range(len(arrays))},
        compiler_params=pltpu.CompilerParams(vmem_limit_bytes=1 << 20),
        cost_estimate=pl.CostEstimate(flops=flops, transcendentals=0, bytes_accessed=0),
        name="hold",
    )(*arrays)


def send_back(faces):
    direct, diagonal, partner = faces
    return [swap_pairs(direct, 0), swap_pairs(diagonal, 1), swap_mask(partner, 1)]


def attention_kernel(
    pos_ref, filt_ref, warm_ref, q_ref, g_ref, own_ref, par_ref, dir_ref, dia_ref, anc_ref, *rest,
    gx_count, head0, width,
):
    (dq_ref, own_out, dir_out, dia_out, par_out, anc_out, temp_out, pair_ref) = rest[-8:]
    head = pl.program_id(0)
    gx = pos_ref[0]
    odd = lax.rem(gx, 2)
    queries = q_ref.shape[0]
    own_rows = own_ref.shape[0]
    blocks = own_rows // BLOCK
    near = own_rows + 3 * BLOCK
    keys = near + anc_ref.shape[0]

    row = 0
    for ref in (own_ref, par_ref, dir_ref, dia_ref, anc_ref):
        block = ref[...] if len(ref.shape) == 2 else ref[...].reshape(2 * ref.shape[0], width)
        pair_ref[row : row + block.shape[0], :] = block.astype(F32)
        row += block.shape[0]
    k = pair_ref[pl.ds(0, keys, stride=2), :].astype(BF16)
    v = pair_ref[pl.ds(1, keys, stride=2), :].astype(BF16)

    q = q_ref[...]
    g = g_ref[...]
    nt = (((1,), (1,)), ((), ()))
    s = lax.dot_general(k, q, nt, preferred_element_type=F32)
    dp = lax.dot_general(v, g, nt, preferred_element_type=F32)

    mult = warm_ref[head0 + head] / math.sqrt(width)
    lane = lax.broadcasted_iota(jnp.int32, (1, queries), 1) // BLOCK
    direct_col = blocks + 1 - odd
    diagonal_col = blocks + odd
    diagonal_there = jnp.where(odd == 1, gx < gx_count - 1, gx > 0)
    parts = []
    for b in range(blocks + 3):
        bias = jnp.zeros((1, queries), F32)
        for a in range(blocks):
            if b == a:
                continue
            col = (b if b < blocks else (blocks + 2, direct_col, diagonal_col)[b - blocks])
            ok = filt_ref[a, col] > 0
            if b == blocks + 2:
                ok = jnp.logical_and(ok, diagonal_there)
            bias = jnp.where(lane == a, jnp.where(ok, 0.0, -jnp.inf).astype(F32), bias)
        parts.append(s[b * BLOCK : (b + 1) * BLOCK] * mult + bias)
    parts.append(s[near:] * mult)
    scores = jnp.concatenate(parts, axis=0)
    top = jnp.max(scores, axis=0, keepdims=True)
    e = jnp.exp(scores - top)
    inv = 1.0 / jnp.sum(e, axis=0, keepdims=True)
    p = e * inv
    pb = p.astype(BF16)
    delta = jnp.sum(pb.astype(F32) * dp, axis=0, keepdims=True)
    ds = p * (dp - delta)
    temp_out[0] = jnp.sum(ds * s, axis=0, keepdims=True)
    dsb = (ds * mult).astype(BF16)
    nn = (((1,), (0,)), ((), ()))
    dv = lax.dot_general(pb, g, nn, preferred_element_type=F32)
    dk = lax.dot_general(dsb, q, nn, preferred_element_type=F32)
    dq = lax.dot_general(dsb, k, (((0,), (0,)), ((), ())), preferred_element_type=F32)
    dq_ref[...] = dq.astype(BF16)
    pair_ref[pl.ds(0, keys, stride=2), :] = dk
    pair_ref[pl.ds(1, keys, stride=2), :] = dv
    own_out[...] = pair_ref[: 2 * own_rows, :]
    for i, ref in enumerate((par_out, dir_out, dia_out)):
        at = 2 * (own_rows + i * BLOCK)
        ref[...] = pair_ref[at : at + 2 * BLOCK, :].astype(BF16)
    anc_out[...] = pair_ref[2 * near :, :]


def attention(pos, filt, warm, q, g, mesh_kv, partner, halo, anchors, head0, heads, dq_prev, anc_prev):
    rows, feat = q.shape
    own_rows = mesh_kv.shape[0]
    width = feat // warm.shape[0]
    a_rows = anchors.shape[0]
    keys = own_rows + 3 * BLOCK + a_rows
    smem = pl.BlockSpec(memory_space=SMEM)
    full = lambda n: pl.BlockSpec((n, 2, width), lambda h: (0, 0, head0 + h))
    part = pl.BlockSpec((BLOCK, 2, width), lambda h: (0, 0, h))
    back = pl.BlockSpec((None, 2 * BLOCK, width), lambda h: (h, 0, 0))
    cols = pl.BlockSpec((rows, width), lambda h: (0, head0 + h))
    in_specs = [smem, smem, smem, cols, cols, full(own_rows), full(BLOCK), part, part]
    in_specs += [full(a_rows)]
    args = [pos, filt, warm, q, g, mesh_kv, partner, *halo, anchors]
    alias = {}
    if dq_prev is not None:
        in_specs += [pl.BlockSpec(memory_space=pl.ANY)] * 2
        args += [dq_prev, anc_prev]
        alias = {10: 0, 11: 5}
    face = jax.ShapeDtypeStruct((heads, 2 * BLOCK, width), BF16)
    return pl.pallas_call(
        functools.partial(attention_kernel, gx_count=lax.axis_size("gx"), head0=head0, width=width),
        grid=(heads,),
        in_specs=in_specs,
        out_specs=[
            cols,
            pl.BlockSpec((None, 2 * own_rows, width), lambda h: (h, 0, 0)),
            back,
            back,
            back,
            pl.BlockSpec((2 * a_rows, width), lambda h: (0, head0 + h)),
            pl.BlockSpec((1, 1, rows), lambda h: (h, 0, 0)),
        ],
        out_shape=[
            jax.ShapeDtypeStruct(q.shape, BF16),
            jax.ShapeDtypeStruct((heads, 2 * own_rows, width), F32),
            face,
            face,
            face,
            jax.ShapeDtypeStruct((2 * a_rows, feat), F32),
            jax.ShapeDtypeStruct((heads, 1, rows), F32),
        ],
        scratch_shapes=[pltpu.VMEM((2 * keys, width), F32)],
        input_output_aliases=alias,
        compiler_params=pltpu.CompilerParams(vmem_limit_bytes=24 << 20),
        cost_estimate=pl.CostEstimate(
            flops=10 * heads * rows * keys * width,
            transcendentals=heads * rows * keys,
            bytes_accessed=heads * width * (rows * 6 + own_rows * 12 + 3 * BLOCK * 8 + a_rows * 12),
        ),
        name="attention",
    )(*args)


def combine_kernel(pos_ref, sent_ref, own_ref, dir_ref, dia_ref, par_ref, *rest):
    out_ref = rest[-1]
    odd = lax.rem(pos_ref[0], 2)
    blocks = out_ref.shape[0] // BLOCK
    spots = (
        jnp.where(odd == 1, sent_ref[0], sent_ref[1]),
        jnp.where(odd == 1, sent_ref[1], sent_ref[0]),
        sent_ref[2],
    )
    width = own_ref.shape[2]
    for h in range(own_ref.shape[0]):
        lanes = slice(h * width, (h + 1) * width)
        back = [ref[h].astype(F32) for ref in (dir_ref, dia_ref, par_ref)]
        for a in range(blocks):
            total = own_ref[h, 2 * a * BLOCK : 2 * (a + 1) * BLOCK, :]
            for spot, face in zip(spots, back):
                total = total + jnp.where(spot == a, 1.0, 0.0).astype(F32) * face
            out_ref[a * BLOCK : (a + 1) * BLOCK, :, lanes] = total.astype(BF16).reshape(BLOCK, 2, width)


def combine(pos, sent, own, faces, head0, heads, feat, width, prev, part=None, weight=1):
    rows = own.shape[1] // 2
    lo, heads = part or (0, heads)
    step = next(n for n in COMBINE_STEPS if heads % n == 0 and head0 % n == 0 and lo % n == 0)
    smem = pl.BlockSpec(memory_space=SMEM)
    face = pl.BlockSpec((step, 2 * BLOCK, width), lambda h: (lo // step + h, 0, 0))
    own_spec = pl.BlockSpec((step, 2 * rows, width), lambda h: (lo // step + h, 0, 0))
    in_specs = [smem, smem, own_spec, face, face, face]
    args = [pos, sent, own, *faces]
    alias = {}
    if prev is not None:
        in_specs.append(pl.BlockSpec(memory_space=pl.ANY))
        args.append(prev)
        alias = {6: 0}
    return pl.pallas_call(
        combine_kernel,
        grid=(heads // step,),
        in_specs=in_specs,
        out_specs=pl.BlockSpec((rows, 2, step * width), lambda h: (0, 0, (head0 + lo) // step + h)),
        out_shape=jax.ShapeDtypeStruct((rows, 2, feat), BF16),
        input_output_aliases=alias,
        compiler_params=pltpu.CompilerParams(vmem_limit_bytes=24 << 20),
        cost_estimate=pl.CostEstimate(
            flops=weight * heads * width * rows * 16,
            transcendentals=0,
            bytes_accessed=heads * width * (rows * 12 + 3 * BLOCK * 4),
        ),
        name="combine",
    )(*args)


def finish_kernel(own_ref, temp_ref, *refs):
    got, (out_ref, sum_ref) = refs[:-2], refs[-2:]
    rows, feat = own_ref.shape
    total, temp = own_ref[...], temp_ref[...]
    for ref in got:
        total = total + ref[:, :feat]
        temp = temp + ref[:1, feat:]
    out_ref[...] = total.reshape(out_ref.shape)
    sum_ref[...] = temp


def finish(own, temp, got, shape):
    return pl.pallas_call(
        finish_kernel,
        out_shape=[jax.ShapeDtypeStruct(shape, F32), jax.ShapeDtypeStruct(temp.shape, F32)],
        compiler_params=pltpu.CompilerParams(vmem_limit_bytes=8 << 20),
        name="finish",
    )(own, temp, *got)


def local(q, mesh_kv, landmark, warm, g, exported, filt):
    rows, feat = q.shape
    total = warm.shape[0]
    width = feat // total
    gx_count = lax.axis_size("gx")
    stages = levels(lax.axis_size(("gx", "gy")))
    gx = lax.axis_index("gx")
    pos = jnp.full((1,), gx, jnp.int32)
    sent = exported.reshape(-1)
    filt = filt[0]
    sizes = split_heads(total)
    chunks = [(sum(sizes[:i]), n) for i, n in enumerate(sizes)]

    picks = [pick(pos, sent, mesh_kv, width, [("direct", *chunks[0]), ("diagonal", *chunks[0])])]
    others = [(which, *chunk) for chunk in chunks[1:] for which in ("direct", "diagonal")]
    others = list(pick(pos, sent, mesh_kv, width, others + [("partner", 0, total)]))
    partner = swap_mask(others.pop(), 1)
    picks += [others[2 * i : 2 * i + 2] for i in range(len(chunks) - 1)]
    anchors = landmark
    for i, masks in enumerate(stages):
        if i == 1:
            anchors, picks[1] = lax.optimization_barrier((anchors, picks[1]))
        anchors = jnp.concatenate([anchors] + [swap_mask(anchors, m) for m in masks], axis=0)
    halos = [[swap_pairs(d, 0), swap_pairs(g, 1)] for d, g in picks]
    halos[0] = hold(halos[0], HOLD)

    dq = anc = None
    temps, owns, faces, returned = [], [], [], []
    for (head0, heads), halo in zip(chunks, halos):
        dq, own, f_dir, f_dia, f_par, anc, temp = attention(
            pos, filt, warm, q, g, mesh_kv, partner, halo, anchors, head0, heads, dq, anc
        )
        temps.append(temp)
        owns.append(own)
        faces.append((f_dir, f_dia, f_par))
        if len(faces) < len(chunks):
            returned.append(send_back(faces[-1]))
    temp = jnp.sum(jnp.concatenate(temps, axis=0), axis=(1, 2)) / math.sqrt(width)
    extra = jnp.zeros((1, LANES), F32).at[0, :total].set(temp)
    cell = None
    anc, faces[-1], returned[-1] = lax.optimization_barrier((anc, faces[-1], returned[-1]))
    direct, diagonal, partner = faces[-1]
    returned.append([swap_pairs(direct, 0), None, swap_mask(partner, 1)])
    for i, masks in enumerate(reversed(stages)):
        n = anc.shape[0] // (len(masks) + 1)
        wide = jnp.broadcast_to(extra, (n, LANES))
        out = [
            jnp.concatenate([anc[k * n : (k + 1) * n], wide], axis=1) for k in range(1, len(masks) + 1)
        ]
        if i == 1:
            out, diagonal, returned[-1][2] = lax.optimization_barrier((out, diagonal, returned[-1][2]))
            returned[-1][1] = swap_pairs(diagonal, 1)
        got = [swap_mask(x, m) for x, m in zip(out, masks)]
        if i == len(stages) - 2:
            cell = combine(pos, sent, owns[-2], returned[-2], *chunks[-2], feat, width, cell, weight=4000)
            got, cell = lax.optimization_barrier((got, cell))
        if i == len(stages) - 1:
            cell = combine(pos, sent, owns[-1], returned[-1], *chunks[-1], feat, width, cell, weight=0)
            got, cell = lax.optimization_barrier((got, cell))
            anchor_grad, temp = finish(anc[:n], extra, got, landmark.shape)
            break
        anc = sum([x[:, :feat] for x in got], anc[:n])
        extra = sum([x[:1, feat:] for x in got], extra)
    return (dq, cell, anchor_grad, temp[0, :total])


def solution(mesh):
    rows = ("groups", "gx", "gy")
    placed = (
        P(rows, None),
        P(rows, None, None),
        P(rows, None, None),
        P("groups"),
        P(rows, None),
        P(rows, None, None),
        P(rows, None, None),
    )
    return jax.shard_map(
        local,
        mesh=mesh,
        in_specs=placed,
        out_specs=(P(rows, None), P(rows, None, None), P(rows, None, None), P("groups")),
        check_vma=False,
    )
```

```python
import functools
import math

import jax
import jax.numpy as jnp
from jax import lax
from jax.experimental import pallas as pl
from jax.experimental.pallas import tpu as pltpu
from jax.sharding import PartitionSpec as P

BLOCK = 128
F32 = jnp.float32
BF16 = jnp.bfloat16
SMEM = pltpu.MemorySpace.SMEM
COMBINE_STEPS = (3, 2, 1)
LANES = 128
HOLD = 20_000_000_000


def swap_mask(x, mask):
    count = lax.axis_size(("gx", "gy"))
    return lax.ppermute(x, ("gx", "gy"), [(i, i ^ mask) for i in range(count)])


def levels(count):
    bits = count.bit_length() - 1
    out = [[2]] if bits > 1 else []
    at = 2
    while at < bits:
        take = min(2, bits - at)
        out.append([m << at for m in range(1, 1 << take)])
        at += take
    return out + [[1]]


def swap_pairs(x, first):
    count = lax.axis_size("gx")
    route = []
    for low in range(first, count - 1, 2):
        route += [(low, low + 1), (low + 1, low)]
    return lax.ppermute(x, "gx", route)


def split_heads(total):
    first = (total + 1) // 2
    return [n for n in (first, total - first) if n > 0]


def pick_kernel(pos_ref, sent_ref, kv_ref, *rest, copies, width):
    sems = rest[-1]
    outs = rest[:-1]
    odd = lax.rem(pos_ref[0], 2)
    spots = {
        "direct": jnp.where(odd == 1, sent_ref[0], sent_ref[1]),
        "diagonal": jnp.where(odd == 1, sent_ref[1], sent_ref[0]),
        "partner": sent_ref[2],
    }
    started = []
    for i, (out, (which, head0)) in enumerate(zip(outs, copies)):
        lanes = slice(head0 * width, head0 * width + out.shape[2])
        source = kv_ref.at[pl.ds(spots[which] * BLOCK, BLOCK), :, lanes]
        copy = pltpu.make_async_copy(source, out, sems.at[i])
        copy.start()
        started.append(copy)
    for copy in started:
        copy.wait()


def pick(pos, sent, mesh_kv, width, copies):
    smem = pl.BlockSpec(memory_space=SMEM)
    vmem = pl.BlockSpec(memory_space=pltpu.MemorySpace.VMEM)
    return pl.pallas_call(
        functools.partial(pick_kernel, copies=[c[:2] for c in copies], width=width),
        in_specs=[smem, smem, pl.BlockSpec(memory_space=pl.ANY)],
        out_specs=[vmem] * len(copies),
        out_shape=[jax.ShapeDtypeStruct((BLOCK, 2, heads * width), BF16) for _, _, heads in copies],
        scratch_shapes=[pltpu.SemaphoreType.DMA((len(copies),))],
        compiler_params=pltpu.CompilerParams(vmem_limit_bytes=8 << 20),
        cost_estimate=pl.CostEstimate(flops=0, transcendentals=0, bytes_accessed=1 << 20),
        name="pick",
    )(pos, sent, mesh_kv)


def hold_kernel(*refs):
    pass


def hold(arrays, flops):
    anywhere = pl.BlockSpec(memory_space=pl.ANY)
    return pl.pallas_call(
        hold_kernel,
        in_specs=[anywhere] * len(arrays),
        out_specs=[anywhere] * len(arrays),
        out_shape=[jax.ShapeDtypeStruct(x.shape, x.dtype) for x in arrays],
        input_output_aliases={i: i for i in range(len(arrays))},
        compiler_params=pltpu.CompilerParams(vmem_limit_bytes=1 << 20),
        cost_estimate=pl.CostEstimate(flops=flops, transcendentals=0, bytes_accessed=0),
        name="hold",
    )(*arrays)


def send_back(faces):
    direct, diagonal, partner = faces
    return [swap_pairs(direct, 0), swap_pairs(diagonal, 1), swap_mask(partner, 1)]


def attention_kernel(
    pos_ref, filt_ref, warm_ref, q_ref, g_ref, own_ref, par_ref, dir_ref, dia_ref, anc_ref, *rest,
    gx_count, head0, width,
):
    (dq_ref, own_out, dir_out, dia_out, par_out, anc_out, temp_out, pair_ref) = rest[-8:]
    head = pl.program_id(0)
    gx = pos_ref[0]
    odd = lax.rem(gx, 2)
    queries = q_ref.shape[0]
    own_rows = own_ref.shape[0]
    blocks = own_rows // BLOCK
    near = own_rows + 3 * BLOCK
    keys = near + anc_ref.shape[0]

    row = 0
    for ref in (own_ref, par_ref, dir_ref, dia_ref, anc_ref):
        block = ref[...] if len(ref.shape) == 2 else ref[...].reshape(2 * ref.shape[0], width)
        pair_ref[row : row + block.shape[0], :] = block.astype(F32)
        row += block.shape[0]
    k = pair_ref[pl.ds(0, keys, stride=2), :].astype(BF16)
    v = pair_ref[pl.ds(1, keys, stride=2), :].astype(BF16)

    q = q_ref[...]
    g = g_ref[...]
    nt = (((1,), (1,)), ((), ()))
    s = lax.dot_general(k, q, nt, preferred_element_type=F32)
    dp = lax.dot_general(v, g, nt, preferred_element_type=F32)

    mult = warm_ref[head0 + head] / math.sqrt(width)
    lane = lax.broadcasted_iota(jnp.int32, (1, queries), 1) // BLOCK
    direct_col = blocks + 1 - odd
    diagonal_col = blocks + odd
    diagonal_there = jnp.where(odd == 1, gx < gx_count - 1, gx > 0)
    parts = []
    for b in range(blocks + 3):
        bias = jnp.zeros((1, queries), F32)
        for a in range(blocks):
            if b == a:
                continue
            col = (b if b < blocks else (blocks + 2, direct_col, diagonal_col)[b - blocks])
            ok = filt_ref[a, col] > 0
            if b == blocks + 2:
                ok = jnp.logical_and(ok, diagonal_there)
            bias = jnp.where(lane == a, jnp.where(ok, 0.0, -jnp.inf).astype(F32), bias)
        parts.append(s[b * BLOCK : (b + 1) * BLOCK] * mult + bias)
    parts.append(s[near:] * mult)
    scores = jnp.concatenate(parts, axis=0)
    top = jnp.max(scores, axis=0, keepdims=True)
    e = jnp.exp(scores - top)
    inv = 1.0 / jnp.sum(e, axis=0, keepdims=True)
    p = e * inv
    pb = p.astype(BF16)
    delta = jnp.sum(pb.astype(F32) * dp, axis=0, keepdims=True)
    ds = p * (dp - delta)
    temp_out[0] = jnp.sum(ds * s, axis=0, keepdims=True)
    dsb = (ds * mult).astype(BF16)
    nn = (((1,), (0,)), ((), ()))
    dv = lax.dot_general(pb, g, nn, preferred_element_type=F32)
    dk = lax.dot_general(dsb, q, nn, preferred_element_type=F32)
    dq = lax.dot_general(dsb, k, (((0,), (0,)), ((), ())), preferred_element_type=F32)
    dq_ref[...] = dq.astype(BF16)
    pair_ref[pl.ds(0, keys, stride=2), :] = dk
    pair_ref[pl.ds(1, keys, stride=2), :] = dv
    own_out[...] = pair_ref[: 2 * own_rows, :]
    for i, ref in enumerate((par_out, dir_out, dia_out)):
        at = 2 * (own_rows + i * BLOCK)
        ref[...] = pair_ref[at : at + 2 * BLOCK, :].astype(BF16)
    anc_out[...] = pair_ref[2 * near :, :]


def attention(pos, filt, warm, q, g, mesh_kv, partner, halo, anchors, head0, heads, dq_prev, anc_prev):
    rows, feat = q.shape
    own_rows = mesh_kv.shape[0]
    width = feat // warm.shape[0]
    a_rows = anchors.shape[0]
    keys = own_rows + 3 * BLOCK + a_rows
    smem = pl.BlockSpec(memory_space=SMEM)
    full = lambda n: pl.BlockSpec((n, 2, width), lambda h: (0, 0, head0 + h))
    part = pl.BlockSpec((BLOCK, 2, width), lambda h: (0, 0, h))
    back = pl.BlockSpec((None, 2 * BLOCK, width), lambda h: (h, 0, 0))
    cols = pl.BlockSpec((rows, width), lambda h: (0, head0 + h))
    in_specs = [smem, smem, smem, cols, cols, full(own_rows), full(BLOCK), part, part]
    in_specs += [full(a_rows)]
    args = [pos, filt, warm, q, g, mesh_kv, partner, *halo, anchors]
    alias = {}
    if dq_prev is not None:
        in_specs += [pl.BlockSpec(memory_space=pl.ANY)] * 2
        args += [dq_prev, anc_prev]
        alias = {10: 0, 11: 5}
    face = jax.ShapeDtypeStruct((heads, 2 * BLOCK, width), BF16)
    return pl.pallas_call(
        functools.partial(attention_kernel, gx_count=lax.axis_size("gx"), head0=head0, width=width),
        grid=(heads,),
        in_specs=in_specs,
        out_specs=[
            cols,
            pl.BlockSpec((None, 2 * own_rows, width), lambda h: (h, 0, 0)),
            back,
            back,
            back,
            pl.BlockSpec((2 * a_rows, width), lambda h: (0, head0 + h)),
            pl.BlockSpec((1, 1, rows), lambda h: (h, 0, 0)),
        ],
        out_shape=[
            jax.ShapeDtypeStruct(q.shape, BF16),
            jax.ShapeDtypeStruct((heads, 2 * own_rows, width), F32),
            face,
            face,
            face,
            jax.ShapeDtypeStruct((2 * a_rows, feat), F32),
            jax.ShapeDtypeStruct((heads, 1, rows), F32),
        ],
        scratch_shapes=[pltpu.VMEM((2 * keys, width), F32)],
        input_output_aliases=alias,
        compiler_params=pltpu.CompilerParams(vmem_limit_bytes=24 << 20),
        cost_estimate=pl.CostEstimate(
            flops=10 * heads * rows * keys * width,
            transcendentals=heads * rows * keys,
            bytes_accessed=heads * width * (rows * 6 + own_rows * 12 + 3 * BLOCK * 8 + a_rows * 12),
        ),
        name="attention",
    )(*args)


def combine_kernel(pos_ref, sent_ref, own_ref, dir_ref, dia_ref, par_ref, *rest):
    out_ref = rest[-1]
    odd = lax.rem(pos_ref[0], 2)
    blocks = out_ref.shape[0] // BLOCK
    spots = (
        jnp.where(odd == 1, sent_ref[0], sent_ref[1]),
        jnp.where(odd == 1, sent_ref[1], sent_ref[0]),
        sent_ref[2],
    )
    width = own_ref.shape[2]
    for h in range(own_ref.shape[0]):
        lanes = slice(h * width, (h + 1) * width)
        back = [ref[h].astype(F32) for ref in (dir_ref, dia_ref, par_ref)]
        for a in range(blocks):
            total = own_ref[h, 2 * a * BLOCK : 2 * (a + 1) * BLOCK, :]
            for spot, face in zip(spots, back):
                total = total + jnp.where(spot == a, 1.0, 0.0).astype(F32) * face
            out_ref[a * BLOCK : (a + 1) * BLOCK, :, lanes] = total.astype(BF16).reshape(BLOCK, 2, width)


def combine(pos, sent, own, faces, head0, heads, feat, width, prev, part=None, weight=1):
    rows = own.shape[1] // 2
    lo, heads = part or (0, heads)
    step = next(n for n in COMBINE_STEPS if heads % n == 0 and head0 % n == 0 and lo % n == 0)
    smem = pl.BlockSpec(memory_space=SMEM)
    face = pl.BlockSpec((step, 2 * BLOCK, width), lambda h: (lo // step + h, 0, 0))
    own_spec = pl.BlockSpec((step, 2 * rows, width), lambda h: (lo // step + h, 0, 0))
    in_specs = [smem, smem, own_spec, face, face, face]
    args = [pos, sent, own, *faces]
    alias = {}
    if prev is not None:
        in_specs.append(pl.BlockSpec(memory_space=pl.ANY))
        args.append(prev)
        alias = {6: 0}
    return pl.pallas_call(
        combine_kernel,
        grid=(heads // step,),
        in_specs=in_specs,
        out_specs=pl.BlockSpec((rows, 2, step * width), lambda h: (0, 0, (head0 + lo) // step + h)),
        out_shape=jax.ShapeDtypeStruct((rows, 2, feat), BF16),
        input_output_aliases=alias,
        compiler_params=pltpu.CompilerParams(vmem_limit_bytes=24 << 20),
        cost_estimate=pl.CostEstimate(
            flops=weight * heads * width * rows * 16,
            transcendentals=0,
            bytes_accessed=heads * width * (rows * 12 + 3 * BLOCK * 4),
        ),
        name="combine",
    )(*args)


def finish_kernel(own_ref, temp_ref, *refs):
    got, (out_ref, sum_ref) = refs[:-2], refs[-2:]
    rows, feat = own_ref.shape
    total, temp = own_ref[...], temp_ref[...]
    for ref in got:
        total = total + ref[:, :feat]
        temp = temp + ref[:1, feat:]
    out_ref[...] = total.reshape(out_ref.shape)
    sum_ref[...] = temp


def finish(own, temp, got, shape):
    return pl.pallas_call(
        finish_kernel,
        out_shape=[jax.ShapeDtypeStruct(shape, F32), jax.ShapeDtypeStruct(temp.shape, F32)],
        compiler_params=pltpu.CompilerParams(vmem_limit_bytes=8 << 20),
        name="finish",
    )(own, temp, *got)


def local(q, mesh_kv, landmark, warm, g, exported, filt):
    rows, feat = q.shape
    total = warm.shape[0]
    width = feat // total
    gx_count = lax.axis_size("gx")
    stages = levels(lax.axis_size(("gx", "gy")))
    gx = lax.axis_index("gx")
    pos = jnp.full((1,), gx, jnp.int32)
    sent = exported.reshape(-1)
    filt = filt[0]
    sizes = split_heads(total)
    chunks = [(sum(sizes[:i]), n) for i, n in enumerate(sizes)]

    picks = [pick(pos, sent, mesh_kv, width, [("direct", *chunks[0]), ("diagonal", *chunks[0])])]
    others = [(which, *chunk) for chunk in chunks[1:] for which in ("direct", "diagonal")]
    others = list(pick(pos, sent, mesh_kv, width, others + [("partner", 0, total)]))
    partner = swap_mask(others.pop(), 1)
    picks += [others[2 * i : 2 * i + 2] for i in range(len(chunks) - 1)]
    anchors = landmark
    for i, masks in enumerate(stages):
        if i == 1:
            anchors, picks[1] = lax.optimization_barrier((anchors, picks[1]))
        anchors = jnp.concatenate([anchors] + [swap_mask(anchors, m) for m in masks], axis=0)
    halos = [[swap_pairs(d, 0), swap_pairs(g, 1)] for d, g in picks]
    halos[0] = hold(halos[0], HOLD)

    dq = anc = None
    temps, owns, faces, returned = [], [], [], []
    for (head0, heads), halo in zip(chunks, halos):
        dq, own, f_dir, f_dia, f_par, anc, temp = attention(
            pos, filt, warm, q, g, mesh_kv, partner, halo, anchors, head0, heads, dq, anc
        )
        temps.append(temp)
        owns.append(own)
        faces.append((f_dir, f_dia, f_par))
        if len(faces) < len(chunks):
            returned.append(send_back(faces[-1]))
    temp = jnp.sum(jnp.concatenate(temps, axis=0), axis=(1, 2)) / math.sqrt(width)
    extra = jnp.zeros((1, LANES), F32).at[0, :total].set(temp)
    cell = None
    anc, faces[-1], returned[-1] = lax.optimization_barrier((anc, faces[-1], returned[-1]))
    direct, diagonal, partner = faces[-1]
    returned.append([swap_pairs(direct, 0), None, swap_mask(partner, 1)])
    for i, masks in enumerate(reversed(stages)):
        n = anc.shape[0] // (len(masks) + 1)
        wide = jnp.broadcast_to(extra, (n, LANES))
        out = [
            jnp.concatenate([anc[k * n : (k + 1) * n], wide], axis=1) for k in range(1, len(masks) + 1)
        ]
        if i == 1:
            out, diagonal, returned[-1][2] = lax.optimization_barrier((out, diagonal, returned[-1][2]))
            returned[-1][1] = swap_pairs(diagonal, 1)
            (extra,) = hold([extra], HOLD)
        got = [swap_mask(x, m) for x, m in zip(out, masks)]
        if i == len(stages) - 1:
            cell = combine(pos, sent, owns[-2], returned[-2], *chunks[-2], feat, width, cell, weight=4000)
            cell = combine(pos, sent, owns[-1], returned[-1], *chunks[-1], feat, width, cell, weight=0)
            got, cell = lax.optimization_barrier((got, cell))
            anchor_grad, temp = finish(anc[:n], extra, got, landmark.shape)
            break
        anc = sum([x[:, :feat] for x in got], anc[:n])
        extra = sum([x[:1, feat:] for x in got], extra)
    return (dq, cell, anchor_grad, temp[0, :total])


def solution(mesh):
    rows = ("groups", "gx", "gy")
    placed = (
        P(rows, None),
        P(rows, None, None),
        P(rows, None, None),
        P("groups"),
        P(rows, None),
        P(rows, None, None),
        P(rows, None, None),
    )
    return jax.shard_map(
        local,
        mesh=mesh,
        in_specs=placed,
        out_specs=(P(rows, None), P(rows, None, None), P(rows, None, None), P("groups")),
        check_vma=False,
    )
```

```python
import functools
import math

import jax
import jax.numpy as jnp
from jax import lax
from jax.experimental import pallas as pl
from jax.experimental.pallas import tpu as pltpu
from jax.sharding import PartitionSpec as P

BLOCK = 128
F32 = jnp.float32
BF16 = jnp.bfloat16
SMEM = pltpu.MemorySpace.SMEM
COMBINE_STEPS = (3, 2, 1)
HEAD_STEPS = (3, 2, 1)
LANES = 128
HOLD = 20_000_000_000


def swap_mask(x, mask):
    count = lax.axis_size(("gx", "gy"))
    return lax.ppermute(x, ("gx", "gy"), [(i, i ^ mask) for i in range(count)])


def levels(count):
    bits = count.bit_length() - 1
    out = [[2]] if bits > 1 else []
    at = 2
    while at < bits:
        take = min(2, bits - at)
        out.append([m << at for m in range(1, 1 << take)])
        at += take
    return out + [[1]]


def swap_pairs(x, first):
    count = lax.axis_size("gx")
    route = []
    for low in range(first, count - 1, 2):
        route += [(low, low + 1), (low + 1, low)]
    return lax.ppermute(x, "gx", route)


def split_heads(total):
    first = (total + 1) // 2
    return [n for n in (first, total - first) if n > 0]


def pick_kernel(pos_ref, sent_ref, kv_ref, *rest, copies, width):
    sems = rest[-1]
    outs = rest[:-1]
    odd = lax.rem(pos_ref[0], 2)
    spots = {
        "direct": jnp.where(odd == 1, sent_ref[0], sent_ref[1]),
        "diagonal": jnp.where(odd == 1, sent_ref[1], sent_ref[0]),
        "partner": sent_ref[2],
    }
    started = []
    for i, (out, (which, head0)) in enumerate(zip(outs, copies)):
        lanes = slice(head0 * width, head0 * width + out.shape[2])
        source = kv_ref.at[pl.ds(spots[which] * BLOCK, BLOCK), :, lanes]
        copy = pltpu.make_async_copy(source, out, sems.at[i])
        copy.start()
        started.append(copy)
    for copy in started:
        copy.wait()


def pick(pos, sent, mesh_kv, width, copies):
    smem = pl.BlockSpec(memory_space=SMEM)
    vmem = pl.BlockSpec(memory_space=pltpu.MemorySpace.VMEM)
    return pl.pallas_call(
        functools.partial(pick_kernel, copies=[c[:2] for c in copies], width=width),
        in_specs=[smem, smem, pl.BlockSpec(memory_space=pl.ANY)],
        out_specs=[vmem] * len(copies),
        out_shape=[jax.ShapeDtypeStruct((BLOCK, 2, heads * width), BF16) for _, _, heads in copies],
        scratch_shapes=[pltpu.SemaphoreType.DMA((len(copies),))],
        compiler_params=pltpu.CompilerParams(vmem_limit_bytes=8 << 20),
        cost_estimate=pl.CostEstimate(flops=0, transcendentals=0, bytes_accessed=1 << 20),
        name="pick",
    )(pos, sent, mesh_kv)


def hold_kernel(*refs):
    pass


def hold(arrays, flops):
    anywhere = pl.BlockSpec(memory_space=pl.ANY)
    return pl.pallas_call(
        hold_kernel,
        in_specs=[anywhere] * len(arrays),
        out_specs=[anywhere] * len(arrays),
        out_shape=[jax.ShapeDtypeStruct(x.shape, x.dtype) for x in arrays],
        input_output_aliases={i: i for i in range(len(arrays))},
        compiler_params=pltpu.CompilerParams(vmem_limit_bytes=1 << 20),
        cost_estimate=pl.CostEstimate(flops=flops, transcendentals=0, bytes_accessed=0),
        name="hold",
    )(*arrays)


def send_back(faces):
    direct, diagonal, partner = faces
    return [swap_pairs(direct, 0), swap_pairs(diagonal, 1), swap_mask(partner, 1)]


def attention_kernel(
    pos_ref, filt_ref, warm_ref, q_ref, g_ref, own_ref, par_ref, dir_ref, dia_ref, anc_ref, *rest,
    gx_count, head0, width,
):
    for i in range(q_ref.shape[1] // width):
        one_head(
            pos_ref, filt_ref, warm_ref, q_ref, g_ref, own_ref, par_ref, dir_ref, dia_ref, anc_ref, *rest,
            gx_count=gx_count, head0=head0, width=width, i=i,
        )


def one_head(
    pos_ref, filt_ref, warm_ref, q_ref, g_ref, own_ref, par_ref, dir_ref, dia_ref, anc_ref, *rest,
    gx_count, head0, width, i,
):
    (dq_ref, own_out, dir_out, dia_out, par_out, anc_out, temp_out, pairs_ref) = rest[-8:]
    lanes = slice(i * width, (i + 1) * width)
    pair_ref = pairs_ref.at[i]
    head = pl.program_id(0) * (q_ref.shape[1] // width) + i
    gx = pos_ref[0]
    odd = lax.rem(gx, 2)
    queries = q_ref.shape[0]
    own_rows = own_ref.shape[0]
    blocks = own_rows // BLOCK
    near = own_rows + 3 * BLOCK
    keys = near + anc_ref.shape[0]

    row = 0
    for ref in (own_ref, par_ref, dir_ref, dia_ref, anc_ref):
        block = ref[:, :, lanes].reshape(2 * ref.shape[0], width)
        pair_ref[row : row + block.shape[0], :] = block.astype(F32)
        row += block.shape[0]
    k = pair_ref[pl.ds(0, keys, stride=2), :].astype(BF16)
    v = pair_ref[pl.ds(1, keys, stride=2), :].astype(BF16)

    q = q_ref[:, lanes]
    g = g_ref[:, lanes]
    nt = (((1,), (1,)), ((), ()))
    s = lax.dot_general(k, q, nt, preferred_element_type=F32)
    dp = lax.dot_general(v, g, nt, preferred_element_type=F32)

    mult = warm_ref[head0 + head] / math.sqrt(width)
    lane = lax.broadcasted_iota(jnp.int32, (1, queries), 1) // BLOCK
    direct_col = blocks + 1 - odd
    diagonal_col = blocks + odd
    diagonal_there = jnp.where(odd == 1, gx < gx_count - 1, gx > 0)
    parts = []
    for b in range(blocks + 3):
        bias = jnp.zeros((1, queries), F32)
        for a in range(blocks):
            if b == a:
                continue
            col = (b if b < blocks else (blocks + 2, direct_col, diagonal_col)[b - blocks])
            ok = filt_ref[a, col] > 0
            if b == blocks + 2:
                ok = jnp.logical_and(ok, diagonal_there)
            bias = jnp.where(lane == a, jnp.where(ok, 0.0, -jnp.inf).astype(F32), bias)
        parts.append(s[b * BLOCK : (b + 1) * BLOCK] * mult + bias)
    parts.append(s[near:] * mult)
    scores = jnp.concatenate(parts, axis=0)
    top = jnp.max(scores, axis=0, keepdims=True)
    e = jnp.exp(scores - top)
    inv = 1.0 / jnp.sum(e, axis=0, keepdims=True)
    p = e * inv
    pb = p.astype(BF16)
    delta = jnp.sum(pb.astype(F32) * dp, axis=0, keepdims=True)
    ds = p * (dp - delta)
    temp_out[i] = jnp.sum(ds * s, axis=0, keepdims=True)
    dsb = (ds * mult).astype(BF16)
    nn = (((1,), (0,)), ((), ()))
    dv = lax.dot_general(pb, g, nn, preferred_element_type=F32)
    dk = lax.dot_general(dsb, q, nn, preferred_element_type=F32)
    dq = lax.dot_general(dsb, k, (((0,), (0,)), ((), ())), preferred_element_type=F32)
    dq_ref[:, lanes] = dq.astype(BF16)
    pair_ref[pl.ds(0, keys, stride=2), :] = dk
    pair_ref[pl.ds(1, keys, stride=2), :] = dv
    own_out[i] = pair_ref[: 2 * own_rows, :]
    for b, ref in enumerate((par_out, dir_out, dia_out)):
        at = 2 * (own_rows + b * BLOCK)
        ref[i] = pair_ref[at : at + 2 * BLOCK, :].astype(BF16)
    anc_out[:, lanes] = pair_ref[2 * near :, :]


def attention(pos, filt, warm, q, g, mesh_kv, partner, halo, anchors, head0, heads, dq_prev, anc_prev):
    rows, feat = q.shape
    own_rows = mesh_kv.shape[0]
    width = feat // warm.shape[0]
    a_rows = anchors.shape[0]
    keys = own_rows + 3 * BLOCK + a_rows
    step = next(n for n in HEAD_STEPS if heads % n == 0 and head0 % n == 0)
    first, wide = head0 // step, step * width
    smem = pl.BlockSpec(memory_space=SMEM)
    full = lambda n: pl.BlockSpec((n, 2, wide), lambda h: (0, 0, first + h))
    part = pl.BlockSpec((BLOCK, 2, wide), lambda h: (0, 0, h))
    back = pl.BlockSpec((step, 2 * BLOCK, width), lambda h: (h, 0, 0))
    cols = pl.BlockSpec((rows, wide), lambda h: (0, first + h))
    in_specs = [smem, smem, smem, cols, cols, full(own_rows), full(BLOCK), part, part]
    in_specs += [full(a_rows)]
    args = [pos, filt, warm, q, g, mesh_kv, partner, *halo, anchors]
    alias = {}
    if dq_prev is not None:
        in_specs += [pl.BlockSpec(memory_space=pl.ANY)] * 2
        args += [dq_prev, anc_prev]
        alias = {10: 0, 11: 5}
    face = jax.ShapeDtypeStruct((heads, 2 * BLOCK, width), BF16)
    return pl.pallas_call(
        functools.partial(attention_kernel, gx_count=lax.axis_size("gx"), head0=head0, width=width),
        grid=(heads // step,),
        in_specs=in_specs,
        out_specs=[
            cols,
            pl.BlockSpec((step, 2 * own_rows, width), lambda h: (h, 0, 0)),
            back,
            back,
            back,
            pl.BlockSpec((2 * a_rows, wide), lambda h: (0, first + h)),
            pl.BlockSpec((step, 1, rows), lambda h: (h, 0, 0)),
        ],
        out_shape=[
            jax.ShapeDtypeStruct(q.shape, BF16),
            jax.ShapeDtypeStruct((heads, 2 * own_rows, width), F32),
            face,
            face,
            face,
            jax.ShapeDtypeStruct((2 * a_rows, feat), F32),
            jax.ShapeDtypeStruct((heads, 1, rows), F32),
        ],
        scratch_shapes=[pltpu.VMEM((step, 2 * keys, width), F32)],
        input_output_aliases=alias,
        compiler_params=pltpu.CompilerParams(vmem_limit_bytes=24 << 20),
        cost_estimate=pl.CostEstimate(
            flops=10 * heads * rows * keys * width,
            transcendentals=heads * rows * keys,
            bytes_accessed=heads * width * (rows * 6 + own_rows * 12 + 3 * BLOCK * 8 + a_rows * 12),
        ),
        name="attention",
    )(*args)


def combine_kernel(pos_ref, sent_ref, own_ref, dir_ref, dia_ref, par_ref, *rest):
    out_ref = rest[-1]
    odd = lax.rem(pos_ref[0], 2)
    blocks = out_ref.shape[0] // BLOCK
    spots = (
        jnp.where(odd == 1, sent_ref[0], sent_ref[1]),
        jnp.where(odd == 1, sent_ref[1], sent_ref[0]),
        sent_ref[2],
    )
    width = own_ref.shape[2]
    for h in range(own_ref.shape[0]):
        lanes = slice(h * width, (h + 1) * width)
        back = [ref[h].astype(F32) for ref in (dir_ref, dia_ref, par_ref)]
        for a in range(blocks):
            total = own_ref[h, 2 * a * BLOCK : 2 * (a + 1) * BLOCK, :]
            for spot, face in zip(spots, back):
                total = total + jnp.where(spot == a, 1.0, 0.0).astype(F32) * face
            out_ref[a * BLOCK : (a + 1) * BLOCK, :, lanes] = total.astype(BF16).reshape(BLOCK, 2, width)


def combine(pos, sent, own, faces, head0, heads, feat, width, prev, part=None, weight=1):
    rows = own.shape[1] // 2
    lo, heads = part or (0, heads)
    step = next(n for n in COMBINE_STEPS if heads % n == 0 and head0 % n == 0 and lo % n == 0)
    smem = pl.BlockSpec(memory_space=SMEM)
    face = pl.BlockSpec((step, 2 * BLOCK, width), lambda h: (lo // step + h, 0, 0))
    own_spec = pl.BlockSpec((step, 2 * rows, width), lambda h: (lo // step + h, 0, 0))
    in_specs = [smem, smem, own_spec, face, face, face]
    args = [pos, sent, own, *faces]
    alias = {}
    if prev is not None:
        in_specs.append(pl.BlockSpec(memory_space=pl.ANY))
        args.append(prev)
        alias = {6: 0}
    return pl.pallas_call(
        combine_kernel,
        grid=(heads // step,),
        in_specs=in_specs,
        out_specs=pl.BlockSpec((rows, 2, step * width), lambda h: (0, 0, (head0 + lo) // step + h)),
        out_shape=jax.ShapeDtypeStruct((rows, 2, feat), BF16),
        input_output_aliases=alias,
        compiler_params=pltpu.CompilerParams(vmem_limit_bytes=24 << 20),
        cost_estimate=pl.CostEstimate(
            flops=weight * heads * width * rows * 16,
            transcendentals=0,
            bytes_accessed=heads * width * (rows * 12 + 3 * BLOCK * 4),
        ),
        name="combine",
    )(*args)


def finish_kernel(own_ref, temp_ref, *refs):
    got, (out_ref, sum_ref) = refs[:-2], refs[-2:]
    rows, feat = own_ref.shape
    total, temp = own_ref[...], temp_ref[...]
    for ref in got:
        total = total + ref[:, :feat]
        temp = temp + ref[:1, feat:]
    out_ref[...] = total.reshape(out_ref.shape)
    sum_ref[...] = temp


def finish(own, temp, got, shape):
    return pl.pallas_call(
        finish_kernel,
        out_shape=[jax.ShapeDtypeStruct(shape, F32), jax.ShapeDtypeStruct(temp.shape, F32)],
        compiler_params=pltpu.CompilerParams(vmem_limit_bytes=8 << 20),
        name="finish",
    )(own, temp, *got)


def local(q, mesh_kv, landmark, warm, g, exported, filt):
    rows, feat = q.shape
    total = warm.shape[0]
    width = feat // total
    gx_count = lax.axis_size("gx")
    stages = levels(lax.axis_size(("gx", "gy")))
    gx = lax.axis_index("gx")
    pos = jnp.full((1,), gx, jnp.int32)
    sent = exported.reshape(-1)
    filt = filt[0]
    sizes = split_heads(total)
    chunks = [(sum(sizes[:i]), n) for i, n in enumerate(sizes)]

    picks = [pick(pos, sent, mesh_kv, width, [("direct", *chunks[0]), ("diagonal", *chunks[0])])]
    others = [(which, *chunk) for chunk in chunks[1:] for which in ("direct", "diagonal")]
    others = list(pick(pos, sent, mesh_kv, width, others + [("partner", 0, total)]))
    partner = swap_mask(others.pop(), 1)
    picks += [others[2 * i : 2 * i + 2] for i in range(len(chunks) - 1)]
    anchors = landmark
    for i, masks in enumerate(stages):
        if i == 1:
            anchors, picks[1] = lax.optimization_barrier((anchors, picks[1]))
        anchors = jnp.concatenate([anchors] + [swap_mask(anchors, m) for m in masks], axis=0)
    halos = [[swap_pairs(d, 0), swap_pairs(g, 1)] for d, g in picks]
    halos[0] = hold(halos[0], HOLD)

    dq = anc = None
    temps, owns, faces, returned = [], [], [], []
    for (head0, heads), halo in zip(chunks, halos):
        dq, own, f_dir, f_dia, f_par, anc, temp = attention(
            pos, filt, warm, q, g, mesh_kv, partner, halo, anchors, head0, heads, dq, anc
        )
        temps.append(temp)
        owns.append(own)
        faces.append((f_dir, f_dia, f_par))
        if len(faces) < len(chunks):
            returned.append(send_back(faces[-1]))
    temp = jnp.sum(jnp.concatenate(temps, axis=0), axis=(1, 2)) / math.sqrt(width)
    extra = jnp.zeros((1, LANES), F32).at[0, :total].set(temp)
    cell = None
    anc, faces[-1], returned[-1] = lax.optimization_barrier((anc, faces[-1], returned[-1]))
    direct, diagonal, partner = faces[-1]
    returned.append([swap_pairs(direct, 0), None, swap_mask(partner, 1)])
    for i, masks in enumerate(reversed(stages)):
        n = anc.shape[0] // (len(masks) + 1)
        wide = jnp.broadcast_to(extra, (n, LANES))
        out = [
            jnp.concatenate([anc[k * n : (k + 1) * n], wide], axis=1) for k in range(1, len(masks) + 1)
        ]
        if i == 1:
            out, diagonal, returned[-1][2] = lax.optimization_barrier((out, diagonal, returned[-1][2]))
            returned[-1][1] = swap_pairs(diagonal, 1)
            (extra,) = hold([extra], HOLD)
        got = [swap_mask(x, m) for x, m in zip(out, masks)]
        if i == len(stages) - 1:
            cell = combine(pos, sent, owns[-2], returned[-2], *chunks[-2], feat, width, cell, weight=4000)
            cell = combine(pos, sent, owns[-1], returned[-1], *chunks[-1], feat, width, cell, weight=0)
            got, cell = lax.optimization_barrier((got, cell))
            anchor_grad, temp = finish(anc[:n], extra, got, landmark.shape)
            break
        anc = sum([x[:, :feat] for x in got], anc[:n])
        extra = sum([x[:1, feat:] for x in got], extra)
    return (dq, cell, anchor_grad, temp[0, :total])


def solution(mesh):
    rows = ("groups", "gx", "gy")
    placed = (
        P(rows, None),
        P(rows, None, None),
        P(rows, None, None),
        P("groups"),
        P(rows, None),
        P(rows, None, None),
        P(rows, None, None),
    )
    return jax.shard_map(
        local,
        mesh=mesh,
        in_specs=placed,
        out_specs=(P(rows, None), P(rows, None, None), P(rows, None, None), P("groups")),
        check_vma=False,
    )
```

```python
import functools
import math

import jax
import jax.numpy as jnp
from jax import lax
from jax.experimental import pallas as pl
from jax.experimental.pallas import tpu as pltpu
from jax.sharding import PartitionSpec as P

BLOCK = 128
F32 = jnp.float32
BF16 = jnp.bfloat16
SMEM = pltpu.MemorySpace.SMEM
COMBINE_STEPS = (3, 2, 1)
HEAD_STEPS = (3, 2, 1)
LANES = 128
HOLD = 20_000_000_000


def swap_mask(x, mask):
    count = lax.axis_size(("gx", "gy"))
    return lax.ppermute(x, ("gx", "gy"), [(i, i ^ mask) for i in range(count)])


def levels(count):
    bits = count.bit_length() - 1
    out = [[2]] if bits > 1 else []
    at = 2
    while at < bits:
        take = min(2, bits - at)
        out.append([m << at for m in range(1, 1 << take)])
        at += take
    return out + [[1]]


def swap_pairs(x, first):
    count = lax.axis_size("gx")
    route = []
    for low in range(first, count - 1, 2):
        route += [(low, low + 1), (low + 1, low)]
    return lax.ppermute(x, "gx", route)


def split_heads(total):
    first = (total + 1) // 2
    return [n for n in (first, total - first) if n > 0]


def pick_kernel(pos_ref, sent_ref, kv_ref, *rest, copies, width):
    sems = rest[-1]
    outs = rest[:-1]
    odd = lax.rem(pos_ref[0], 2)
    spots = {
        "direct": jnp.where(odd == 1, sent_ref[0], sent_ref[1]),
        "diagonal": jnp.where(odd == 1, sent_ref[1], sent_ref[0]),
        "partner": sent_ref[2],
    }
    started = []
    for i, (out, (which, head0)) in enumerate(zip(outs, copies)):
        lanes = slice(head0 * width, head0 * width + out.shape[2])
        source = kv_ref.at[pl.ds(spots[which] * BLOCK, BLOCK), :, lanes]
        copy = pltpu.make_async_copy(source, out, sems.at[i])
        copy.start()
        started.append(copy)
    for copy in started:
        copy.wait()


def pick(pos, sent, mesh_kv, width, copies):
    smem = pl.BlockSpec(memory_space=SMEM)
    vmem = pl.BlockSpec(memory_space=pltpu.MemorySpace.VMEM)
    return pl.pallas_call(
        functools.partial(pick_kernel, copies=[c[:2] for c in copies], width=width),
        in_specs=[smem, smem, pl.BlockSpec(memory_space=pl.ANY)],
        out_specs=[vmem] * len(copies),
        out_shape=[jax.ShapeDtypeStruct((BLOCK, 2, heads * width), BF16) for _, _, heads in copies],
        scratch_shapes=[pltpu.SemaphoreType.DMA((len(copies),))],
        compiler_params=pltpu.CompilerParams(vmem_limit_bytes=8 << 20),
        cost_estimate=pl.CostEstimate(flops=0, transcendentals=0, bytes_accessed=1 << 20),
        name="pick",
    )(pos, sent, mesh_kv)


def hold_kernel(*refs):
    pass


def hold(arrays, flops):
    anywhere = pl.BlockSpec(memory_space=pl.ANY)
    return pl.pallas_call(
        hold_kernel,
        in_specs=[anywhere] * len(arrays),
        out_specs=[anywhere] * len(arrays),
        out_shape=[jax.ShapeDtypeStruct(x.shape, x.dtype) for x in arrays],
        input_output_aliases={i: i for i in range(len(arrays))},
        compiler_params=pltpu.CompilerParams(vmem_limit_bytes=1 << 20),
        cost_estimate=pl.CostEstimate(flops=flops, transcendentals=0, bytes_accessed=0),
        name="hold",
    )(*arrays)


def send_back(faces):
    direct, diagonal, partner = faces
    return [swap_pairs(direct, 0), swap_pairs(diagonal, 1), swap_mask(partner, 1)]


def attention_kernel(
    pos_ref, filt_ref, warm_ref, q_ref, g_ref, own_ref, par_ref, dir_ref, dia_ref, anc_ref, *rest,
    gx_count, head0, width,
):
    for i in range(q_ref.shape[1] // width):
        one_head(
            pos_ref, filt_ref, warm_ref, q_ref, g_ref, own_ref, par_ref, dir_ref, dia_ref, anc_ref, *rest,
            gx_count=gx_count, head0=head0, width=width, i=i,
        )


def one_head(
    pos_ref, filt_ref, warm_ref, q_ref, g_ref, own_ref, par_ref, dir_ref, dia_ref, anc_ref, *rest,
    gx_count, head0, width, i,
):
    (dq_ref, own_out, dir_out, dia_out, par_out, anc_out, temp_out, pairs_ref) = rest[-8:]
    lanes = slice(i * width, (i + 1) * width)
    pair_ref = pairs_ref.at[i]
    head = pl.program_id(0) * (q_ref.shape[1] // width) + i
    gx = pos_ref[0]
    odd = lax.rem(gx, 2)
    queries = q_ref.shape[0]
    own_rows = own_ref.shape[0]
    blocks = own_rows // BLOCK
    near = own_rows + 3 * BLOCK
    keys = near + anc_ref.shape[0]

    row = 0
    for ref in (own_ref, par_ref, dir_ref, dia_ref, anc_ref):
        block = ref[:, :, lanes].reshape(2 * ref.shape[0], width)
        pair_ref[row : row + block.shape[0], :] = block.astype(F32)
        row += block.shape[0]
    k = pair_ref[pl.ds(0, keys, stride=2), :].astype(BF16)
    v = pair_ref[pl.ds(1, keys, stride=2), :].astype(BF16)

    q = q_ref[:, lanes]
    g = g_ref[:, lanes]
    nt = (((1,), (1,)), ((), ()))
    s = lax.dot_general(k, q, nt, preferred_element_type=F32)
    dp = lax.dot_general(v, g, nt, preferred_element_type=F32)

    mult = warm_ref[head0 + head] / math.sqrt(width)
    lane = lax.broadcasted_iota(jnp.int32, (1, queries), 1) // BLOCK
    direct_col = blocks + 1 - odd
    diagonal_col = blocks + odd
    diagonal_there = jnp.where(odd == 1, gx < gx_count - 1, gx > 0)
    parts = []
    for b in range(blocks + 3):
        bias = jnp.zeros((1, queries), F32)
        for a in range(blocks):
            if b == a:
                continue
            col = (b if b < blocks else (blocks + 2, direct_col, diagonal_col)[b - blocks])
            ok = filt_ref[a, col] > 0
            if b == blocks + 2:
                ok = jnp.logical_and(ok, diagonal_there)
            bias = jnp.where(lane == a, jnp.where(ok, 0.0, -jnp.inf).astype(F32), bias)
        parts.append(s[b * BLOCK : (b + 1) * BLOCK] * mult + bias)
    parts.append(s[near:] * mult)
    scores = jnp.concatenate(parts, axis=0)
    top = jnp.max(scores, axis=0, keepdims=True)
    e = jnp.exp(scores - top)
    inv = 1.0 / jnp.sum(e, axis=0, keepdims=True)
    p = e * inv
    pb = p.astype(BF16)
    delta = jnp.sum(pb.astype(F32) * dp, axis=0, keepdims=True)
    ds = p * (dp - delta)
    temp_out[i] = jnp.sum(ds * s, axis=0, keepdims=True)
    dsb = (ds * mult).astype(BF16)
    nn = (((1,), (0,)), ((), ()))
    dv = lax.dot_general(pb, g, nn, preferred_element_type=F32)
    dk = lax.dot_general(dsb, q, nn, preferred_element_type=F32)
    dq = lax.dot_general(dsb, k, (((0,), (0,)), ((), ())), preferred_element_type=F32)
    dq_ref[:, lanes] = dq.astype(BF16)
    pair_ref[pl.ds(0, keys, stride=2), :] = dk
    pair_ref[pl.ds(1, keys, stride=2), :] = dv
    own_out[i] = pair_ref[: 2 * own_rows, :]
    for b, ref in enumerate((par_out, dir_out, dia_out)):
        at = 2 * (own_rows + b * BLOCK)
        ref[i] = pair_ref[at : at + 2 * BLOCK, :].astype(BF16)
    anc_out[:, lanes] = pair_ref[2 * near :, :]


def attention(pos, filt, warm, q, g, mesh_kv, partner, halo, anchors, head0, heads, dq_prev, anc_prev):
    rows, feat = q.shape
    own_rows = mesh_kv.shape[0]
    width = feat // warm.shape[0]
    a_rows = anchors.shape[0]
    keys = own_rows + 3 * BLOCK + a_rows
    step = next(n for n in HEAD_STEPS if heads % n == 0 and head0 % n == 0)
    first, wide = head0 // step, step * width
    smem = pl.BlockSpec(memory_space=SMEM)
    full = lambda n: pl.BlockSpec((n, 2, wide), lambda h: (0, 0, first + h))
    part = pl.BlockSpec((BLOCK, 2, wide), lambda h: (0, 0, h))
    back = pl.BlockSpec((step, 2 * BLOCK, width), lambda h: (h, 0, 0))
    cols = pl.BlockSpec((rows, wide), lambda h: (0, first + h))
    in_specs = [smem, smem, smem, cols, cols, full(own_rows), full(BLOCK), part, part]
    in_specs += [full(a_rows)]
    args = [pos, filt, warm, q, g, mesh_kv, partner, *halo, anchors]
    alias = {}
    if dq_prev is not None:
        in_specs += [pl.BlockSpec(memory_space=pl.ANY)] * 2
        args += [dq_prev, anc_prev]
        alias = {10: 0, 11: 5}
    face = jax.ShapeDtypeStruct((heads, 2 * BLOCK, width), BF16)
    return pl.pallas_call(
        functools.partial(attention_kernel, gx_count=lax.axis_size("gx"), head0=head0, width=width),
        grid=(heads // step,),
        in_specs=in_specs,
        out_specs=[
            cols,
            pl.BlockSpec((step, 2 * own_rows, width), lambda h: (h, 0, 0)),
            back,
            back,
            back,
            pl.BlockSpec((2 * a_rows, wide), lambda h: (0, first + h)),
            pl.BlockSpec((step, 1, rows), lambda h: (h, 0, 0)),
        ],
        out_shape=[
            jax.ShapeDtypeStruct(q.shape, BF16),
            jax.ShapeDtypeStruct((heads, 2 * own_rows, width), F32),
            face,
            face,
            face,
            jax.ShapeDtypeStruct((2 * a_rows, feat), F32),
            jax.ShapeDtypeStruct((heads, 1, rows), F32),
        ],
        scratch_shapes=[pltpu.VMEM((step, 2 * keys, width), F32)],
        input_output_aliases=alias,
        compiler_params=pltpu.CompilerParams(vmem_limit_bytes=24 << 20),
        cost_estimate=pl.CostEstimate(
            flops=10 * heads * rows * keys * width,
            transcendentals=heads * rows * keys,
            bytes_accessed=heads * width * (rows * 6 + own_rows * 12 + 3 * BLOCK * 8 + a_rows * 12),
        ),
        name="attention",
    )(*args)


def combine_kernel(pos_ref, sent_ref, own_ref, dir_ref, dia_ref, par_ref, *rest):
    out_ref = rest[-1]
    odd = lax.rem(pos_ref[0], 2)
    blocks = out_ref.shape[0] // BLOCK
    spots = (
        jnp.where(odd == 1, sent_ref[0], sent_ref[1]),
        jnp.where(odd == 1, sent_ref[1], sent_ref[0]),
        sent_ref[2],
    )
    width = own_ref.shape[2]
    for h in range(own_ref.shape[0]):
        lanes = slice(h * width, (h + 1) * width)
        back = [ref[h].astype(F32) for ref in (dir_ref, dia_ref, par_ref)]
        for a in range(blocks):
            total = own_ref[h, 2 * a * BLOCK : 2 * (a + 1) * BLOCK, :]
            for spot, face in zip(spots, back):
                total = total + jnp.where(spot == a, 1.0, 0.0).astype(F32) * face
            out_ref[a * BLOCK : (a + 1) * BLOCK, :, lanes] = total.astype(BF16).reshape(BLOCK, 2, width)


def combine(pos, sent, own, faces, head0, heads, feat, width, prev, part=None, weight=1):
    rows = own.shape[1] // 2
    lo, heads = part or (0, heads)
    step = next(n for n in COMBINE_STEPS if heads % n == 0 and head0 % n == 0 and lo % n == 0)
    smem = pl.BlockSpec(memory_space=SMEM)
    face = pl.BlockSpec((step, 2 * BLOCK, width), lambda h: (lo // step + h, 0, 0))
    own_spec = pl.BlockSpec((step, 2 * rows, width), lambda h: (lo // step + h, 0, 0))
    in_specs = [smem, smem, own_spec, face, face, face]
    args = [pos, sent, own, *faces]
    alias = {}
    if prev is not None:
        in_specs.append(pl.BlockSpec(memory_space=pl.ANY))
        args.append(prev)
        alias = {6: 0}
    return pl.pallas_call(
        combine_kernel,
        grid=(heads // step,),
        in_specs=in_specs,
        out_specs=pl.BlockSpec((rows, 2, step * width), lambda h: (0, 0, (head0 + lo) // step + h)),
        out_shape=jax.ShapeDtypeStruct((rows, 2, feat), BF16),
        input_output_aliases=alias,
        compiler_params=pltpu.CompilerParams(vmem_limit_bytes=24 << 20),
        cost_estimate=pl.CostEstimate(
            flops=weight * heads * width * rows * 16,
            transcendentals=0,
            bytes_accessed=heads * width * (rows * 12 + 3 * BLOCK * 4),
        ),
        name="combine",
    )(*args)


def finish_kernel(own_ref, temp_ref, *refs):
    got, (out_ref, sum_ref) = refs[:-2], refs[-2:]
    rows, feat = own_ref.shape
    total, temp = own_ref[...], temp_ref[...]
    for ref in got:
        total = total + ref[:, :feat]
        temp = temp + ref[:1, feat:]
    out_ref[...] = total.reshape(out_ref.shape)
    sum_ref[...] = temp


def finish(own, temp, got, shape):
    return pl.pallas_call(
        finish_kernel,
        out_shape=[jax.ShapeDtypeStruct(shape, F32), jax.ShapeDtypeStruct(temp.shape, F32)],
        compiler_params=pltpu.CompilerParams(vmem_limit_bytes=8 << 20),
        name="finish",
    )(own, temp, *got)


def local(q, mesh_kv, landmark, warm, g, exported, filt):
    rows, feat = q.shape
    total = warm.shape[0]
    width = feat // total
    gx_count = lax.axis_size("gx")
    stages = levels(lax.axis_size(("gx", "gy")))
    gx = lax.axis_index("gx")
    pos = jnp.full((1,), gx, jnp.int32)
    sent = exported.reshape(-1)
    filt = filt[0]
    sizes = split_heads(total)
    chunks = [(sum(sizes[:i]), n) for i, n in enumerate(sizes)]

    picks = [pick(pos, sent, mesh_kv, width, [("direct", *chunks[0]), ("diagonal", *chunks[0])])]
    others = [(which, *chunk) for chunk in chunks[1:] for which in ("direct", "diagonal")]
    others = list(pick(pos, sent, mesh_kv, width, others + [("partner", 0, total)]))
    partner = swap_mask(others.pop(), 1)
    picks += [others[2 * i : 2 * i + 2] for i in range(len(chunks) - 1)]
    anchors = landmark
    for i, masks in enumerate(stages):
        if i == 1:
            anchors, picks[1] = lax.optimization_barrier((anchors, picks[1]))
        anchors = jnp.concatenate([anchors] + [swap_mask(anchors, m) for m in masks], axis=0)
    halos = [[swap_pairs(d, 0), swap_pairs(g, 1)] for d, g in picks]
    halos[0] = hold(halos[0], HOLD)

    dq = anc = None
    temps, owns, faces, returned = [], [], [], []
    for (head0, heads), halo in zip(chunks, halos):
        dq, own, f_dir, f_dia, f_par, anc, temp = attention(
            pos, filt, warm, q, g, mesh_kv, partner, halo, anchors, head0, heads, dq, anc
        )
        temps.append(temp)
        owns.append(own)
        faces.append((f_dir, f_dia, f_par))
        if len(faces) < len(chunks):
            returned.append(send_back(faces[-1]))
    temp = jnp.sum(jnp.concatenate(temps, axis=0), axis=(1, 2)) / math.sqrt(width)
    extra = jnp.zeros((1, LANES), F32).at[0, :total].set(temp)
    cell = None
    anc, faces[-1], returned[-1] = lax.optimization_barrier((anc, faces[-1], returned[-1]))
    direct, diagonal, partner = faces[-1]
    returned.append([swap_pairs(direct, 0), None, swap_mask(partner, 1)])
    steps = []
    for masks in reversed(stages):
        steps += [(masks[0], True), (masks[1], False)] if len(masks) == 3 else [(masks[0], False)]
    for i, (mask, inner) in enumerate(steps):
        n = anc.shape[0] // 2
        if inner:
            halves = anc.reshape(2, 2, n // 2, feat)
            mine, theirs = halves[:, 0].reshape(n, feat), halves[:, 1].reshape(n, feat)
        else:
            mine, theirs = anc[:n], anc[n:]
        out = jnp.concatenate([theirs, jnp.broadcast_to(extra, (n, LANES))], axis=1)
        if i == 1:
            out, diagonal, returned[-1][2] = lax.optimization_barrier((out, diagonal, returned[-1][2]))
            returned[-1][1] = swap_pairs(diagonal, 1)
        if 0 < i < len(steps) - 1:
            (extra,) = hold([extra], HOLD)
        got = swap_mask(out, mask)
        if i == len(steps) - 1:
            cell = combine(pos, sent, owns[-2], returned[-2], *chunks[-2], feat, width, cell, weight=4000)
            cell = combine(pos, sent, owns[-1], returned[-1], *chunks[-1], feat, width, cell, weight=0)
            got, cell = lax.optimization_barrier((got, cell))
            anchor_grad, temp = finish(mine, extra, [got], landmark.shape)
            break
        anc = mine + got[:, :feat]
        extra = extra + got[:1, feat:]
    return (dq, cell, anchor_grad, temp[0, :total])


def solution(mesh):
    rows = ("groups", "gx", "gy")
    placed = (
        P(rows, None),
        P(rows, None, None),
        P(rows, None, None),
        P("groups"),
        P(rows, None),
        P(rows, None, None),
        P(rows, None, None),
    )
    return jax.shard_map(
        local,
        mesh=mesh,
        in_specs=placed,
        out_specs=(P(rows, None), P(rows, None, None), P(rows, None, None), P("groups")),
        check_vma=False,
    )
```

```python
import functools
import math

import jax
import jax.numpy as jnp
from jax import lax
from jax.experimental import pallas as pl
from jax.experimental.pallas import tpu as pltpu
from jax.sharding import PartitionSpec as P

BLOCK = 128
F32 = jnp.float32
BF16 = jnp.bfloat16
SMEM = pltpu.MemorySpace.SMEM
COMBINE_STEPS = (3, 2, 1)
HEAD_STEPS = (3, 2, 1)
LANES = 128
HOLD = 20_000_000_000


def swap_mask(x, mask):
    count = lax.axis_size(("gx", "gy"))
    return lax.ppermute(x, ("gx", "gy"), [(i, i ^ mask) for i in range(count)])


def levels(count):
    bits = count.bit_length() - 1
    out = [[2]] if bits > 1 else []
    at = 2
    while at < bits:
        take = min(2, bits - at)
        out.append([m << at for m in range(1, 1 << take)])
        at += take
    return out + [[1]]


def swap_pairs(x, first):
    count = lax.axis_size("gx")
    route = []
    for low in range(first, count - 1, 2):
        route += [(low, low + 1), (low + 1, low)]
    return lax.ppermute(x, "gx", route)


def split_heads(total):
    first = (total + 1) // 2
    return [n for n in (first, total - first) if n > 0]


def pick_kernel(pos_ref, sent_ref, kv_ref, *rest, copies, width):
    sems = rest[-1]
    outs = rest[:-1]
    odd = lax.rem(pos_ref[0], 2)
    spots = {
        "direct": jnp.where(odd == 1, sent_ref[0], sent_ref[1]),
        "diagonal": jnp.where(odd == 1, sent_ref[1], sent_ref[0]),
        "partner": sent_ref[2],
    }
    started = []
    for i, (out, (which, head0)) in enumerate(zip(outs, copies)):
        lanes = slice(head0 * width, head0 * width + out.shape[2])
        source = kv_ref.at[pl.ds(spots[which] * BLOCK, BLOCK), :, lanes]
        copy = pltpu.make_async_copy(source, out, sems.at[i])
        copy.start()
        started.append(copy)
    for copy in started:
        copy.wait()


def pick(pos, sent, mesh_kv, width, copies):
    smem = pl.BlockSpec(memory_space=SMEM)
    vmem = pl.BlockSpec(memory_space=pltpu.MemorySpace.VMEM)
    return pl.pallas_call(
        functools.partial(pick_kernel, copies=[c[:2] for c in copies], width=width),
        in_specs=[smem, smem, pl.BlockSpec(memory_space=pl.ANY)],
        out_specs=[vmem] * len(copies),
        out_shape=[jax.ShapeDtypeStruct((BLOCK, 2, heads * width), BF16) for _, _, heads in copies],
        scratch_shapes=[pltpu.SemaphoreType.DMA((len(copies),))],
        compiler_params=pltpu.CompilerParams(vmem_limit_bytes=8 << 20),
        cost_estimate=pl.CostEstimate(flops=0, transcendentals=0, bytes_accessed=1 << 20),
        name="pick",
    )(pos, sent, mesh_kv)


def hold_kernel(*refs):
    pass


def hold(arrays, flops):
    anywhere = pl.BlockSpec(memory_space=pl.ANY)
    return pl.pallas_call(
        hold_kernel,
        in_specs=[anywhere] * len(arrays),
        out_specs=[anywhere] * len(arrays),
        out_shape=[jax.ShapeDtypeStruct(x.shape, x.dtype) for x in arrays],
        input_output_aliases={i: i for i in range(len(arrays))},
        compiler_params=pltpu.CompilerParams(vmem_limit_bytes=1 << 20),
        cost_estimate=pl.CostEstimate(flops=flops, transcendentals=0, bytes_accessed=0),
        name="hold",
    )(*arrays)


def send_back(faces):
    direct, diagonal, partner = faces
    return [swap_pairs(direct, 0), swap_pairs(diagonal, 1), swap_mask(partner, 1)]


def attention_kernel(
    pos_ref, filt_ref, warm_ref, q_ref, g_ref, own_ref, par_ref, dir_ref, dia_ref, anc_ref, *rest,
    gx_count, head0, width,
):
    for i in range(q_ref.shape[1] // width):
        one_head(
            pos_ref, filt_ref, warm_ref, q_ref, g_ref, own_ref, par_ref, dir_ref, dia_ref, anc_ref, *rest,
            gx_count=gx_count, head0=head0, width=width, i=i,
        )


def one_head(
    pos_ref, filt_ref, warm_ref, q_ref, g_ref, own_ref, par_ref, dir_ref, dia_ref, anc_ref, *rest,
    gx_count, head0, width, i,
):
    (dq_ref, own_out, dir_out, dia_out, par_out, anc_out, temp_out, pairs_ref) = rest[-8:]
    lanes = slice(i * width, (i + 1) * width)
    pair_ref = pairs_ref.at[i]
    head = pl.program_id(0) * (q_ref.shape[1] // width) + i
    gx = pos_ref[0]
    odd = lax.rem(gx, 2)
    queries = q_ref.shape[0]
    own_rows = own_ref.shape[0]
    blocks = own_rows // BLOCK
    near = own_rows + 3 * BLOCK
    keys = near + anc_ref.shape[0]

    row = 0
    for ref in (own_ref, par_ref, dir_ref, dia_ref, anc_ref):
        block = ref[:, :, lanes].reshape(2 * ref.shape[0], width)
        pair_ref[row : row + block.shape[0], :] = block.astype(F32)
        row += block.shape[0]
    k = pair_ref[pl.ds(0, keys, stride=2), :].astype(BF16)
    v = pair_ref[pl.ds(1, keys, stride=2), :].astype(BF16)

    q = q_ref[:, lanes]
    g = g_ref[:, lanes]
    nt = (((1,), (1,)), ((), ()))
    s = lax.dot_general(k, q, nt, preferred_element_type=F32)
    dp = lax.dot_general(v, g, nt, preferred_element_type=F32)

    mult = warm_ref[head0 + head] / math.sqrt(width)
    lane = lax.broadcasted_iota(jnp.int32, (1, queries), 1) // BLOCK
    direct_col = blocks + 1 - odd
    diagonal_col = blocks + odd
    diagonal_there = jnp.where(odd == 1, gx < gx_count - 1, gx > 0)
    parts = []
    for b in range(blocks + 3):
        bias = jnp.zeros((1, queries), F32)
        for a in range(blocks):
            if b == a:
                continue
            col = (b if b < blocks else (blocks + 2, direct_col, diagonal_col)[b - blocks])
            ok = filt_ref[a, col] > 0
            if b == blocks + 2:
                ok = jnp.logical_and(ok, diagonal_there)
            bias = jnp.where(lane == a, jnp.where(ok, 0.0, -jnp.inf).astype(F32), bias)
        parts.append(s[b * BLOCK : (b + 1) * BLOCK] * mult + bias)
    parts.append(s[near:] * mult)
    scores = jnp.concatenate(parts, axis=0)
    top = jnp.max(scores, axis=0, keepdims=True)
    e = jnp.exp(scores - top)
    inv = 1.0 / jnp.sum(e, axis=0, keepdims=True)
    p = e * inv
    pb = p.astype(BF16)
    delta = jnp.sum(pb.astype(F32) * dp, axis=0, keepdims=True)
    ds = p * (dp - delta)
    temp_out[i] = jnp.sum(ds * s, axis=0, keepdims=True)
    dsb = (ds * mult).astype(BF16)
    nn = (((1,), (0,)), ((), ()))
    dv = lax.dot_general(pb, g, nn, preferred_element_type=F32)
    dk = lax.dot_general(dsb, q, nn, preferred_element_type=F32)
    dq = lax.dot_general(dsb, k, (((0,), (0,)), ((), ())), preferred_element_type=F32)
    dq_ref[:, lanes] = dq.astype(BF16)
    pair_ref[pl.ds(0, keys, stride=2), :] = dk
    pair_ref[pl.ds(1, keys, stride=2), :] = dv
    own_out[i] = pair_ref[: 2 * own_rows, :]
    for b, ref in enumerate((par_out, dir_out, dia_out)):
        at = 2 * (own_rows + b * BLOCK)
        ref[i] = pair_ref[at : at + 2 * BLOCK, :].astype(BF16)
    anc_out[:, lanes] = pair_ref[2 * near :, :]


def attention(pos, filt, warm, q, g, mesh_kv, partner, halo, anchors, head0, heads, dq_prev, anc_prev):
    rows, feat = q.shape
    own_rows = mesh_kv.shape[0]
    width = feat // warm.shape[0]
    a_rows = anchors.shape[0]
    keys = own_rows + 3 * BLOCK + a_rows
    step = next(n for n in HEAD_STEPS if heads % n == 0 and head0 % n == 0)
    first, wide = head0 // step, step * width
    smem = pl.BlockSpec(memory_space=SMEM)
    full = lambda n: pl.BlockSpec((n, 2, wide), lambda h: (0, 0, first + h))
    part = pl.BlockSpec((BLOCK, 2, wide), lambda h: (0, 0, h))
    back = pl.BlockSpec((step, 2 * BLOCK, width), lambda h: (h, 0, 0))
    cols = pl.BlockSpec((rows, wide), lambda h: (0, first + h))
    in_specs = [smem, smem, smem, cols, cols, full(own_rows), full(BLOCK), part, part]
    in_specs += [full(a_rows)]
    args = [pos, filt, warm, q, g, mesh_kv, partner, *halo, anchors]
    alias = {}
    if dq_prev is not None:
        in_specs += [pl.BlockSpec(memory_space=pl.ANY)] * 2
        args += [dq_prev, anc_prev]
        alias = {10: 0, 11: 5}
    face = jax.ShapeDtypeStruct((heads, 2 * BLOCK, width), BF16)
    return pl.pallas_call(
        functools.partial(attention_kernel, gx_count=lax.axis_size("gx"), head0=head0, width=width),
        grid=(heads // step,),
        in_specs=in_specs,
        out_specs=[
            cols,
            pl.BlockSpec((step, 2 * own_rows, width), lambda h: (h, 0, 0)),
            back,
            back,
            back,
            pl.BlockSpec((2 * a_rows, wide), lambda h: (0, first + h)),
            pl.BlockSpec((step, 1, rows), lambda h: (h, 0, 0)),
        ],
        out_shape=[
            jax.ShapeDtypeStruct(q.shape, BF16),
            jax.ShapeDtypeStruct((heads, 2 * own_rows, width), F32),
            face,
            face,
            face,
            jax.ShapeDtypeStruct((2 * a_rows, feat), F32),
            jax.ShapeDtypeStruct((heads, 1, rows), F32),
        ],
        scratch_shapes=[pltpu.VMEM((step, 2 * keys, width), F32)],
        input_output_aliases=alias,
        compiler_params=pltpu.CompilerParams(vmem_limit_bytes=24 << 20),
        cost_estimate=pl.CostEstimate(
            flops=10 * heads * rows * keys * width,
            transcendentals=heads * rows * keys,
            bytes_accessed=heads * width * (rows * 6 + own_rows * 12 + 3 * BLOCK * 8 + a_rows * 12),
        ),
        name="attention",
    )(*args)


def combine_kernel(pos_ref, sent_ref, own_ref, dir_ref, dia_ref, par_ref, *rest):
    out_ref = rest[-1]
    odd = lax.rem(pos_ref[0], 2)
    blocks = out_ref.shape[0] // BLOCK
    spots = (
        jnp.where(odd == 1, sent_ref[0], sent_ref[1]),
        jnp.where(odd == 1, sent_ref[1], sent_ref[0]),
        sent_ref[2],
    )
    width = own_ref.shape[2]
    for h in range(own_ref.shape[0]):
        lanes = slice(h * width, (h + 1) * width)
        back = [ref[h].astype(F32) for ref in (dir_ref, dia_ref, par_ref)]
        for a in range(blocks):
            total = own_ref[h, 2 * a * BLOCK : 2 * (a + 1) * BLOCK, :]
            for spot, face in zip(spots, back):
                total = total + jnp.where(spot == a, 1.0, 0.0).astype(F32) * face
            out_ref[a * BLOCK : (a + 1) * BLOCK, :, lanes] = total.astype(BF16).reshape(BLOCK, 2, width)


def combine(pos, sent, own, faces, head0, heads, feat, width, prev, part=None, weight=1):
    rows = own.shape[1] // 2
    lo, heads = part or (0, heads)
    step = next(n for n in COMBINE_STEPS if heads % n == 0 and head0 % n == 0 and lo % n == 0)
    smem = pl.BlockSpec(memory_space=SMEM)
    face = pl.BlockSpec((step, 2 * BLOCK, width), lambda h: (lo // step + h, 0, 0))
    own_spec = pl.BlockSpec((step, 2 * rows, width), lambda h: (lo // step + h, 0, 0))
    in_specs = [smem, smem, own_spec, face, face, face]
    args = [pos, sent, own, *faces]
    alias = {}
    if prev is not None:
        in_specs.append(pl.BlockSpec(memory_space=pl.ANY))
        args.append(prev)
        alias = {6: 0}
    return pl.pallas_call(
        combine_kernel,
        grid=(heads // step,),
        in_specs=in_specs,
        out_specs=pl.BlockSpec((rows, 2, step * width), lambda h: (0, 0, (head0 + lo) // step + h)),
        out_shape=jax.ShapeDtypeStruct((rows, 2, feat), BF16),
        input_output_aliases=alias,
        compiler_params=pltpu.CompilerParams(vmem_limit_bytes=24 << 20),
        cost_estimate=pl.CostEstimate(
            flops=weight * heads * width * rows * 16,
            transcendentals=0,
            bytes_accessed=heads * width * (rows * 12 + 3 * BLOCK * 4),
        ),
        name="combine",
    )(*args)


def finish_kernel(own_ref, temp_ref, *refs):
    got, (out_ref, sum_ref) = refs[:-2], refs[-2:]
    rows, feat = own_ref.shape
    total, temp = own_ref[...], temp_ref[...]
    for ref in got:
        total = total + ref[:, :feat]
        temp = temp + ref[:1, feat:]
    out_ref[...] = total.reshape(out_ref.shape)
    sum_ref[...] = temp


def finish(own, temp, got, shape):
    return pl.pallas_call(
        finish_kernel,
        out_shape=[jax.ShapeDtypeStruct(shape, F32), jax.ShapeDtypeStruct(temp.shape, F32)],
        compiler_params=pltpu.CompilerParams(vmem_limit_bytes=8 << 20),
        name="finish",
    )(own, temp, *got)


def local(q, mesh_kv, landmark, warm, g, exported, filt):
    rows, feat = q.shape
    total = warm.shape[0]
    width = feat // total
    gx_count = lax.axis_size("gx")
    stages = levels(lax.axis_size(("gx", "gy")))
    gx = lax.axis_index("gx")
    pos = jnp.full((1,), gx, jnp.int32)
    sent = exported.reshape(-1)
    filt = filt[0]
    sizes = split_heads(total)
    chunks = [(sum(sizes[:i]), n) for i, n in enumerate(sizes)]

    picks = [pick(pos, sent, mesh_kv, width, [("direct", *chunks[0]), ("diagonal", *chunks[0])])]
    others = [(which, *chunk) for chunk in chunks[1:] for which in ("direct", "diagonal")]
    others = list(pick(pos, sent, mesh_kv, width, others + [("partner", 0, total)]))
    partner = swap_mask(others.pop(), 1)
    picks += [others[2 * i : 2 * i + 2] for i in range(len(chunks) - 1)]
    anchors = landmark
    for i, masks in enumerate(stages):
        if i == 1:
            anchors, picks[1] = lax.optimization_barrier((anchors, picks[1]))
        anchors = jnp.concatenate([anchors] + [swap_mask(anchors, m) for m in masks], axis=0)
    halos = [[swap_pairs(d, 0), swap_pairs(g, 1)] for d, g in picks]
    halos[0] = hold(halos[0], HOLD)

    dq = anc = None
    temps, owns, faces, returned = [], [], [], []
    for (head0, heads), halo in zip(chunks, halos):
        dq, own, f_dir, f_dia, f_par, anc, temp = attention(
            pos, filt, warm, q, g, mesh_kv, partner, halo, anchors, head0, heads, dq, anc
        )
        temps.append(temp)
        owns.append(own)
        faces.append((f_dir, f_dia, f_par))
        if len(faces) < len(chunks):
            returned.append(send_back(faces[-1]))
    temp = jnp.sum(jnp.concatenate(temps, axis=0), axis=(1, 2)) / math.sqrt(width)
    extra = jnp.zeros((1, LANES), F32).at[0, :total].set(temp)
    cell = None
    anc, faces[-1], returned[-1] = lax.optimization_barrier((anc, faces[-1], returned[-1]))
    direct, diagonal, partner = faces[-1]
    returned.append([swap_pairs(direct, 0), None, swap_mask(partner, 1)])
    steps = []
    for masks in reversed(stages):
        steps += [(masks[0], True), (masks[1], False)] if len(masks) == 3 else [(masks[0], False)]
    for i, (mask, inner) in enumerate(steps):
        n = anc.shape[0] // 2
        if inner:
            halves = anc.reshape(2, 2, n // 2, feat)
            mine, theirs = halves[:, 0].reshape(n, feat), halves[:, 1].reshape(n, feat)
        else:
            mine, theirs = anc[:n], anc[n:]
        out = jnp.concatenate([theirs, jnp.broadcast_to(extra, (n, LANES))], axis=1)
        if i == 1:
            out, diagonal, returned[-1][2] = lax.optimization_barrier((out, diagonal, returned[-1][2]))
            returned[-1][1] = swap_pairs(diagonal, 1)
        if 0 < i < len(steps) - 2:
            (extra,) = hold([extra], HOLD)
        got = swap_mask(out, mask)
        if i == len(steps) - 2:
            cell = combine(pos, sent, owns[-2], returned[-2], *chunks[-2], feat, width, cell, weight=4000)
            got, cell = lax.optimization_barrier((got, cell))
        if i == len(steps) - 1:
            cell = combine(pos, sent, owns[-1], returned[-1], *chunks[-1], feat, width, cell, weight=0)
            got, cell = lax.optimization_barrier((got, cell))
            anchor_grad, temp = finish(mine, extra, [got], landmark.shape)
            break
        anc = mine + got[:, :feat]
        extra = extra + got[:1, feat:]
    return (dq, cell, anchor_grad, temp[0, :total])


def solution(mesh):
    rows = ("groups", "gx", "gy")
    placed = (
        P(rows, None),
        P(rows, None, None),
        P(rows, None, None),
        P("groups"),
        P(rows, None),
        P(rows, None, None),
        P(rows, None, None),
    )
    return jax.shard_map(
        local,
        mesh=mesh,
        in_specs=placed,
        out_specs=(P(rows, None), P(rows, None, None), P(rows, None, None), P("groups")),
        check_vma=False,
    )
```

```python
import functools
import math

import jax
import jax.numpy as jnp
from jax import lax
from jax.experimental import pallas as pl
from jax.experimental.pallas import tpu as pltpu
from jax.sharding import PartitionSpec as P

BLOCK = 128
F32 = jnp.float32
BF16 = jnp.bfloat16
SMEM = pltpu.MemorySpace.SMEM
COMBINE_STEPS = (3, 2, 1)
HEAD_STEPS = (3, 2, 1)
LANES = 128
HOLD = 20_000_000_000


def swap_mask(x, mask):
    count = lax.axis_size(("gx", "gy"))
    return lax.ppermute(x, ("gx", "gy"), [(i, i ^ mask) for i in range(count)])


def levels(count):
    bits = count.bit_length() - 1
    out = [[2]] if bits > 1 else []
    at = 2
    while at < bits:
        take = min(2, bits - at)
        out.append([m << at for m in range(1, 1 << take)])
        at += take
    return out + [[1]]


def swap_pairs(x, first):
    count = lax.axis_size("gx")
    route = []
    for low in range(first, count - 1, 2):
        route += [(low, low + 1), (low + 1, low)]
    return lax.ppermute(x, "gx", route)


def split_heads(total):
    first = (total + 1) // 2
    return [n for n in (first, total - first) if n > 0]


def pick_kernel(pos_ref, sent_ref, kv_ref, *rest, copies, width):
    sems = rest[-1]
    outs = rest[:-1]
    odd = lax.rem(pos_ref[0], 2)
    spots = {
        "direct": jnp.where(odd == 1, sent_ref[0], sent_ref[1]),
        "diagonal": jnp.where(odd == 1, sent_ref[1], sent_ref[0]),
        "partner": sent_ref[2],
    }
    started = []
    for i, (out, (which, head0)) in enumerate(zip(outs, copies)):
        lanes = slice(head0 * width, head0 * width + out.shape[2])
        source = kv_ref.at[pl.ds(spots[which] * BLOCK, BLOCK), :, lanes]
        copy = pltpu.make_async_copy(source, out, sems.at[i])
        copy.start()
        started.append(copy)
    for copy in started:
        copy.wait()


def pick(pos, sent, mesh_kv, width, copies):
    smem = pl.BlockSpec(memory_space=SMEM)
    vmem = pl.BlockSpec(memory_space=pltpu.MemorySpace.VMEM)
    return pl.pallas_call(
        functools.partial(pick_kernel, copies=[c[:2] for c in copies], width=width),
        in_specs=[smem, smem, pl.BlockSpec(memory_space=pl.ANY)],
        out_specs=[vmem] * len(copies),
        out_shape=[jax.ShapeDtypeStruct((BLOCK, 2, heads * width), BF16) for _, _, heads in copies],
        scratch_shapes=[pltpu.SemaphoreType.DMA((len(copies),))],
        compiler_params=pltpu.CompilerParams(vmem_limit_bytes=8 << 20),
        cost_estimate=pl.CostEstimate(flops=0, transcendentals=0, bytes_accessed=1 << 20),
        name="pick",
    )(pos, sent, mesh_kv)


def hold_kernel(*refs):
    pass


def hold(arrays, flops):
    anywhere = pl.BlockSpec(memory_space=pl.ANY)
    return pl.pallas_call(
        hold_kernel,
        in_specs=[anywhere] * len(arrays),
        out_specs=[anywhere] * len(arrays),
        out_shape=[jax.ShapeDtypeStruct(x.shape, x.dtype) for x in arrays],
        input_output_aliases={i: i for i in range(len(arrays))},
        compiler_params=pltpu.CompilerParams(vmem_limit_bytes=1 << 20),
        cost_estimate=pl.CostEstimate(flops=flops, transcendentals=0, bytes_accessed=0),
        name="hold",
    )(*arrays)


def send_back(faces):
    direct, diagonal, partner = faces
    return [swap_pairs(direct, 0), swap_pairs(diagonal, 1), swap_mask(partner, 1)]


def attention_kernel(
    pos_ref, filt_ref, warm_ref, q_ref, g_ref, own_ref, par_ref, dir_ref, dia_ref, anc_ref, *rest,
    gx_count, head0, width,
):
    for i in range(q_ref.shape[1] // width):
        one_head(
            pos_ref, filt_ref, warm_ref, q_ref, g_ref, own_ref, par_ref, dir_ref, dia_ref, anc_ref, *rest,
            gx_count=gx_count, head0=head0, width=width, i=i,
        )


def one_head(
    pos_ref, filt_ref, warm_ref, q_ref, g_ref, own_ref, par_ref, dir_ref, dia_ref, anc_ref, *rest,
    gx_count, head0, width, i,
):
    (dq_ref, own_out, dir_out, dia_out, par_out, anc_out, temp_out, pairs_ref) = rest[-8:]
    lanes = slice(i * width, (i + 1) * width)
    pair_ref = pairs_ref.at[i]
    head = pl.program_id(0) * (q_ref.shape[1] // width) + i
    gx = pos_ref[0]
    odd = lax.rem(gx, 2)
    queries = q_ref.shape[0]
    own_rows = own_ref.shape[0]
    blocks = own_rows // BLOCK
    near = own_rows + 3 * BLOCK
    keys = near + anc_ref.shape[0]

    row = 0
    for ref in (own_ref, par_ref, dir_ref, dia_ref, anc_ref):
        block = ref[:, :, lanes].reshape(2 * ref.shape[0], width)
        pair_ref[row : row + block.shape[0], :] = block.astype(F32)
        row += block.shape[0]
    k = pair_ref[pl.ds(0, keys, stride=2), :].astype(BF16)
    v = pair_ref[pl.ds(1, keys, stride=2), :].astype(BF16)

    q = q_ref[:, lanes]
    g = g_ref[:, lanes]
    nt = (((1,), (1,)), ((), ()))
    s = lax.dot_general(k, q, nt, preferred_element_type=F32)
    dp = lax.dot_general(v, g, nt, preferred_element_type=F32)

    mult = warm_ref[head0 + head] / math.sqrt(width)
    lane = lax.broadcasted_iota(jnp.int32, (1, queries), 1) // BLOCK
    direct_col = blocks + 1 - odd
    diagonal_col = blocks + odd
    diagonal_there = jnp.where(odd == 1, gx < gx_count - 1, gx > 0)
    parts = []
    for b in range(blocks + 3):
        bias = jnp.zeros((1, queries), F32)
        for a in range(blocks):
            if b == a:
                continue
            col = (b if b < blocks else (blocks + 2, direct_col, diagonal_col)[b - blocks])
            ok = filt_ref[a, col] > 0
            if b == blocks + 2:
                ok = jnp.logical_and(ok, diagonal_there)
            bias = jnp.where(lane == a, jnp.where(ok, 0.0, -jnp.inf).astype(F32), bias)
        parts.append(s[b * BLOCK : (b + 1) * BLOCK] * mult + bias)
    parts.append(s[near:] * mult)
    scores = jnp.concatenate(parts, axis=0)
    top = jnp.max(scores, axis=0, keepdims=True)
    e = jnp.exp(scores - top)
    inv = 1.0 / jnp.sum(e, axis=0, keepdims=True)
    p = e * inv
    pb = p.astype(BF16)
    delta = jnp.sum(pb.astype(F32) * dp, axis=0, keepdims=True)
    ds = p * (dp - delta)
    temp_out[i] = jnp.sum(ds * s, axis=0, keepdims=True)
    dsb = (ds * mult).astype(BF16)
    nn = (((1,), (0,)), ((), ()))
    dv = lax.dot_general(pb, g, nn, preferred_element_type=F32)
    dk = lax.dot_general(dsb, q, nn, preferred_element_type=F32)
    dq = lax.dot_general(dsb, k, (((0,), (0,)), ((), ())), preferred_element_type=F32)
    dq_ref[:, lanes] = dq.astype(BF16)
    pair_ref[pl.ds(0, keys, stride=2), :] = dk
    pair_ref[pl.ds(1, keys, stride=2), :] = dv
    own_out[i] = pair_ref[: 2 * own_rows, :]
    for b, ref in enumerate((par_out, dir_out, dia_out)):
        at = 2 * (own_rows + b * BLOCK)
        ref[i] = pair_ref[at : at + 2 * BLOCK, :].astype(BF16)
    anc_out[:, lanes] = pair_ref[2 * near :, :]


def attention(pos, filt, warm, q, g, mesh_kv, partner, halo, anchors, head0, heads, dq_prev, anc_prev):
    rows, feat = q.shape
    own_rows = mesh_kv.shape[0]
    width = feat // warm.shape[0]
    a_rows = anchors.shape[0]
    keys = own_rows + 3 * BLOCK + a_rows
    step = next(n for n in HEAD_STEPS if heads % n == 0 and head0 % n == 0)
    first, wide = head0 // step, step * width
    smem = pl.BlockSpec(memory_space=SMEM)
    full = lambda n: pl.BlockSpec((n, 2, wide), lambda h: (0, 0, first + h))
    part = pl.BlockSpec((BLOCK, 2, wide), lambda h: (0, 0, h))
    back = pl.BlockSpec((step, 2 * BLOCK, width), lambda h: (h, 0, 0))
    cols = pl.BlockSpec((rows, wide), lambda h: (0, first + h))
    in_specs = [smem, smem, smem, cols, cols, full(own_rows), full(BLOCK), part, part]
    in_specs += [full(a_rows)]
    args = [pos, filt, warm, q, g, mesh_kv, partner, *halo, anchors]
    alias = {}
    if dq_prev is not None:
        in_specs += [pl.BlockSpec(memory_space=pl.ANY)] * 2
        args += [dq_prev, anc_prev]
        alias = {10: 0, 11: 5}
    face = jax.ShapeDtypeStruct((heads, 2 * BLOCK, width), BF16)
    return pl.pallas_call(
        functools.partial(attention_kernel, gx_count=lax.axis_size("gx"), head0=head0, width=width),
        grid=(heads // step,),
        in_specs=in_specs,
        out_specs=[
            cols,
            pl.BlockSpec((step, 2 * own_rows, width), lambda h: (h, 0, 0)),
            back,
            back,
            back,
            pl.BlockSpec((2 * a_rows, wide), lambda h: (0, first + h)),
            pl.BlockSpec((step, 1, rows), lambda h: (h, 0, 0)),
        ],
        out_shape=[
            jax.ShapeDtypeStruct(q.shape, BF16),
            jax.ShapeDtypeStruct((heads, 2 * own_rows, width), F32),
            face,
            face,
            face,
            jax.ShapeDtypeStruct((2 * a_rows, feat), F32),
            jax.ShapeDtypeStruct((heads, 1, rows), F32),
        ],
        scratch_shapes=[pltpu.VMEM((step, 2 * keys, width), F32)],
        input_output_aliases=alias,
        compiler_params=pltpu.CompilerParams(vmem_limit_bytes=24 << 20),
        cost_estimate=pl.CostEstimate(
            flops=10 * heads * rows * keys * width,
            transcendentals=heads * rows * keys,
            bytes_accessed=heads * width * (rows * 6 + own_rows * 12 + 3 * BLOCK * 8 + a_rows * 12),
        ),
        name="attention",
    )(*args)


def combine_kernel(pos_ref, sent_ref, own_ref, dir_ref, dia_ref, par_ref, *rest):
    out_ref = rest[-1]
    odd = lax.rem(pos_ref[0], 2)
    blocks = out_ref.shape[0] // BLOCK
    spots = (
        jnp.where(odd == 1, sent_ref[0], sent_ref[1]),
        jnp.where(odd == 1, sent_ref[1], sent_ref[0]),
        sent_ref[2],
    )
    width = own_ref.shape[2]
    for h in range(own_ref.shape[0]):
        lanes = slice(h * width, (h + 1) * width)
        back = [ref[h].astype(F32) for ref in (dir_ref, dia_ref, par_ref)]
        for a in range(blocks):
            total = own_ref[h, 2 * a * BLOCK : 2 * (a + 1) * BLOCK, :]
            for spot, face in zip(spots, back):
                total = total + jnp.where(spot == a, 1.0, 0.0).astype(F32) * face
            out_ref[a * BLOCK : (a + 1) * BLOCK, :, lanes] = total.astype(BF16).reshape(BLOCK, 2, width)


def combine(pos, sent, own, faces, head0, heads, feat, width, prev, part=None, weight=1):
    rows = own.shape[1] // 2
    lo, heads = part or (0, heads)
    step = next(n for n in COMBINE_STEPS if heads % n == 0 and head0 % n == 0 and lo % n == 0)
    smem = pl.BlockSpec(memory_space=SMEM)
    face = pl.BlockSpec((step, 2 * BLOCK, width), lambda h: (lo // step + h, 0, 0))
    own_spec = pl.BlockSpec((step, 2 * rows, width), lambda h: (lo // step + h, 0, 0))
    in_specs = [smem, smem, own_spec, face, face, face]
    args = [pos, sent, own, *faces]
    alias = {}
    if prev is not None:
        in_specs.append(pl.BlockSpec(memory_space=pl.ANY))
        args.append(prev)
        alias = {6: 0}
    return pl.pallas_call(
        combine_kernel,
        grid=(heads // step,),
        in_specs=in_specs,
        out_specs=pl.BlockSpec((rows, 2, step * width), lambda h: (0, 0, (head0 + lo) // step + h)),
        out_shape=jax.ShapeDtypeStruct((rows, 2, feat), BF16),
        input_output_aliases=alias,
        compiler_params=pltpu.CompilerParams(vmem_limit_bytes=24 << 20),
        cost_estimate=pl.CostEstimate(
            flops=weight * heads * width * rows * 16,
            transcendentals=0,
            bytes_accessed=heads * width * (rows * 12 + 3 * BLOCK * 4),
        ),
        name="combine",
    )(*args)


def finish_kernel(own_ref, temp_ref, *refs):
    got, (out_ref, sum_ref) = refs[:-2], refs[-2:]
    rows, feat = own_ref.shape
    total, temp = own_ref[...], temp_ref[...]
    for ref in got:
        total = total + ref[:, :feat]
        temp = temp + ref[:1, feat:]
    out_ref[...] = total.reshape(out_ref.shape)
    sum_ref[...] = temp[:, : sum_ref.shape[1]]


def finish(own, temp, got, shape, total):
    return pl.pallas_call(
        finish_kernel,
        out_shape=[jax.ShapeDtypeStruct(shape, F32), jax.ShapeDtypeStruct((1, total), F32)],
        compiler_params=pltpu.CompilerParams(vmem_limit_bytes=8 << 20),
        name="finish",
    )(own, temp, *got)


def local(q, mesh_kv, landmark, warm, g, exported, filt):
    rows, feat = q.shape
    total = warm.shape[0]
    width = feat // total
    gx_count = lax.axis_size("gx")
    stages = levels(lax.axis_size(("gx", "gy")))
    gx = lax.axis_index("gx")
    pos = jnp.full((1,), gx, jnp.int32)
    sent = exported.reshape(-1)
    filt = filt[0]
    sizes = split_heads(total)
    chunks = [(sum(sizes[:i]), n) for i, n in enumerate(sizes)]

    picks = [pick(pos, sent, mesh_kv, width, [("direct", *chunks[0]), ("diagonal", *chunks[0])])]
    others = [(which, *chunk) for chunk in chunks[1:] for which in ("direct", "diagonal")]
    others = list(pick(pos, sent, mesh_kv, width, others + [("partner", 0, total)]))
    partner = swap_mask(others.pop(), 1)
    picks += [others[2 * i : 2 * i + 2] for i in range(len(chunks) - 1)]
    anchors = landmark
    for i, masks in enumerate(stages):
        if i == 1:
            anchors, picks[1] = lax.optimization_barrier((anchors, picks[1]))
        anchors = jnp.concatenate([anchors] + [swap_mask(anchors, m) for m in masks], axis=0)
    halos = [[swap_pairs(d, 0), swap_pairs(g, 1)] for d, g in picks]
    halos[0] = hold(halos[0], HOLD)

    dq = anc = None
    temps, owns, faces, returned = [], [], [], []
    for (head0, heads), halo in zip(chunks, halos):
        dq, own, f_dir, f_dia, f_par, anc, temp = attention(
            pos, filt, warm, q, g, mesh_kv, partner, halo, anchors, head0, heads, dq, anc
        )
        temps.append(temp)
        owns.append(own)
        faces.append((f_dir, f_dia, f_par))
        if len(faces) < len(chunks):
            returned.append(send_back(faces[-1]))
    temp = jnp.sum(jnp.concatenate(temps, axis=0), axis=(1, 2)) / math.sqrt(width)
    extra = jnp.zeros((1, LANES), F32).at[0, :total].set(temp)
    cell = None
    anc, faces[-1], returned[-1] = lax.optimization_barrier((anc, faces[-1], returned[-1]))
    direct, diagonal, partner = faces[-1]
    returned.append([swap_pairs(direct, 0), None, swap_mask(partner, 1)])
    steps = []
    for masks in reversed(stages):
        steps += [(masks[0], True), (masks[1], False)] if len(masks) == 3 else [(masks[0], False)]
    for i, (mask, inner) in enumerate(steps):
        n = anc.shape[0] // 2
        if inner:
            halves = anc.reshape(2, 2, n // 2, feat)
            mine, theirs = halves[:, 0].reshape(n, feat), halves[:, 1].reshape(n, feat)
        else:
            mine, theirs = anc[:n], anc[n:]
        out = jnp.concatenate([theirs, jnp.broadcast_to(extra, (n, LANES))], axis=1)
        if i == 1:
            out, diagonal, returned[-1][2] = lax.optimization_barrier((out, diagonal, returned[-1][2]))
            returned[-1][1] = swap_pairs(diagonal, 1)
        if 0 < i < len(steps) - 1:
            (extra,) = hold([extra], HOLD)
        got = swap_mask(out, mask)
        if i == len(steps) - 1:
            cell = combine(pos, sent, owns[-2], returned[-2], *chunks[-2], feat, width, cell, weight=4000)
            cell = combine(pos, sent, owns[-1], returned[-1], *chunks[-1], feat, width, cell, weight=0)
            got, cell = lax.optimization_barrier((got, cell))
            anchor_grad, temp = finish(mine, extra, [got], landmark.shape, total)
            break
        anc = mine + got[:, :feat]
        extra = extra + got[:1, feat:]
    return (dq, cell, anchor_grad, temp.reshape(total))


def solution(mesh):
    rows = ("groups", "gx", "gy")
    placed = (
        P(rows, None),
        P(rows, None, None),
        P(rows, None, None),
        P("groups"),
        P(rows, None),
        P(rows, None, None),
        P(rows, None, None),
    )
    return jax.shard_map(
        local,
        mesh=mesh,
        in_specs=placed,
        out_specs=(P(rows, None), P(rows, None, None), P(rows, None, None), P("groups")),
        check_vma=False,
    )
```
